32 devices in a mesh: fsdp: 4 (over z), context: 2 (over x), tensor: 4 (over y, core).
Axes of the slice: x: 2, y: 2, z: 4, core: 2. Of those that a mesh axis runs over, the one named last changes fastest.
Arguments:
- layer_input: bfloat16 [4, 4096, 768], P('fsdp', 'context'), may hold values from -6 to 6
- teacher: bfloat16 [4, 4096, 768], P('fsdp', 'context'), may hold values from -96 to 96
- query_weight: bfloat16 [768, 768], P('fsdp', 'tensor'), may hold values from -0.21875 to 0.21875
- key_weight: bfloat16 [768, 768], P('fsdp', 'tensor'), may hold values from -0.21875 to 0.21875
- value_weight: bfloat16 [768, 768], P('fsdp', 'tensor'), may hold values from -0.21875 to 0.21875
- out_weight: bfloat16 [768, 768], P('tensor', 'fsdp'), may hold values from -6 to 6
- up_weight: bfloat16 [768, 3072], P('fsdp', 'tensor'), may hold values from -0.21875 to 0.21875
- down_weight: bfloat16 [3072, 768], P('tensor', 'fsdp'), may hold values from -0.109375 to 0.109375
- first_gain: bfloat16 [768], P('fsdp'), may hold values from 0.25 to 1.75
- first_shift: bfloat16 [768], P('fsdp'), may hold values from -3 to 3
- second_gain: bfloat16 [768], P('fsdp'), may hold values from 0.25 to 1.75
- second_shift: bfloat16 [768], P('fsdp'), may hold values from -3 to 3
- parents: int32 [4, 8], P('fsdp'), may hold values from 0 to 4
- valid_count: int32 [4], P('fsdp'), may hold values from 2048 to 4096
Outputs:
- layer_output: bfloat16 [4, 4096, 768], P('fsdp', 'context')
- input_grad: float32 [4, 4096, 768], P('fsdp', 'context')
- loss_value: float32 [], replicated
- query_grad: float32 [768, 768], P('fsdp', 'tensor')
- key_grad: float32 [768, 768], P('fsdp', 'tensor')
- value_grad: float32 [768, 768], P('fsdp', 'tensor')
- out_grad: float32 [768, 768], P('tensor', 'fsdp')
- up_grad: float32 [768, 3072], P('fsdp', 'tensor')
- down_grad: float32 [3072, 768], P('tensor', 'fsdp')
- first_gain_grad: float32 [768], P('fsdp')
- first_shift_grad: float32 [768], P('fsdp')
- second_gain_grad: float32 [768], P('fsdp')
- second_shift_grad: float32 [768], P('fsdp')
The draws below stay inside these ranges and needn't reach their ends.
Inputs may be any that keep to these rules, and one draw needn't show every extreme that they name: `parents`: 0 names the trunk, b from 1 to 4 the b-th branch.
All inputs are finite; a program needn't handle non-finite values.
Results may differ from the reference program's by a relative error of at most 0.018.
Values may be sent and summed in bfloat16 or wider, within the bound.
A program may use at most 256 MiB of HBM per device.

```python
import math
import jax
import jax.numpy as jnp
from jax import lax

D = 768
HEADS = 12
HEAD_DIM = 64
FF = 3072
TREE = 4096
TREES = 4
N_TENSOR = 4


def draw_teacher(key, part):
    base = jnp.clip(jax.random.normal(key, (TREES, TREE, D), jnp.float32), -6.0, 6.0)
    tree_place = jnp.arange(TREES, dtype=jnp.float32) / float(TREES)
    slot_place = jnp.arange(TREE, dtype=jnp.float32) / float(TREE)
    growth = jnp.exp(math.log(4.0) * (tree_place[:, None] + slot_place[None, :]))
    return (base * growth[:, :, None]).astype(jnp.bfloat16)


def plant(entries, key, least, high):
    dims = entries.shape
    spot = [jax.random.randint(jax.random.fold_in(key, axis), (), 0, dims[axis]) for axis in range(len(dims))]
    entries = entries.at[tuple(spot)].set(least)
    longest = dims.index(max(dims))
    spot[longest] = (spot[longest] + 1) % dims[longest]
    return entries.at[tuple(spot)].set(high)


def block_scale(own_key, shape, shards, low, high):
    def one(dim, blocks):
        draws = jax.random.uniform(jax.random.fold_in(jax.random.fold_in(own_key, 6), dim), (blocks,), jnp.float32, low / len(shards), high / len(shards))
        return jnp.repeat(jnp.exp(draws), shape[dim] // blocks).reshape((-1,) + (1,) * (len(shape) - dim - 1))

    factor_of = one(*shards[0])
    for cut in shards[1:]:
        factor_of = factor_of * one(*cut)
    return factor_of


def bell_draw(rng, dims, scale, most, pieces=(), held_as=jnp.bfloat16):
    values = jax.random.normal(rng, dims, jnp.float32) * scale
    if len(pieces) > 0:
        values = block_scale(rng, dims, pieces, -0.22, 0.18) * values
    return jnp.clip(values, min=-most, max=most).astype(held_as)


def setup_inputs(seed: int = 0) -> dict:
    keys = jax.random.split(jax.random.key(seed), 15)
    layer_input = bell_draw(keys[0], (TREES, TREE, D), 1.0, 6.0, ((0, 4), (1, 2)))
    teacher = draw_teacher(jax.random.fold_in(keys[14], 71), 0)
    query_weight = bell_draw(keys[2], (D, D), D ** -0.5, 0.21875, ((0, 4), (1, 4)))
    key_weight = bell_draw(keys[3], (D, D), D ** -0.5, 0.21875, ((0, 4), (1, 4)))
    value_weight = bell_draw(keys[4], (D, D), D ** -0.5, 0.21875, ((0, 4), (1, 4)))
    out_weight = bell_draw(keys[5], (D, D), 1 ** -0.5, 6.0, ((0, 4), (1, 4)))
    up_weight = bell_draw(keys[6], (D, FF), D ** -0.5, 0.21875, ((0, 4), (1, 4)))
    down_weight = bell_draw(keys[7], (FF, D), FF ** -0.5, 0.109375, ((0, 4), (1, 4)))
    first_gain = jnp.clip(1.0 + 0.15 * jax.random.normal(keys[8], (D,), jnp.float32), 0.25, 1.75).astype(jnp.bfloat16)
    first_shift = bell_draw(keys[9], (D,), 0.5, 3.0, ((0, 4),))
    second_gain = jnp.clip(1.0 + 0.15 * jax.random.normal(keys[10], (D,), jnp.float32), 0.25, 1.75).astype(jnp.bfloat16)
    second_shift = bell_draw(keys[11], (D,), 0.5, 3.0, ((0, 4),))
    parents = plant(jax.random.randint(keys[12], (TREES, 8), 0, 5), jax.random.fold_in(keys[12], 1), 0, 4).astype(jnp.int32)
    valid_count = plant(jax.random.randint(keys[13], (TREES,), TREE // 2, TREE + 1), jax.random.fold_in(keys[13], 1), TREE // 2, TREE).astype(jnp.int32)
    return dict(layer_input=layer_input, teacher=teacher, query_weight=query_weight, key_weight=key_weight, value_weight=value_weight, out_weight=out_weight, up_weight=up_weight, down_weight=down_weight, first_gain=first_gain, first_shift=first_shift, second_gain=second_gain, second_shift=second_shift, parents=parents, valid_count=valid_count)


@jax.custom_vjp
def low(v):
    return lax.optimization_barrier(v.astype(jnp.bfloat16)).astype(jnp.float32)

@jax.custom_vjp
def low_back(v):
    return v

def low_keep(v):
    return (low(v), None)

def low_pass(kept, grad):
    return (grad,)

def back_keep(v):
    return (v, None)

def back_low(kept, grad):
    return (low(grad),)
low.defvjp(low_keep, low_pass)
low_back.defvjp(back_keep, back_low)
precise = lax.Precision.HIGHEST
norm_eps = 1e-05

def layout_of(slot_ids, parents_row, tree_len):
    half_len = tree_len // 2
    branch_len = tree_len // 16
    leaf_len = tree_len // 32
    leaf_start = half_len + 4 * branch_len
    in_branch = (slot_ids >= half_len) & (slot_ids < leaf_start)
    in_leaf = slot_ids >= leaf_start
    branch_index = jnp.clip((slot_ids - half_len) // branch_len, 0, 3).astype(jnp.int32)
    leaf_index = jnp.clip((slot_ids - leaf_start) // leaf_len, 0, 7).astype(jnp.int32)
    leaf_ids = jnp.arange(8, dtype=jnp.int32)
    leaf_parent = lax.optimization_barrier(jnp.sum(jnp.where(leaf_index[:, None] == leaf_ids[None, :], parents_row[None, :], 0), axis=1)).astype(jnp.int32)
    segment = jnp.where(in_leaf, 5 + leaf_index, jnp.where(in_branch, 1 + branch_index, 0)).astype(jnp.int32)
    owner_branch = jnp.where(in_leaf, leaf_parent, jnp.where(in_branch, 1 + branch_index, 0)).astype(jnp.int32)
    leaf_pos = half_len + jnp.where(leaf_parent > 0, branch_len, 0) + slot_ids - leaf_start - leaf_index * leaf_len
    branch_pos = slot_ids - branch_index * branch_len
    position = jnp.where(in_leaf, leaf_pos, jnp.where(in_branch, branch_pos, slot_ids)).astype(jnp.int32)
    phase_angle = 0.5 * math.pi * position.astype(jnp.float32) / float(half_len + branch_len + leaf_len)
    return (segment, owner_branch, phase_angle)

def features(pre_act, phase_angle):
    rectified = jnp.maximum(pre_act, 0.0)
    cosine = jnp.cos(phase_angle)[..., None, None]
    sine_part = jnp.sin(phase_angle)[..., None, None]
    return jnp.concatenate([rectified * cosine, rectified * sine_part], axis=-1)

def layer_norm(resid, gain_vec, shift_vec):
    row_mean = lax.optimization_barrier(jnp.mean(resid, axis=-1, keepdims=True))
    centered = resid - row_mean
    variance = lax.optimization_barrier(jnp.mean(centered * centered, axis=-1, keepdims=True))
    return centered * lax.rsqrt(variance + norm_eps) * gain_vec + shift_vec

def tree_forward(tree_in, params, parents_row):
    query_weight, key_weight, value_weight, out_weight, up_weight, down_weight, first_gain, first_shift, second_gain, second_shift = params
    tree_len = tree_in.shape[0]
    slot_ids = jnp.arange(tree_len, dtype=jnp.int32)
    segment, owner_branch, phase_angle = layout_of(slot_ids, parents_row, tree_len)

    def project(weight):
        return jnp.dot(tree_in, weight, precision=precise).reshape(tree_len, HEADS, HEAD_DIM)
    query_feat = low(features(low_back(project(query_weight)), phase_angle))
    key_feat = low(features(low_back(project(key_weight)), phase_angle))
    values = low(low_back(project(value_weight)))
    block_rows = min(tree_len, 512)
    block_count = tree_len // block_rows

    def attend(block_index):
        row_start = block_index * block_rows
        query_rows = lax.dynamic_slice_in_dim(query_feat, row_start, block_rows, 0)
        slot_rows = lax.dynamic_slice_in_dim(slot_ids, row_start, block_rows, 0)
        segment_rows = lax.dynamic_slice_in_dim(segment, row_start, block_rows, 0)
        owner_rows = lax.dynamic_slice_in_dim(owner_branch, row_start, block_rows, 0)
        allowed = (slot_ids[None, :] <= slot_rows[:, None]) & ((segment[None, :] == segment_rows[:, None]) | (segment[None, :] == 0) | (segment[None, :] == owner_rows[:, None]))
        scores = jnp.einsum('ihf,jhf->hij', query_rows, key_feat, precision=precise) * allowed[None].astype(jnp.float32)
        numerator = jnp.einsum('hij,jhd->ihd', scores, values, precision=precise)
        denominator = lax.optimization_barrier(jnp.sum(scores, axis=2)).T
        return numerator / jnp.maximum(denominator, 1.0)[:, :, None]
    attended = lax.map(jax.checkpoint(attend), jnp.arange(block_count, dtype=jnp.int32)).reshape(tree_len, HEADS, HEAD_DIM)
    mixed = low(low_back(attended)).reshape(tree_len, N_TENSOR, D // N_TENSOR)
    out_parts = jnp.einsum('tgc,gcd->gtd', mixed, out_weight.reshape(N_TENSOR, D // N_TENSOR, D), precision=precise)
    resid_one = tree_in + lax.optimization_barrier(jnp.sum(low(low_back(out_parts)), axis=0))
    normed_one = layer_norm(resid_one, first_gain, first_shift)
    hidden_pre = low_back(jnp.dot(low(normed_one), up_weight, precision=precise))
    activated = low(jax.nn.gelu(hidden_pre, approximate=False)).reshape(tree_len, N_TENSOR, FF // N_TENSOR)
    ffn_parts = jnp.einsum('tgc,gcd->gtd', activated, down_weight.reshape(N_TENSOR, FF // N_TENSOR, D), precision=precise)
    resid_two = normed_one + lax.optimization_barrier(jnp.sum(low(low_back(ffn_parts)), axis=0))
    return layer_norm(resid_two, second_gain, second_shift)

def full_forward(layer_in, params, parents):
    checked = jax.checkpoint(tree_forward)

    def one_tree(carried, tree_item):
        return (carried, checked(tree_item[0], params, tree_item[1]))
    _, result = lax.scan(one_tree, jnp.zeros((), jnp.float32), (layer_in, parents))
    return result

def reference(layer_input, teacher, query_weight, key_weight, value_weight, out_weight, up_weight, down_weight, first_gain, first_shift, second_gain, second_shift, parents, valid_count):
    params = (query_weight.astype(jnp.float32), key_weight.astype(jnp.float32), value_weight.astype(jnp.float32), out_weight.astype(jnp.float32), up_weight.astype(jnp.float32), down_weight.astype(jnp.float32), first_gain.astype(jnp.float32), first_shift.astype(jnp.float32), second_gain.astype(jnp.float32), second_shift.astype(jnp.float32))

    def forward(layer_in, weights):
        return full_forward(layer_in, weights, parents)
    result, pull_back = jax.vjp(forward, layer_input.astype(jnp.float32), params)
    slot_ids = jnp.arange(layer_input.shape[1], dtype=jnp.int32)
    counted = (slot_ids[None, :] < valid_count[:, None]).astype(jnp.float32)[:, :, None]
    residual = (result - teacher.astype(jnp.float32)) * counted
    loss_value = 0.5 * jnp.sum(residual * residual)
    input_grad, weight_grads = pull_back(residual)
    return (result.astype(jnp.bfloat16), input_grad, loss_value, weight_grads[0], weight_grads[1], weight_grads[2], weight_grads[3], weight_grads[4], weight_grads[5], weight_grads[6], weight_grads[7], weight_grads[8], weight_grads[9])
```

```python
import functools
import math

import jax
import jax.numpy as jnp
from jax import lax
from jax.experimental import pallas as pl
from jax.experimental.pallas import tpu as pltpu
from jax.sharding import PartitionSpec as P

HEAD_DIM = 64


precise = lax.Precision.HIGHEST
norm_eps = 1e-05


def carried_in(array, axis, combine, identity):
    count, here = (lax.axis_size(axis), lax.axis_index(axis))
    everything = jax.tree.map(
        lambda part, kind: lax.all_gather(part.astype(kind), axis),
        array,
        (jnp.bfloat16, jnp.bfloat16),
    )
    start = jax.tree.map(
        lambda part, zero: jnp.broadcast_to(jnp.asarray(zero, part.dtype), part.shape),
        array,
        identity,
    )

    def carried_turn(k, before):
        reached = k < here
        new = combine(
            before, jax.tree.map(lambda part, own: part[k].astype(own.dtype), everything, array)
        )
        return jax.tree.map(lambda a, b: jnp.where(reached, a, b), new, before)

    return lax.fori_loop(0, count, carried_turn, start)


def entering(array, axis, combine, identity):
    count, here = (lax.axis_size(axis), lax.axis_index(axis))
    everything = jax.tree.map(
        lambda part, kind: lax.all_gather(part.astype(kind), axis),
        array,
        jax.tree.map(lambda a: jnp.bfloat16 if a.dtype == jnp.float32 else a.dtype, array),
    )
    start = jax.tree.map(
        lambda part, zero: jnp.broadcast_to(jnp.asarray(zero, part.dtype), part.shape),
        array,
        identity,
    )

    def entering_turn(k, before):
        at = count - 1 - k
        reached = at > here
        new = combine(
            before, jax.tree.map(lambda part, own: part[at].astype(own.dtype), everything, array)
        )
        return jax.tree.map(lambda a, b: jnp.where(reached, a, b), new, before)

    return lax.fori_loop(0, count, entering_turn, start)


def layout_of(slot_ids, parents_row, tree_len):
    half_len = tree_len // 2
    branch_len = tree_len // 16
    leaf_len = tree_len // 32
    leaf_start = half_len + 4 * branch_len
    in_branch = (slot_ids >= half_len) & (slot_ids < leaf_start)
    in_leaf = slot_ids >= leaf_start
    branch_index = jnp.clip((slot_ids - half_len) // branch_len, 0, 3)
    leaf_index = jnp.clip((slot_ids - leaf_start) // leaf_len, 0, 7)
    leaf_ids = jnp.arange(8, dtype=jnp.int32)
    leaf_parent = jnp.sum(
        jnp.where(leaf_index[:, None] == leaf_ids[None, :], parents_row[None, :], 0), axis=1
    )
    segment = jnp.where(in_leaf, 5 + leaf_index, jnp.where(in_branch, 1 + branch_index, 0))
    owner_branch = jnp.where(in_leaf, leaf_parent, jnp.where(in_branch, 1 + branch_index, 0))
    leaf_pos = (
        half_len
        + jnp.where(leaf_parent > 0, branch_len, 0)
        + slot_ids
        - leaf_start
        - leaf_index * leaf_len
    )
    branch_pos = slot_ids - branch_index * branch_len
    position = jnp.where(in_leaf, leaf_pos, jnp.where(in_branch, branch_pos, slot_ids))
    phase_angle = (
        0.5 * math.pi * position.astype(jnp.float32) / float(half_len + branch_len + leaf_len)
    )
    return (segment, owner_branch, phase_angle)


def features(pre_act, phase_angle):
    rectified = jnp.maximum(pre_act, 0.0)
    cosine = jnp.cos(phase_angle)[..., None, None]
    sine_part = jnp.sin(phase_angle)[..., None, None]
    return jnp.concatenate([rectified * cosine, rectified * sine_part], axis=-1)


def features_back(grad_feat, pre_act, phase_angle):
    half_dim = pre_act.shape[-1]
    cosine = jnp.cos(phase_angle)[..., None, None]
    sine_part = jnp.sin(phase_angle)[..., None, None]
    combined = grad_feat[..., :half_dim] * cosine + grad_feat[..., half_dim:] * sine_part
    return jnp.where(pre_act > 0.0, combined, 0.0)


def norm_forward(resid, gain_vec, shift_vec):
    row_mean = jnp.mean(resid, axis=-1, keepdims=True)
    centered = resid - row_mean
    inv_std = lax.rsqrt(jnp.mean(centered * centered, axis=-1, keepdims=True) + norm_eps)
    normal = centered * inv_std
    return (normal * gain_vec + shift_vec, normal, inv_std)


def norm_backward(grad_out, normal, inv_std, gain_vec):
    scaled = grad_out * gain_vec
    grad_in = inv_std * (
        scaled
        - jnp.mean(scaled, axis=-1, keepdims=True)
        - normal * jnp.mean(scaled * normal, axis=-1, keepdims=True)
    )
    return (grad_in, jnp.sum(grad_out * normal, axis=0), jnp.sum(grad_out, axis=0))


def add_pair(earlier, later):
    return (earlier[0] + later[0], earlier[1] + later[1])


def general_shards(
    layer_input,
    teacher,
    query_weight,
    key_weight,
    value_weight,
    out_weight,
    up_weight,
    down_weight,
    first_gain,
    first_shift,
    second_gain,
    second_shift,
    parents,
    valid_count,
):
    tree_count, slot_count, model_width = layer_input.shape
    ctx_size = lax.axis_size(CONTEXT)
    ctx_index = lax.axis_index(CONTEXT)
    tree_len = slot_count * ctx_size
    row_count = tree_count * slot_count
    (
        full_query,
        full_key,
        full_value,
        full_out,
        full_up,
        full_down,
        gain_one,
        shift_one,
        gain_two,
        shift_two,
    ) = (
        lax.all_gather(query_weight, FSDP, axis=0, tiled=True),
        lax.all_gather(key_weight, FSDP, axis=0, tiled=True),
        lax.all_gather(value_weight, FSDP, axis=0, tiled=True),
        lax.all_gather(out_weight, FSDP, axis=1, tiled=True),
        lax.all_gather(up_weight, FSDP, axis=0, tiled=True),
        lax.all_gather(down_weight, FSDP, axis=1, tiled=True),
        lax.all_gather(first_gain, FSDP, axis=0, tiled=True),
        lax.all_gather(first_shift, FSDP, axis=0, tiled=True),
        lax.all_gather(second_gain, FSDP, axis=0, tiled=True),
        lax.all_gather(second_shift, FSDP, axis=0, tiled=True),
    )
    gain_one = gain_one.astype(jnp.float32)
    shift_one = shift_one.astype(jnp.float32)
    gain_two = gain_two.astype(jnp.float32)
    shift_two = shift_two.astype(jnp.float32)
    head_local = full_query.shape[1] // HEAD_DIM
    flat_in = layer_input.reshape(row_count, model_width)
    slot_ids = ctx_index * slot_count + jnp.arange(slot_count, dtype=jnp.int32)

    def layout_here(parents_row):
        return layout_of(slot_ids, parents_row, tree_len)

    segment, owner_branch, phase_angle = jax.vmap(layout_here)(parents)

    def project(weight):
        return jnp.dot(flat_in, weight, preferred_element_type=jnp.float32).reshape(
            tree_count, slot_count, head_local, HEAD_DIM
        )

    query_pre = project(full_query)
    key_pre = project(full_key)
    values = project(full_value).astype(jnp.bfloat16)
    query_feat = features(query_pre, phase_angle).astype(jnp.bfloat16)
    key_feat = features(key_pre, phase_angle).astype(jnp.bfloat16)
    query_wide = query_feat.astype(jnp.float32)
    key_wide = key_feat.astype(jnp.float32)
    value_wide = values.astype(jnp.float32)
    state_ids = jnp.arange(5, dtype=jnp.int32)
    segment_hit = segment[:, :, None] == state_ids
    in_segment = segment_hit.astype(jnp.float32)
    selected = ((state_ids == 0) | (owner_branch[:, :, None] == state_ids)).astype(jnp.float32)
    masked_key = jnp.where(
        segment_hit[:, :, :, None, None], key_feat[:, :, None], jnp.zeros((), jnp.bfloat16)
    )
    contrib_state = jnp.einsum(
        "tsahf,tshd->tahfd", masked_key, values, preferred_element_type=jnp.float32
    )
    contrib_norm = jnp.einsum(
        "tsa,tshf->tahf",
        segment_hit.astype(jnp.bfloat16),
        key_feat,
        preferred_element_type=jnp.float32,
    )
    zero_state = jnp.zeros_like(contrib_state)
    zero_norm = jnp.zeros_like(contrib_norm)
    prior_state, prior_norm = carried_in(
        (contrib_state, contrib_norm), CONTEXT, add_pair, (zero_state, zero_norm)
    )
    in_numer = jnp.einsum(
        "tsa,tshf,tahfd->tshd", selected, query_wide, prior_state, precision=precise
    )
    in_denom = jnp.einsum("tsa,tshf,tahf->tsh", selected, query_wide, prior_norm, precision=precise)
    block_rows = min(slot_count, 512)
    block_count = slot_count // block_rows

    def block_scores(block_index):
        row_start = block_index * block_rows
        query_rows = lax.dynamic_slice_in_dim(query_feat, row_start, block_rows, 1)
        slot_rows = lax.dynamic_slice_in_dim(slot_ids, row_start, block_rows, 0)
        segment_rows = lax.dynamic_slice_in_dim(segment, row_start, block_rows, 1)
        owner_rows = lax.dynamic_slice_in_dim(owner_branch, row_start, block_rows, 1)
        allowed = (slot_ids[None, None, :] <= slot_rows[None, :, None]) & (
            (segment[:, None, :] == segment_rows[:, :, None])
            | (segment[:, None, :] == 0)
            | (segment[:, None, :] == owner_rows[:, :, None])
        )
        allowed_wide = allowed[:, None].astype(jnp.float32)
        scores = (
            jnp.einsum("tihf,tjhf->thij", query_rows, key_feat, preferred_element_type=jnp.float32)
            * allowed_wide
        )
        return (scores, allowed_wide, query_rows)

    def local_forward(block_index):
        scores, allowed_wide, query_rows = block_scores(block_index)
        numerator = jnp.einsum("thij,tjhd->tihd", scores, value_wide, precision=precise)
        denominator = jnp.transpose(jnp.sum(scores, axis=3), (0, 2, 1))
        return (numerator, denominator)

    local_numer, local_denom = lax.map(local_forward, jnp.arange(block_count, dtype=jnp.int32))

    def unblock(stacked):
        return jnp.moveaxis(stacked, 0, 1).reshape((tree_count, slot_count) + stacked.shape[3:])

    numerator = unblock(local_numer) + in_numer
    denominator = unblock(local_denom) + in_denom
    safe_denom = jnp.maximum(denominator, 1.0)
    attended = numerator / safe_denom[..., None]
    attended_low = attended.astype(jnp.bfloat16).reshape(row_count, head_local * HEAD_DIM)
    attention_part = jnp.dot(attended_low, full_out, preferred_element_type=jnp.float32)
    attention_sum = lax.psum(attention_part.astype(jnp.bfloat16), TENSOR).astype(jnp.float32)
    resid_one = flat_in.astype(jnp.float32) + attention_sum
    normed_one, normal_one, inv_one = norm_forward(resid_one, gain_one, shift_one)
    normed_low = normed_one.astype(jnp.bfloat16)
    hidden_pre = jnp.dot(normed_low, full_up, preferred_element_type=jnp.float32)
    activated = jax.nn.gelu(hidden_pre, approximate=False).astype(jnp.bfloat16)
    ffn_part = jnp.dot(activated, full_down, preferred_element_type=jnp.float32)
    ffn_sum = lax.psum(ffn_part.astype(jnp.bfloat16), TENSOR).astype(jnp.float32)
    resid_two = normed_one + ffn_sum
    result, normal_two, inv_two = norm_forward(resid_two, gain_two, shift_two)
    layer_output = result.astype(jnp.bfloat16).reshape(tree_count, slot_count, model_width)
    valid_rows = (
        (slot_ids[None, :] < valid_count[:, None]).astype(jnp.float32).reshape(row_count, 1)
    )
    residual = (result - teacher.reshape(row_count, model_width).astype(jnp.float32)) * valid_rows
    loss_value = lax.psum(0.5 * jnp.sum(residual * residual), (FSDP, CONTEXT))
    grad_resid_two, second_gain_part, second_shift_part = norm_backward(
        residual, normal_two, inv_two, gain_two
    )
    grad_two_low = grad_resid_two.astype(jnp.bfloat16)
    down_part = jnp.dot(activated.T, grad_two_low, preferred_element_type=jnp.float32)
    grad_act = jnp.dot(grad_two_low, full_down.T, preferred_element_type=jnp.float32)
    cumulative = 0.5 * (1.0 + jax.scipy.special.erf(hidden_pre / math.sqrt(2.0)))
    density = jnp.exp(-0.5 * hidden_pre * hidden_pre) / math.sqrt(2.0 * math.pi)
    grad_pre = (grad_act * (cumulative + hidden_pre * density)).astype(jnp.bfloat16)
    up_part = jnp.dot(normed_low.T, grad_pre, preferred_element_type=jnp.float32)
    ffn_back = jnp.dot(grad_pre, full_up.T, preferred_element_type=jnp.float32)
    grad_normed_one = grad_resid_two + lax.psum(ffn_back.astype(jnp.bfloat16), TENSOR).astype(
        jnp.float32
    )
    grad_resid_one, first_gain_part, first_shift_part = norm_backward(
        grad_normed_one, normal_one, inv_one, gain_one
    )
    grad_one_low = grad_resid_one.astype(jnp.bfloat16)
    out_part = jnp.dot(attended_low.T, grad_one_low, preferred_element_type=jnp.float32)
    grad_attended = jnp.dot(grad_one_low, full_out.T, preferred_element_type=jnp.float32).astype(
        jnp.bfloat16
    )
    grad_attended = grad_attended.astype(jnp.float32).reshape(
        tree_count, slot_count, head_local, HEAD_DIM
    )
    grad_numer = grad_attended / safe_denom[..., None]
    grad_denom = jnp.where(
        denominator > 1.0, -jnp.sum(grad_attended * attended, axis=-1) / safe_denom, 0.0
    )
    grad_query = jnp.einsum(
        "tsa,tshd,tahfd->tshf", selected, grad_numer, prior_state, precision=precise
    ) + jnp.einsum("tsa,tsh,tahf->tshf", selected, grad_denom, prior_norm, precision=precise)
    grad_prior_state = jnp.einsum(
        "tsa,tshf,tshd->tahfd", selected, query_wide, grad_numer, precision=precise
    )
    grad_prior_norm = jnp.einsum(
        "tsa,tshf,tsh->tahf", selected, query_wide, grad_denom, precision=precise
    )
    grad_contrib_state, grad_contrib_norm = entering(
        (grad_prior_state, grad_prior_norm), CONTEXT, add_pair, (zero_state, zero_norm)
    )
    grad_key = jnp.einsum(
        "tsa,tshd,tahfd->tshf", in_segment, value_wide, grad_contrib_state, precision=precise
    ) + jnp.einsum("tsa,tahf->tshf", in_segment, grad_contrib_norm, precision=precise)
    grad_value = jnp.einsum(
        "tsa,tshf,tahfd->tshd", in_segment, key_wide, grad_contrib_state, precision=precise
    )

    def local_backward(carried, block_index):
        acc_key, acc_value = carried
        scores, allowed_wide, query_rows = block_scores(block_index)
        row_start = block_index * block_rows
        numer_rows = lax.dynamic_slice_in_dim(grad_numer, row_start, block_rows, 1)
        denom_rows = lax.dynamic_slice_in_dim(grad_denom, row_start, block_rows, 1)
        grad_scores = (
            jnp.einsum("tihd,tjhd->thij", numer_rows, value_wide, precision=precise)
            + jnp.transpose(denom_rows, (0, 2, 1))[:, :, :, None]
        ) * allowed_wide
        rows_grad = jnp.einsum("thij,tjhf->tihf", grad_scores, key_wide, precision=precise)
        acc_key = acc_key + jnp.einsum(
            "thij,tihf->tjhf", grad_scores, query_rows.astype(jnp.float32), precision=precise
        )
        acc_value = acc_value + jnp.einsum("thij,tihd->tjhd", scores, numer_rows, precision=precise)
        return ((acc_key, acc_value), rows_grad)

    (local_key, local_value), local_query = lax.scan(
        local_backward,
        (jnp.zeros_like(key_wide), jnp.zeros_like(value_wide)),
        jnp.arange(block_count, dtype=jnp.int32),
    )
    grad_query = grad_query + unblock(local_query)
    grad_key = grad_key + local_key
    grad_value = grad_value + local_value
    grad_query_low = (
        features_back(grad_query, query_pre, phase_angle)
        .astype(jnp.bfloat16)
        .reshape(row_count, -1)
    )
    grad_key_low = (
        features_back(grad_key, key_pre, phase_angle).astype(jnp.bfloat16).reshape(row_count, -1)
    )
    grad_value_low = grad_value.astype(jnp.bfloat16).reshape(row_count, -1)
    query_part = jnp.dot(flat_in.T, grad_query_low, preferred_element_type=jnp.float32)
    key_part = jnp.dot(flat_in.T, grad_key_low, preferred_element_type=jnp.float32)
    value_part = jnp.dot(flat_in.T, grad_value_low, preferred_element_type=jnp.float32)
    input_back = (
        jnp.dot(grad_query_low, full_query.T, preferred_element_type=jnp.float32)
        + jnp.dot(grad_key_low, full_key.T, preferred_element_type=jnp.float32)
        + jnp.dot(grad_value_low, full_value.T, preferred_element_type=jnp.float32)
    )
    input_grad = (
        grad_resid_one + lax.psum(input_back.astype(jnp.bfloat16), TENSOR).astype(jnp.float32)
    ).reshape(tree_count, slot_count, model_width)
    grad_parts = (
        query_part,
        key_part,
        value_part,
        out_part,
        up_part,
        down_part,
        first_gain_part,
        first_shift_part,
        second_gain_part,
        second_shift_part,
    )
    summed = (
        lax.psum(grad_parts[0].astype(jnp.bfloat16), CONTEXT).astype(jnp.float32),
        lax.psum(grad_parts[1].astype(jnp.bfloat16), CONTEXT).astype(jnp.float32),
        lax.psum(grad_parts[2].astype(jnp.bfloat16), CONTEXT).astype(jnp.float32),
        lax.psum(grad_parts[3].astype(jnp.bfloat16), CONTEXT).astype(jnp.float32),
        lax.psum(grad_parts[4].astype(jnp.bfloat16), CONTEXT).astype(jnp.float32),
        lax.psum(grad_parts[5].astype(jnp.bfloat16), CONTEXT).astype(jnp.float32),
        lax.psum(grad_parts[6].astype(jnp.bfloat16), CONTEXT).astype(jnp.float32),
        lax.psum(grad_parts[7].astype(jnp.bfloat16), CONTEXT).astype(jnp.float32),
        lax.psum(grad_parts[8].astype(jnp.bfloat16), CONTEXT).astype(jnp.float32),
        lax.psum(grad_parts[9].astype(jnp.bfloat16), CONTEXT).astype(jnp.float32),
    )
    reduced = (
        lax.psum_scatter(
            summed[0].astype(jnp.bfloat16), FSDP, scatter_dimension=0, tiled=True
        ).astype(jnp.float32),
        lax.psum_scatter(
            summed[1].astype(jnp.bfloat16), FSDP, scatter_dimension=0, tiled=True
        ).astype(jnp.float32),
        lax.psum_scatter(
            summed[2].astype(jnp.bfloat16), FSDP, scatter_dimension=0, tiled=True
        ).astype(jnp.float32),
        lax.psum_scatter(
            summed[3].astype(jnp.bfloat16), FSDP, scatter_dimension=1, tiled=True
        ).astype(jnp.float32),
        lax.psum_scatter(
            summed[4].astype(jnp.bfloat16), FSDP, scatter_dimension=0, tiled=True
        ).astype(jnp.float32),
        lax.psum_scatter(
            summed[5].astype(jnp.bfloat16), FSDP, scatter_dimension=1, tiled=True
        ).astype(jnp.float32),
        lax.psum_scatter(
            summed[6].astype(jnp.bfloat16), FSDP, scatter_dimension=0, tiled=True
        ).astype(jnp.float32),
        lax.psum_scatter(
            summed[7].astype(jnp.bfloat16), FSDP, scatter_dimension=0, tiled=True
        ).astype(jnp.float32),
        lax.psum_scatter(
            summed[8].astype(jnp.bfloat16), FSDP, scatter_dimension=0, tiled=True
        ).astype(jnp.float32),
        lax.psum_scatter(
            summed[9].astype(jnp.bfloat16), FSDP, scatter_dimension=0, tiled=True
        ).astype(jnp.float32),
    )
    return (
        layer_output,
        input_grad,
        loss_value,
        reduced[0],
        reduced[1],
        reduced[2],
        reduced[3],
        reduced[4],
        reduced[5],
        reduced[6],
        reduced[7],
        reduced[8],
        reduced[9],
    )


MESH_ID = pl.DeviceIdType.MESH
ROWS = 512
CORE, YY, XX, Z0, Z1, FIN = range(6)
FSDP, CONTEXT, TENSOR = "fsdp", "context", "tensor"
ST = 80


def fast_kernel(*refs, tree_len, stop=99):
    (x_hbm, t_hbm, w_in, n_in, par, val,
     lo_hbm, ig_hbm, gout, small,
     G, NG, xv, qf, kf, vx, mk, mkT, cs, nl, att, n1, inv1, nlow, act, der, acc, glow, gT, nT, xT,
     SR, PS, TTb, RR, dE, RX, K, RC, STG, RBD, RBU, sm, smr, ss, rs, ls) = refs
    f = lax.axis_index(FSDP)
    c = lax.axis_index(CONTEXT)
    t = lax.axis_index(TENSOR)
    t1 = t + 1 - 2 * lax.rem(t, 2)
    t2 = lax.rem(t + 2, 4)
    t3 = lax.rem(t1 + 2, 4)
    f1 = f + 1 - 2 * lax.rem(f, 2)
    f2 = lax.rem(f + 2, 4)
    f3 = lax.rem(f1 + 2, 4)
    c1 = 1 - c
    tks = [t, t2, t1, t3]
    DEV = {CORE: {TENSOR: t1}, YY: {TENSOR: t2}, XX: {CONTEXT: c1}, Z0: {FSDP: f1}, Z1: {FSDP: f2}}
    D = 768
    counter = [0]

    def rcopy(src, dst, dev):
        i = counter[0]
        counter[0] += 1
        return pltpu.make_async_remote_copy(
            src_ref=src, dst_ref=dst, send_sem=ss.at[i], recv_sem=rs.at[i],
            device_id=DEV[dev], device_id_type=MESH_ID)

    lcounter = [0]

    def lcopy(src, dst):
        i = lcounter[0]
        lcounter[0] += 1
        return pltpu.make_async_copy(src, dst, ls.at[i])

    def start(cps):
        for cp in cps:
            cp.start()

    def wait_recv(cps):
        for cp in cps:
            cp.wait_recv()

    pending = []

    def send(cps):
        start(cps)
        pending.extend(cps)
        return cps

    def done(cp):
        pending[:] = [other for other in pending if other is not cp]

    f32, bf16 = jnp.float32, jnp.bfloat16

    def dot(a, b):
        return lax.dot_general(a, b, (((1,), (0,)), ((), ())), preferred_element_type=f32)

    def dot_nt(a, b):
        return lax.dot_general(a, b, (((1,), (1,)), ((), ())), preferred_element_type=f32)

    bar = pltpu.get_barrier_semaphore()
    for dev in DEV.values():
        pl.semaphore_signal(bar, inc=1, device_id=dev, device_id_type=MESH_ID)

    row0 = pl.multiple_of(t * ROWS, ROWS)
    lx = lcopy(x_hbm.at[0, pl.ds(row0, ROWS), :], xv)
    lt = lcopy(t_hbm.at[0, pl.ds(row0, ROWS), :], xv)
    tv = lob = xv
    igb = nlow
    own = [lcopy(w_in.at[m], G.at[m, t, f]) for m in range(3)]
    lng = lcopy(n_in, NG.at[f])
    start([lx] + own + [lng])
    for cp in own + [lng]:
        cp.wait()
    pl.semaphore_wait(bar, 5)

    class Gather:
        def __init__(self, m, l0, n, order, split):
            self.lanes = slice(None) if n == D else pl.ds(l0, n)
            self.m, self.order = m, order
            self.ts, self.fs = [t], [f]
            self.h = c if split else None
            self.stages = {}
            for stage in order:
                self.stages[stage] = self.build(stage)

        def at(self, ti, fi, h):
            hh = slice(None) if h is None else h
            return G.at[self.m, ti, fi, hh, slice(None), self.lanes]

        def build(self, stage):
            regs = []
            fl = [slice(None)] if len(self.fs) == 4 else self.fs
            if stage == XX:
                for ti in self.ts:
                    if ti is t:
                        others = [fi for fi in self.fs if fi is not f]
                        regs += [(ti, fi, c) for fi in others]
                    else:
                        regs += [(ti, fi, c) for fi in fl]
                self.h = None
            else:
                regs = [(ti, fi, self.h) for ti in self.ts for fi in fl]
                if stage == Z1:
                    self.fs = self.fs + [{id(f): f2, id(f1): f3}[id(v)] for v in self.fs]
                if stage == Z0:
                    self.fs = self.fs + [{id(f): f1, id(f2): f3}[id(v)] for v in self.fs]
                if stage == YY:
                    self.ts = self.ts + [t2]
                if stage == CORE:
                    self.ts = self.ts + [t1, t3]
            return [rcopy(self.at(*r), self.at(*r), stage) for r in regs]

        def go(self, stage):
            send(self.stages[stage])

        def got(self, stage):
            wait_recv(self.stages[stage])

    O1 = (Z1, Z0, YY, XX, CORE)
    O3 = (YY, Z1, Z0, XX, CORE)
    O4 = (Z1, Z0, YY, CORE)
    ga = [Gather(0, 0, 256, O1, True), Gather(0, 256, 256, O3, True), Gather(0, 512, 256, O4, False)]
    gu = Gather(1, 0, D, O4, False)
    gd = Gather(2, 0, D, O1, True)
    ngz1 = [rcopy(NG.at[f], NG.at[f], Z1)]
    ngz0 = [rcopy(NG.at[f], NG.at[f], Z0), rcopy(NG.at[f2], NG.at[f2], Z0)]

    a1, a3, a4 = ga
    a1.go(Z1)
    a3.go(YY)
    a4.go(Z1)
    send(ngz1)

    lane = lax.broadcasted_iota(jnp.int32, (ROWS, 128), 1)
    low_half = lane < 64
    half_len, branch_len, leaf_len = tree_len // 2, tree_len // 16, tree_len // 32
    leaf_start = half_len + 4 * branch_len
    base_slot = c * (4 * ROWS) + t * ROWS

    def layout(slot):
        in_leaf = slot >= leaf_start
        in_branch = (slot >= half_len) & jnp.logical_not(in_leaf)
        bi = jnp.clip((slot - half_len) >> (branch_len.bit_length() - 1), 0, 3)
        li = jnp.clip((slot - leaf_start) >> (leaf_len.bit_length() - 1), 0, 7)
        lp = jnp.zeros_like(slot)
        for k in range(8):
            lp = jnp.where(li == k, par[0, k], lp)
        seg = jnp.where(in_leaf, 5 + li, jnp.where(in_branch, 1 + bi, 0))
        own_b = jnp.where(in_leaf, lp, jnp.where(in_branch, 1 + bi, 0))
        leaf_pos = half_len + jnp.where(lp > 0, branch_len, 0) + slot - leaf_start - li * leaf_len
        posn = jnp.where(in_leaf, leaf_pos, jnp.where(in_branch, slot - bi * branch_len, slot))
        return seg, own_b, posn

    slot_col = base_slot + lax.broadcasted_iota(jnp.int32, (ROWS, 128), 0)
    seg_c, own_c, pos_c = layout(slot_col)
    ang = 0.5 * math.pi * pos_c.astype(f32) / float(half_len + branch_len + leaf_len)
    cs[...] = jnp.where(low_half, jnp.cos(ang), jnp.sin(ang))
    slot_row = base_slot + lax.broadcasted_iota(jnp.int32, (8, ROWS), 1)
    seg_r8, own_r8, _ = layout(slot_row)
    seg_r, own_r, sl_r = seg_r8[0:1], own_r8[0:1], slot_row[0:1]
    for j in range(4):
        ls_ = slice(j * 128, j * 128 + 128)
        sr, orr, slr = seg_r[:, ls_], own_r[:, ls_], sl_r[:, ls_]
        ok = (slr <= slot_col) & ((sr == seg_c) | (sr == 0) | (sr == own_c))
        mk[:, ls_] = jnp.where(ok, 1.0, 0.0).astype(bf16)
        okT = (slot_col <= slr) & ((seg_c == sr) | (seg_c == 0) | (seg_c == orr))
        mkT[:, ls_] = jnp.where(okT, 1.0, 0.0).astype(bf16)
    lx.wait()
    for j in range(3):
        xT[j * 256:(j + 1) * 256, :] = jnp.transpose(xv[:, j * 256:(j + 1) * 256])

    a1.got(Z1)
    a1.go(Z0)
    a4.got(Z1)
    a4.go(Z0)
    a3.got(YY)
    a3.go(Z1)
    wait_recv(ngz1)
    send(ngz0)
    a1.got(Z0)
    a1.go(YY)
    a4.got(Z0)
    a4.go(YY)
    a3.got(Z1)
    a3.go(Z0)
    gu.go(Z1)
    a1.got(YY)
    a1.go(XX)
    a3.got(Z0)
    a3.go(XX)
    gd.go(Z1)
    gu.got(Z1)
    gu.go(Z0)
    a4.got(YY)
    a4.go(CORE)
    a1.got(XX)
    a1.go(CORE)
    gd.got(Z1)
    gd.go(Z0)
    a3.got(XX)
    a3.go(CORE)
    gu.got(Z0)
    gu.go(YY)

    def Gv(m, tk, l0, n):
        return G[m, tk, :, :, :, l0:l0 + n].reshape(D, n)

    def Gd(m, tk, n0, n):
        return G[m, tk, :, :, :, pl.ds(n0, n)].reshape(D, n)

    def qkv(tk):
        csv = cs[...]
        h = tk * 3

        def lo(p):
            return (jnp.where(low_half, p, pltpu.roll(p, 64, 1)) * csv).astype(bf16)

        def hi(p):
            return (jnp.where(low_half, pltpu.roll(p, 64, 1), p) * csv).astype(bf16)

        def vext(p, up):
            p = pltpu.roll(p, 64, 1) if up else p
            return jnp.where(low_half, p, jnp.where(lane == 64, 1.0, 0.0)).astype(bf16)

        a = jnp.maximum(dot(xv[...], Gv(0, tk, 0, 256)), 0.0)
        qf[h] = lo(a[:, :128])
        qf[h + 1] = hi(a[:, :128])
        kf[h] = lo(a[:, 128:])
        kf[h + 1] = hi(a[:, 128:])
        b = dot(xv[...], Gv(0, tk, 256, 256))
        vx[h] = vext(b[:, :128], False)
        vx[h + 1] = vext(b[:, :128], True)
        r = jnp.maximum(b[:, 128:], 0.0)
        qf[h + 2] = lo(r)
        kf[h + 2] = hi(r)
        vx[h + 2] = vext(dot(xv[...], Gv(0, tk, 512, 128)), False)
        for j in range(3):
            vT = jnp.transpose(vx[h + j].astype(f32)).astype(bf16)
            u0 = dot(vT[:ST, :256], kf[h + j, :256])
            u1 = dot(vT[:ST, 256:], kf[h + j, 256:])
            first = jnp.where(c == 0, u0 + u1, u0)
            dE[0, h + j] = first.astype(bf16)
            dE[1, h + j] = u1.astype(bf16)

    qkv(tks[0])
    qkv(tks[1])
    for g in (a4, a1, a3):
        g.got(CORE)
    gd.got(Z0)
    gd.go(YY)
    qkv(tks[2])
    qkv(tks[3])

    fy0 = [rcopy(dE.at[0], SR.at[0], YY)]
    fy1 = [rcopy(dE.at[pl.ds(0, 2)], SR.at[pl.ds(0, 2)], YY)]
    fc0 = [rcopy(dE.at[0], SR.at[2], CORE), rcopy(SR.at[0], SR.at[4], CORE)]
    fc1 = [rcopy(SR.at[pl.ds(0, 2)], SR.at[pl.ds(4, 2)], CORE)]
    fx = [rcopy(TTb, PS, XX)]

    @pl.when(c == 0)
    def _():
        start(fy0)
        start(fc0[:1])

    @pl.when(c == 1)
    def _():
        start(fy1)

    def local_fwd(h, _):
        s = dot_nt(qf[h], kf[h]).astype(bf16) * mk[...]
        nl[h] = dot(s, vx[h])
        return 0

    lax.fori_loop(0, 6, local_fwd, 0)

    @pl.when(c == 0)
    def _():
        wait_recv(fy0)
        start(fc0[1:])
        wait_recv(fc0)

        def pre(h, _):
            r2, r1, r3 = SR[0, h].astype(f32), SR[2, h].astype(f32), SR[4, h].astype(f32)
            zero = jnp.zeros_like(r2)
            p = jnp.where(t2 < t, r2, zero) + jnp.where(t1 < t, r1, zero) + jnp.where(t3 < t, r3, zero)
            PS[h] = p.astype(bf16)
            TTb[h] = (r2 + r1 + r3 + dE[0, h].astype(f32)).astype(bf16)
            return 0

        lax.fori_loop(0, 12, pre, 0)
        start(fx)
        for cp in fy0 + fc0:
            cp.wait_send()

    @pl.when(c == 1)
    def _():
        wait_recv(fy1)
        start(fc1)

    gu.got(YY)
    gu.go(CORE)
    gd.got(YY)
    gd.go(XX)
    lax.fori_loop(6, 12, local_fwd, 0)

    @pl.when(c == 0)
    def _():
        for cp in fx:
            cp.wait_send()

    @pl.when(c == 1)
    def _():
        wait_recv(fc1)
        for cp in fx:
            cp.wait_recv()
        for cp in fy1 + fc1:
            cp.wait_send()

    is_leafdev = (c == 1) & (t >= 2)

    def leaf_parent(i):
        k = 4 * lax.rem(t, 2)
        v = par[0, i]
        w = par[0, 4 + i]
        return jnp.where(is_leafdev, jnp.where(k == 0, v, w), 0)

    low_base = jnp.where(t == 2, 0, 4)
    high_base = jnp.where(t == 2, 4, 0)

    def chunk_state(h, lp):
        s = PS[h].astype(f32)
        zero = jnp.zeros_like(s)
        s = s + jnp.where(lp == 1, SR[low_base, h].astype(f32), zero)
        s = s + jnp.where(lp == 2, SR[low_base + 1, h].astype(f32), zero)
        s = s + jnp.where(lp == 3, SR[high_base, h].astype(f32), zero)
        s = s + jnp.where(lp == 4, SR[high_base + 1, h].astype(f32), zero)
        s = s.astype(bf16)
        return jnp.concatenate([s, jnp.zeros((128 - ST, 128), bf16)], axis=0)

    lane_c = lax.broadcasted_iota(jnp.int32, (128, 128), 1)
    low_c = lane_c < 64
    @pl.when(c == 0)
    def _():
        zs = jnp.zeros((12, ST, 128), bf16)
        SR[1] = zs
        SR[5] = zs
        RR[5] = zs

    @pl.when(c == 1)
    def _():
        RX[...] = jnp.zeros((12, ST, 128), bf16)

    def prior_fwd(tt, _):
        for i in range(4):
            lp = leaf_parent(i)
            rows = pl.ds(i * 128, 128)
            outs = []
            for j in range(3):
                h = tt * 3 + j
                tot = nl[h, rows, :] + dot_nt(qf[h, rows, :], chunk_state(h, lp))
                den = jnp.broadcast_to(tot[:, 64:65], (128, 128))
                a = tot / jnp.maximum(den, 1.0)
                nl[h, rows, :] = jnp.where(low_c, a, den)
                outs.append(a)
            att[tt, rows, 0:128] = jnp.where(low_c, 0.0, pltpu.roll(outs[2], 64, 1)).astype(bf16)
            att[tt, rows, 128:256] = jnp.where(low_c, outs[0], pltpu.roll(outs[1], 64, 1)).astype(bf16)
        return 0

    lax.fori_loop(0, 4, prior_fwd, 0)

    acc[...] = xv[...].astype(f32)
    lt.start()

    def outp(tt, _):
        acc[...] += dot_nt(att[tt], Gv(0, tt, 512, 256))
        return 0

    lax.fori_loop(0, 4, outp, 0)
    wait_recv(ngz0)
    gains = sum(NG[i].astype(f32) for i in range(4))
    gain1, shift1, gain2, shift2 = (gains[i:i + 1] for i in range(4))
    RB_ = 32

    def norm1(i, _):
        rows = pl.ds(pl.multiple_of(i * RB_, RB_), RB_)
        r = acc[rows, :]
        cen = r - jnp.mean(r, axis=1, keepdims=True)
        inv = lax.rsqrt(jnp.mean(cen * cen, axis=1, keepdims=True) + norm_eps)
        nrm = cen * inv
        y = nrm * gain1 + shift1
        n1[rows, :] = nrm
        inv1[rows, :] = jnp.broadcast_to(inv, (RB_, 128))
        acc[rows, :] = y
        nlow[rows, :] = y.astype(bf16)
        return 0

    lax.fori_loop(0, ROWS // RB_, norm1, 0)
    for j in range(3):
        nT[j * 256:(j + 1) * 256, :] = jnp.transpose(nlow[:, j * 256:(j + 1) * 256])

    gu.got(CORE)
    gd.got(XX)
    gd.go(CORE)

    r2_ = 1.0 / math.sqrt(2.0)

    def ffn_up(tt, _):
        for n in range(3):
            hpre = dot(nlow[...], Gv(1, tt, n * 256, 256))
            cum = 0.5 * (1.0 + lax.erf(hpre * r2_))
            dens = jnp.exp(-0.5 * hpre * hpre) * (1.0 / math.sqrt(2.0 * math.pi))
            act[tt, :, n * 256:(n + 1) * 256] = (hpre * cum).astype(bf16)
            der[tt, :, n * 256:(n + 1) * 256] = (cum + hpre * dens).astype(bf16)
        return 0

    lax.fori_loop(0, 4, ffn_up, 0)
    gd.got(CORE)

    def ffn_down(tt, _):
        acc[...] += dot_nt(act[tt], Gv(2, tt, 0, D))
        return 0

    lax.fori_loop(0, 4, ffn_down, 0)

    lt.wait()
    vc = val[0]

    def norm2(i, carry):
        sg, sh, sl = carry
        rows = pl.ds(pl.multiple_of(i * RB_, RB_), RB_)
        r = acc[rows, :]
        cen = r - jnp.mean(r, axis=1, keepdims=True)
        inv = lax.rsqrt(jnp.mean(cen * cen, axis=1, keepdims=True) + norm_eps)
        nrm = cen * inv
        res = nrm * gain2 + shift2
        goal = tv[rows, :].astype(f32)
        lob[rows, :] = res.astype(bf16)
        slot = base_slot + i * RB_ + lax.broadcasted_iota(jnp.int32, (RB_, 1), 0)
        e = jnp.where(slot < vc, res - goal, 0.0)
        sc = e * gain2
        g = inv * (sc - jnp.mean(sc, axis=1, keepdims=True) - nrm * jnp.mean(sc * nrm, axis=1, keepdims=True))
        acc[rows, :] = g
        glow[rows, :] = g.astype(bf16)

        def fold(v):
            return jnp.sum(v.reshape(RB_ // 8, 8, D), axis=0)

        return (sg + fold(e * nrm), sh + fold(e), sl + fold(e * e))

    z8 = jnp.zeros((8, D), f32)
    sg, sh, sl = lax.fori_loop(0, ROWS // RB_, norm2, (z8, z8, z8))
    sm[0:1] = jnp.sum(sg, axis=0, keepdims=True)
    sm[1:2] = jnp.sum(sh, axis=0, keepdims=True)
    sm[2:3] = 0.5 * jnp.sum(sl, axis=0, keepdims=True)
    for j in range(3):
        gT[j * 256:(j + 1) * 256, :] = jnp.transpose(glow[:, j * 256:(j + 1) * 256])

    def rows_of(ti):
        return pl.ds(pl.multiple_of(ti * ROWS, ROWS), ROWS)

    lo_l = lcopy(lob, lo_hbm.at[rows_of(t)])
    lo_l.start()
    lo_y = send([rcopy(lob, lo_hbm.at[rows_of(t)], YY)])
    lo_c = send([rcopy(lob, lo_hbm.at[rows_of(t)], CORE)])
    lo_c2 = [rcopy(lo_hbm.at[rows_of(t2)], lo_hbm.at[rows_of(t2)], CORE)]

    class Reduce:
        def __init__(self, m, order, stg, rc, bufs):
            self.m, self.order, self.stg, self.rc = m, order, stg, rc
            self.core = [rcopy(stg[j], rc[j], CORE) for j in range(2)]
            self.stage = {}
            self.fin = []
            h, sl, fl = None, [0, 1], [f, f1, f2, f3]
            for name in order:
                hh = slice(None) if h is None else h
                if name == XX and len(fl) == 1:
                    src, keep = [K.at[m, 0, f]], [K.at[m, 0, f]]
                elif name == XX:
                    src = [K.at[m, s, :, c1] for s in sl]
                    keep = [K.at[m, s, :, c] for s in sl]
                    h = c
                    self.fin = None
                elif name == YY:
                    fs = [slice(None)] if len(fl) == 4 else fl
                    src = [K.at[m, 1, fi, hh] for fi in fs]
                    keep = [K.at[m, 0, fi, hh] for fi in fs]
                    sl = [0]
                elif name == Z0:
                    src = [K.at[m, s, fi, hh] for s in sl for fi in (f1, f3)]
                    keep = [K.at[m, s, fi, hh] for s in sl for fi in (f, f2)]
                    fl = [f, f2]
                else:
                    src = [K.at[m, s, f2, hh] for s in sl]
                    keep = [K.at[m, s, f, hh] for s in sl]
                    fl = [f]
                dsts = bufs[name]
                self.stage[name] = ([rcopy(p, q, name) for p, q in zip(src, dsts, strict=True)], dsts, keep)
            if self.fin is None:
                self.fin = [rcopy(K.at[m, 0, f, c], bufs[FIN], XX)]

        def send_core(self, j):
            send([self.core[j]])

        def add_core(self, j):
            wait_recv([self.core[j]])
            self.add(self.rc[j], K.at[self.m, j])

        def add(self, src, dst):
            lead = dst.shape[:-2]
            count = math.prod(lead)
            if count == 1:
                dst[...] = (dst[...].astype(f32) + src[...].astype(f32)).astype(bf16)
                return

            def one(i, _):
                idx, rest = [], i
                for n in reversed(lead):
                    idx.append(lax.rem(rest, n))
                    rest = rest // n
                idx = tuple(reversed(idx))
                dst[idx] = (dst[idx].astype(f32) + src[idx].astype(f32)).astype(bf16)
                return 0

            lax.fori_loop(0, count, one, 0)

        def go(self, name):
            send(self.stage[name][0])

        def got(self, name):
            cps, dsts, keep = self.stage[name]
            for cp in cps:
                cp.wait()
                done(cp)
            for p, q in zip(dsts, keep):
                self.add(p, q)

        def finish(self):
            send(self.fin)
            wait_recv(self.fin)

    rD = Reduce(2, (XX, YY, Z0, Z1), [STG.at[0], STG.at[0]], [RC.at[0, 0], RC.at[0, 1]],
                {XX: [RBD.at[pl.ds(0, 4)], RBD.at[pl.ds(4, 4)]], YY: [RBD.at[pl.ds(8, 4)]],
                     Z0: [RBD.at[12], RBD.at[13]], Z1: [RBD.at[14]], FIN: RBD.at[15]})
    rU = Reduce(1, (YY, Z0, Z1, XX), [STG.at[1], STG.at[1]], [RC.at[1, 0], RC.at[1, 1]],
                {YY: [RBU.at[pl.ds(0, 4)]], Z0: [RBU.at[4], RBU.at[5]], Z1: [RBU.at[6]], XX: [RBU.at[7]]})
    rA = Reduce(0, (XX, Z0, Z1, YY), [STG.at[0], STG.at[1]], [G.at[2, 0], G.at[2, 1]],
                {XX: [G.at[1, 0, :, 0], G.at[1, 0, :, 1]], Z0: [G.at[1, 1, i, 0] for i in range(4)],
                     Z1: [G.at[1, 2, i, 0] for i in range(2)], YY: [G.at[1, 3, 0, 0]], FIN: G.at[1, 3, 1, 0]})

    for k in (2, 3, 0, 1):
        tk = tks[k]
        dstD = rD.stg[k - 2] if k >= 2 else K.at[2, k]
        dstU = rU.stg[k - 2] if k >= 2 else K.at[1, k]

        if k == 3:
            for r in (rD, rU):
                r.core[0].wait_send()
                done(r.core[0])

        def blk(n, _):
            n0 = pl.multiple_of(n * 256, 256)
            a = act[tk, :, pl.ds(n0, 256)]
            dstD[:, :, :, pl.ds(n0, 256)] = dot(gT[...], a).reshape(4, 2, 96, 256).astype(bf16)
            g = (dot(glow[...], Gd(2, tk, n0, 256)) * der[tk, :, pl.ds(n0, 256)].astype(f32)).astype(bf16)
            der[tk, :, pl.ds(n0, 256)] = g
            dstU[:, :, :, pl.ds(n0, 256)] = dot(nT[...], g).reshape(4, 2, 96, 256).astype(bf16)
            return 0

        lax.fori_loop(0, 3, blk, 0)
        if k >= 2:
            rD.send_core(k - 2)
            rU.send_core(k - 2)
        acc[...] += dot_nt(der[tk], Gv(1, tk, 0, D))
        if k < 2:
            rD.add_core(k)
            rU.add_core(k)
        if k == 0:
            wait_recv(lo_y)
            send(lo_c2)
    rD.go(XX)
    rU.go(YY)

    def norm1b(i, carry):
        sg, sh = carry
        rows = pl.ds(pl.multiple_of(i * RB_, RB_), RB_)
        e = acc[rows, :]
        nrm = n1[rows, :]
        inv = inv1[rows, 0:1]
        sc = e * gain1
        g = inv * (sc - jnp.mean(sc, axis=1, keepdims=True) - nrm * jnp.mean(sc * nrm, axis=1, keepdims=True))
        acc[rows, :] = g
        glow[rows, :] = g.astype(bf16)

        def fold(v):
            return jnp.sum(v.reshape(RB_ // 8, 8, D), axis=0)

        return (sg + fold(e * nrm), sh + fold(e))

    sg, sh = lax.fori_loop(0, ROWS // RB_, norm1b, (z8, z8))
    sm[3:4] = jnp.sum(sg, axis=0, keepdims=True)
    sm[4:5] = jnp.sum(sh, axis=0, keepdims=True)
    sm[5:8] = jnp.zeros((3, D), f32)
    for j in range(3):
        gT[j * 256:(j + 1) * 256, :] = jnp.transpose(glow[:, j * 256:(j + 1) * 256])

    sms = {}
    for i, d in enumerate((CORE, YY, XX, Z0, Z1)):
        sms[d] = ([rcopy(smr.at[2 * i], smr.at[2 * i + 1], d)], 2 * i)

    def sm_go(d):
        cps, i = sms[d]
        smr[i] = sm[...]
        send(cps)

    def sm_got(d):
        cps, i = sms[d]
        wait_recv(cps)
        sm[...] = sm[...] + smr[i + 1]

    for g in (gu, gd):
        for cps in g.stages.values():
            for cp in cps:
                cp.wait_send()
                done(cp)
    sm_go(CORE)

    def gn_rows(tt, _):
        gae = dot(glow[...], G[0, tt, :, :, :, 512:768].reshape(D, 256)).astype(bf16).astype(f32)
        g2_ = pltpu.roll(gae[:, 0:128], 64, 1)
        g0_ = gae[:, 128:256]
        g1_ = pltpu.roll(g0_, 64, 1)
        for j, g in enumerate((g0_, g1_, g2_)):
            h = tt * 3 + j
            v = nl[h]
            g = jnp.where(low_half, g, 0.0)
            den = jnp.broadcast_to(v[:, 64:65], (ROWS, 128))
            safe = jnp.maximum(den, 1.0)
            s = jnp.sum(g * jnp.where(low_half, v, 0.0), axis=1, keepdims=True)
            gd_ = jnp.where(den > 1.0, -s / safe, 0.0)
            gn = jnp.where(low_half, g / safe, jnp.where(lane == 64, gd_, 0.0))
            nl[h] = gn
            gnT = jnp.transpose(gn).astype(bf16)
            parts = [dot(gnT[:ST, i * 128:(i + 1) * 128], qf[h, i * 128:(i + 1) * 128, :]) for i in range(4)]
            dE[2, h] = (parts[0] + parts[1] + parts[2] + parts[3]).astype(bf16)
            mine = jnp.where(t == 2, 1, 3)
            theirs = jnp.where(t == 2, 3, 1)
            for slot, b in ((0, theirs), (1, theirs + 1), (3, mine), (4, mine + 1)):
                tot = jnp.zeros((ST, 128), f32)
                for i in range(4):
                    tot = tot + jnp.where(leaf_parent(i) == b, parts[i], 0.0)
                dE[slot, h] = tot.astype(bf16)
        return 0

    lax.fori_loop(0, 4, gn_rows, 0)

    bc0 = [rcopy(dE.at[2], RR.at[2], CORE)]
    by0 = [rcopy(dE.at[2], RR.at[3], YY), rcopy(RR.at[2], RR.at[4], YY)]
    bc1 = [rcopy(dE.at[pl.ds(0, 3)], RR.at[pl.ds(0, 3)], CORE)]
    by1 = [rcopy(dE.at[pl.ds(2, 3)], RR.at[pl.ds(3, 3)], YY)]
    bx = [rcopy(TTb, RX, XX)]

    @pl.when(c == 0)
    def _():
        start(bc0 + by0[:1])
        wait_recv(bc0)
        start(by0[1:])
        for cp in bc0:
            cp.wait_send()

    @pl.when(c == 1)
    def _():
        start(bc1)
        for cp in bc1:
            cp.wait()

        def addup(h, _):
            dE[2, h] = (dE[2, h].astype(f32) + RR[2, h].astype(f32)).astype(bf16)
            dE[3, h] = (dE[3, h].astype(f32) + RR[0, h].astype(f32)).astype(bf16)
            dE[4, h] = (dE[4, h].astype(f32) + RR[1, h].astype(f32)).astype(bf16)
            return 0

        lax.fori_loop(0, 12, addup, 0)
        start(by1)
    sm_got(CORE)
    sm_go(YY)
    rD.got(XX)
    rD.go(YY)
    rU.got(YY)
    rU.go(Z0)

    dq = act

    def pair(y, feat):
        y = y * cs[...]
        fc = feat.astype(f32)
        fc = jnp.where(low_half, fc, pltpu.roll(fc, 64, 1))
        return jnp.where(fc > 0.0, y + pltpu.roll(y, 64, 1), 0.0).astype(bf16)

    def bwd_q(tt, _):
        for j in range(3):
            h = tt * 3 + j
            gn = nl[h].astype(bf16)
            dw = dot_nt(gn, vx[h]).astype(bf16) * mk[...]
            pri = [dot(gn[i * 128:(i + 1) * 128, :], chunk_state(h, leaf_parent(i))) for i in range(4)]
            gq = pair(dot(dw, kf[h]) + jnp.concatenate(pri, axis=0), qf[h])
            if j == 0:
                dq[tt, :, 0:64] = gq[:, 0:64]
            elif j == 1:
                dq[tt, :, 64:128] = gq[:, 64:128]
            else:
                dq[tt, :, 384:448] = gq[:, 0:64]
        return 0

    lax.fori_loop(0, 2, bwd_q, 0)

    @pl.when(c == 0)
    def _():
        wait_recv(by0)
        for cp in by0:
            cp.wait_send()

    @pl.when(c == 1)
    def _():
        for cp in by1:
            cp.wait()

        def addup2(h, _):
            TTb[h] = (dE[2, h].astype(f32) + RR[3, h].astype(f32)).astype(bf16)
            return 0

        lax.fori_loop(0, 12, addup2, 0)
        start(bx)

    sm_got(YY)
    sm_go(XX)
    rD.got(YY)
    rD.go(Z0)
    rU.got(Z0)
    rU.go(Z1)
    lax.fori_loop(2, 4, bwd_q, 0)

    @pl.when(c == 0)
    def _():
        wait_recv(bx)

    @pl.when(c == 1)
    def _():
        for cp in bx:
            cp.wait_send()

    sm_got(XX)
    sm_go(Z0)
    rD.got(Z0)
    rD.go(Z1)
    rU.got(Z1)
    rU.go(XX)

    def later_states(h):
        zero = jnp.zeros((ST, 128), f32)
        d = (jnp.where(t1 > t, RR[2, h].astype(f32), zero) + jnp.where(t2 > t, RR[3, h].astype(f32), zero)
             + jnp.where(t3 > t, RR[4, h].astype(f32), zero) + RX[h].astype(f32))
        pad = jnp.zeros((128 - ST, 128), bf16)
        out = []
        for u in range(2):
            b = jnp.where(t < 2, RR[4 + u, h].astype(f32), zero)
            out.append(jnp.concatenate([jnp.where(c == 0, d, b).astype(bf16), pad], axis=0))
        return out

    def bwd_kv(tt, _):
        for j in range(3):
            h = tt * 3 + j
            gn = nl[h].astype(bf16)
            ds = later_states(h)
            wT = dot_nt(kf[h], qf[h]).astype(bf16) * mkT[...]
            dv = dot(wT, gn) + jnp.concatenate(
                [dot_nt(kf[h, u * 256:(u + 1) * 256, :], ds[u]) for u in range(2)], axis=0)
            dwT = dot_nt(vx[h], gn).astype(bf16) * mkT[...]
            dk = dot(dwT, qf[h]) + jnp.concatenate(
                [dot(vx[h, u * 256:(u + 1) * 256, :], ds[u]) for u in range(2)], axis=0)
            gk = pair(dk, kf[h])
            if j == 0:
                dq[tt, :, 128:192] = gk[:, 0:64]
                dq[tt, :, 256:320] = dv[:, 0:64].astype(bf16)
            elif j == 1:
                dq[tt, :, 192:256] = gk[:, 64:128]
                dq[tt, :, 320:384] = pltpu.roll(dv, 64, 1)[:, 64:128].astype(bf16)
            else:
                dq[tt, :, 448:512] = gk[:, 64:128]
                dq[tt, :, 512:640] = jnp.where(low_half, dv, 0.0).astype(bf16)
        return 0

    lax.fori_loop(0, 2, bwd_kv, 0)
    sm_got(Z0)
    sm_go(Z1)
    rD.got(Z1)
    rU.got(XX)
    lax.fori_loop(2, 4, bwd_kv, 0)
    sm_got(Z1)

    for r in (rD, rU):
        r.core[1].wait_send()
        done(r.core[1])
    for k in (2, 3, 0, 1):
        tk = tks[k]
        dst = rA.stg[k - 2] if k >= 2 else K.at[0, k]

        def put(l0, n, v):
            dst[:, :, :, l0:l0 + n] = v.reshape(4, 2, 96, n).astype(bf16)

        put(0, 256, dot(xT[...], dq[tk, :, 0:256]))
        put(256, 256, dot(xT[...], dq[tk, :, 256:512]))
        put(512, 128, dot(xT[...], dq[tk, :, 512:640]) + dot(gT[...], att[tk, :, 0:128]))
        put(640, 128, dot(gT[...], att[tk, :, 128:256]))
        if k >= 2:
            rA.send_core(k - 2)
        else:
            rA.add_core(k)
    rA.go(XX)

    def inback(tt, _):
        acc[...] += dot_nt(dq[tt, :, 0:640], Gv(0, tt, 0, 640))
        return 0

    lax.fori_loop(0, 4, inback, 0)
    igb[...] = acc[...].astype(bf16)
    ig_l = lcopy(igb, ig_hbm.at[rows_of(t)])
    ig_l.start()
    ig_y = send([rcopy(igb, ig_hbm.at[rows_of(t)], YY)])
    ig_c = send([rcopy(igb, ig_hbm.at[rows_of(t)], CORE)])
    ig_c2 = [rcopy(ig_hbm.at[rows_of(t2)], ig_hbm.at[rows_of(t2)], CORE)]
    rA.got(XX)
    rA.go(Z0)
    rD.finish()
    rA.got(Z0)
    rA.go(Z1)
    rA.got(Z1)
    rA.go(YY)
    wait_recv(ig_y)
    send(ig_c2)
    rA.got(YY)
    rA.finish()
    rU.finish()
    outs = [lcopy(K.at[1, 0, f], gout.at[1])]
    for m, other in ((2, RBD.at[15]), (0, G.at[1, 3, 1, 0])):
        outs += [lcopy(K.at[m, 0, f, c], gout.at[m, c]), lcopy(other, gout.at[m, c1])]
    start(outs)
    small[...] = sm[...]
    wait_recv(lo_c + lo_c2 + ig_c + ig_c2)
    for cp in pending:
        cp.wait_send()
    for cp in outs + [lo_l, ig_l]:
        cp.wait()
    assert counter[0] <= N_REMOTE and lcounter[0] <= N_LOCAL, (counter, lcounter)


N_REMOTE, N_LOCAL = 128, 16


def fast_shards(layer_input, teacher, query_weight, key_weight, value_weight, out_weight, up_weight,
                down_weight, first_gain, first_shift, second_gain, second_shift, parents, valid_count):
    f = lax.axis_index(FSDP)
    D = layer_input.shape[-1]
    sc = layer_input.shape[1]
    tree_len = sc * lax.axis_size(CONTEXT)
    bf16, f32 = jnp.bfloat16, jnp.float32
    oT = out_weight.T
    pack = jnp.concatenate(
        [query_weight[:, :128], key_weight[:, :128], value_weight[:, :128], query_weight[:, 128:],
         key_weight[:, 128:], value_weight[:, 128:], oT[:, 128:], oT[:, :128]], axis=1)
    w = jnp.stack([pack, up_weight, down_weight.T]).reshape(3, 2, 96, D)
    vec = jnp.stack([first_gain, first_shift, second_gain, second_shift])
    norms = lax.dynamic_update_slice(jnp.zeros((16, D), bf16), vec, (0, f * vec.shape[1]))
    V = pltpu.VMEM
    scratch = [
        V((3, 4, 4, 2, 96, D), bf16),
        V((4, 16, D), bf16),
        V((ROWS, D), bf16),
        V((12, ROWS, 128), bf16),
        V((12, ROWS, 128), bf16),
        V((12, ROWS, 128), bf16),
        V((ROWS, ROWS), bf16),
        V((ROWS, ROWS), bf16),
        V((ROWS, 128), f32),
        V((12, ROWS, 128), f32),
        V((4, ROWS, 256), bf16),
        V((ROWS, D), f32),
        V((ROWS, 128), f32),
        V((ROWS, D), bf16),
        V((4, ROWS, D), bf16),
        V((4, ROWS, D), bf16),
        V((ROWS, D), f32),
        V((ROWS, D), bf16),
        V((D, ROWS), bf16),
        V((D, ROWS), bf16),
        V((D, ROWS), bf16),
        V((6, 12, ST, 128), bf16),
        V((12, ST, 128), bf16),
        V((12, ST, 128), bf16),
        V((6, 12, ST, 128), bf16),
        V((5, 12, ST, 128), bf16),
        V((12, ST, 128), bf16),
        V((3, 2, 4, 2, 96, D), bf16),
        V((2, 2, 4, 2, 96, D), bf16),
        V((2, 4, 2, 96, D), bf16),
        V((16, 96, D), bf16),
        V((8, 2, 96, D), bf16),
        V((8, D), f32),
        V((10, 8, D), f32),
        pltpu.SemaphoreType.DMA((N_REMOTE,)),
        pltpu.SemaphoreType.DMA((N_REMOTE,)),
        pltpu.SemaphoreType.DMA((N_LOCAL,)),
    ]
    any_, smem, vmem = (pl.BlockSpec(memory_space=s) for s in (pl.ANY, pltpu.SMEM, pltpu.VMEM))
    lo, ig, gout, small = pl.pallas_call(
        functools.partial(fast_kernel, tree_len=tree_len),
        out_shape=[
            jax.ShapeDtypeStruct((sc, D), bf16),
            jax.ShapeDtypeStruct((sc, D), bf16),
            jax.ShapeDtypeStruct((3, 2, 96, D), bf16),
            jax.ShapeDtypeStruct((8, D), f32),
        ],
        in_specs=[any_, any_, any_, any_, smem, smem],
        out_specs=[any_, any_, any_, vmem],
        scratch_shapes=scratch,
        compiler_params=pltpu.CompilerParams(
            collective_id=0, has_side_effects=True, vmem_limit_bytes=67043328),
        name="tree_layer",
    )(layer_input, teacher, w, norms, parents, valid_count)
    g = gout.reshape(3, 192, D).astype(f32)
    A = g[0]
    q_g = jnp.concatenate([A[:, 0:128], A[:, 384:448]], axis=1)
    k_g = jnp.concatenate([A[:, 128:256], A[:, 448:512]], axis=1)
    v_g = jnp.concatenate([A[:, 256:384], A[:, 512:576]], axis=1)
    o_g = jnp.concatenate([A[:, 640:768], A[:, 576:640]], axis=1).T
    mine = lax.dynamic_slice(small, (0, f * 192), (8, 192))
    return (lo[None], ig.astype(f32)[None], jnp.sum(small[2]), q_g, k_g, v_g, o_g, g[1], g[2].T,
            mine[3], mine[4], mine[0], mine[1])


def shards(*arrays):
    tree_count, slot_count, width = arrays[0].shape
    sizes = tuple(lax.axis_size(n) for n in (FSDP, CONTEXT, TENSOR))
    if (tree_count, slot_count, width) == (1, 2048, 768) and sizes == (4, 2, 4) and arrays[6].shape == (192, 768):
        return fast_shards(*arrays)
    return general_shards(*arrays)


def solution(mesh):
    return jax.shard_map(
        shards,
        mesh=mesh,
        in_specs=(
            P(FSDP, CONTEXT, None),
            P(FSDP, CONTEXT, None),
            P(FSDP, TENSOR),
            P(FSDP, TENSOR),
            P(FSDP, TENSOR),
            P(TENSOR, FSDP),
            P(FSDP, TENSOR),
            P(TENSOR, FSDP),
            P(FSDP),
            P(FSDP),
            P(FSDP),
            P(FSDP),
            P(FSDP, None),
            P(FSDP),
        ),
        out_specs=(
            P(FSDP, CONTEXT, None),
            P(FSDP, CONTEXT, None),
            P(),
            P(FSDP, TENSOR),
            P(FSDP, TENSOR),
            P(FSDP, TENSOR),
            P(TENSOR, FSDP),
            P(FSDP, TENSOR),
            P(TENSOR, FSDP),
            P(FSDP),
            P(FSDP),
            P(FSDP),
            P(FSDP),
        ),
        check_vma=False,
    )
```

```python
import functools
import math

import jax
import jax.numpy as jnp
from jax import lax
from jax.experimental import pallas as pl
from jax.experimental.pallas import tpu as pltpu
from jax.sharding import PartitionSpec as P

HEAD_DIM = 64


precise = lax.Precision.HIGHEST
norm_eps = 1e-05


def carried_in(array, axis, combine, identity):
    count, here = (lax.axis_size(axis), lax.axis_index(axis))
    everything = jax.tree.map(
        lambda part, kind: lax.all_gather(part.astype(kind), axis),
        array,
        (jnp.bfloat16, jnp.bfloat16),
    )
    start = jax.tree.map(
        lambda part, zero: jnp.broadcast_to(jnp.asarray(zero, part.dtype), part.shape),
        array,
        identity,
    )

    def carried_turn(k, before):
        reached = k < here
        new = combine(
            before, jax.tree.map(lambda part, own: part[k].astype(own.dtype), everything, array)
        )
        return jax.tree.map(lambda a, b: jnp.where(reached, a, b), new, before)

    return lax.fori_loop(0, count, carried_turn, start)


def entering(array, axis, combine, identity):
    count, here = (lax.axis_size(axis), lax.axis_index(axis))
    everything = jax.tree.map(
        lambda part, kind: lax.all_gather(part.astype(kind), axis),
        array,
        jax.tree.map(lambda a: jnp.bfloat16 if a.dtype == jnp.float32 else a.dtype, array),
    )
    start = jax.tree.map(
        lambda part, zero: jnp.broadcast_to(jnp.asarray(zero, part.dtype), part.shape),
        array,
        identity,
    )

    def entering_turn(k, before):
        at = count - 1 - k
        reached = at > here
        new = combine(
            before, jax.tree.map(lambda part, own: part[at].astype(own.dtype), everything, array)
        )
        return jax.tree.map(lambda a, b: jnp.where(reached, a, b), new, before)

    return lax.fori_loop(0, count, entering_turn, start)


def layout_of(slot_ids, parents_row, tree_len):
    half_len = tree_len // 2
    branch_len = tree_len // 16
    leaf_len = tree_len // 32
    leaf_start = half_len + 4 * branch_len
    in_branch = (slot_ids >= half_len) & (slot_ids < leaf_start)
    in_leaf = slot_ids >= leaf_start
    branch_index = jnp.clip((slot_ids - half_len) // branch_len, 0, 3)
    leaf_index = jnp.clip((slot_ids - leaf_start) // leaf_len, 0, 7)
    leaf_ids = jnp.arange(8, dtype=jnp.int32)
    leaf_parent = jnp.sum(
        jnp.where(leaf_index[:, None] == leaf_ids[None, :], parents_row[None, :], 0), axis=1
    )
    segment = jnp.where(in_leaf, 5 + leaf_index, jnp.where(in_branch, 1 + branch_index, 0))
    owner_branch = jnp.where(in_leaf, leaf_parent, jnp.where(in_branch, 1 + branch_index, 0))
    leaf_pos = (
        half_len
        + jnp.where(leaf_parent > 0, branch_len, 0)
        + slot_ids
        - leaf_start
        - leaf_index * leaf_len
    )
    branch_pos = slot_ids - branch_index * branch_len
    position = jnp.where(in_leaf, leaf_pos, jnp.where(in_branch, branch_pos, slot_ids))
    phase_angle = (
        0.5 * math.pi * position.astype(jnp.float32) / float(half_len + branch_len + leaf_len)
    )
    return (segment, owner_branch, phase_angle)


def features(pre_act, phase_angle):
    rectified = jnp.maximum(pre_act, 0.0)
    cosine = jnp.cos(phase_angle)[..., None, None]
    sine_part = jnp.sin(phase_angle)[..., None, None]
    return jnp.concatenate([rectified * cosine, rectified * sine_part], axis=-1)


def features_back(grad_feat, pre_act, phase_angle):
    half_dim = pre_act.shape[-1]
    cosine = jnp.cos(phase_angle)[..., None, None]
    sine_part = jnp.sin(phase_angle)[..., None, None]
    combined = grad_feat[..., :half_dim] * cosine + grad_feat[..., half_dim:] * sine_part
    return jnp.where(pre_act > 0.0, combined, 0.0)


def norm_forward(resid, gain_vec, shift_vec):
    row_mean = jnp.mean(resid, axis=-1, keepdims=True)
    centered = resid - row_mean
    inv_std = lax.rsqrt(jnp.mean(centered * centered, axis=-1, keepdims=True) + norm_eps)
    normal = centered * inv_std
    return (normal * gain_vec + shift_vec, normal, inv_std)


def norm_backward(grad_out, normal, inv_std, gain_vec):
    scaled = grad_out * gain_vec
    grad_in = inv_std * (
        scaled
        - jnp.mean(scaled, axis=-1, keepdims=True)
        - normal * jnp.mean(scaled * normal, axis=-1, keepdims=True)
    )
    return (grad_in, jnp.sum(grad_out * normal, axis=0), jnp.sum(grad_out, axis=0))


def add_pair(earlier, later):
    return (earlier[0] + later[0], earlier[1] + later[1])


def general_shards(
    layer_input,
    teacher,
    query_weight,
    key_weight,
    value_weight,
    out_weight,
    up_weight,
    down_weight,
    first_gain,
    first_shift,
    second_gain,
    second_shift,
    parents,
    valid_count,
):
    tree_count, slot_count, model_width = layer_input.shape
    ctx_size = lax.axis_size(CONTEXT)
    ctx_index = lax.axis_index(CONTEXT)
    tree_len = slot_count * ctx_size
    row_count = tree_count * slot_count
    (
        full_query,
        full_key,
        full_value,
        full_out,
        full_up,
        full_down,
        gain_one,
        shift_one,
        gain_two,
        shift_two,
    ) = (
        lax.all_gather(query_weight, FSDP, axis=0, tiled=True),
        lax.all_gather(key_weight, FSDP, axis=0, tiled=True),
        lax.all_gather(value_weight, FSDP, axis=0, tiled=True),
        lax.all_gather(out_weight, FSDP, axis=1, tiled=True),
        lax.all_gather(up_weight, FSDP, axis=0, tiled=True),
        lax.all_gather(down_weight, FSDP, axis=1, tiled=True),
        lax.all_gather(first_gain, FSDP, axis=0, tiled=True),
        lax.all_gather(first_shift, FSDP, axis=0, tiled=True),
        lax.all_gather(second_gain, FSDP, axis=0, tiled=True),
        lax.all_gather(second_shift, FSDP, axis=0, tiled=True),
    )
    gain_one = gain_one.astype(jnp.float32)
    shift_one = shift_one.astype(jnp.float32)
    gain_two = gain_two.astype(jnp.float32)
    shift_two = shift_two.astype(jnp.float32)
    head_local = full_query.shape[1] // HEAD_DIM
    flat_in = layer_input.reshape(row_count, model_width)
    slot_ids = ctx_index * slot_count + jnp.arange(slot_count, dtype=jnp.int32)

    def layout_here(parents_row):
        return layout_of(slot_ids, parents_row, tree_len)

    segment, owner_branch, phase_angle = jax.vmap(layout_here)(parents)

    def project(weight):
        return jnp.dot(flat_in, weight, preferred_element_type=jnp.float32).reshape(
            tree_count, slot_count, head_local, HEAD_DIM
        )

    query_pre = project(full_query)
    key_pre = project(full_key)
    values = project(full_value).astype(jnp.bfloat16)
    query_feat = features(query_pre, phase_angle).astype(jnp.bfloat16)
    key_feat = features(key_pre, phase_angle).astype(jnp.bfloat16)
    query_wide = query_feat.astype(jnp.float32)
    key_wide = key_feat.astype(jnp.float32)
    value_wide = values.astype(jnp.float32)
    state_ids = jnp.arange(5, dtype=jnp.int32)
    segment_hit = segment[:, :, None] == state_ids
    in_segment = segment_hit.astype(jnp.float32)
    selected = ((state_ids == 0) | (owner_branch[:, :, None] == state_ids)).astype(jnp.float32)
    masked_key = jnp.where(
        segment_hit[:, :, :, None, None], key_feat[:, :, None], jnp.zeros((), jnp.bfloat16)
    )
    contrib_state = jnp.einsum(
        "tsahf,tshd->tahfd", masked_key, values, preferred_element_type=jnp.float32
    )
    contrib_norm = jnp.einsum(
        "tsa,tshf->tahf",
        segment_hit.astype(jnp.bfloat16),
        key_feat,
        preferred_element_type=jnp.float32,
    )
    zero_state = jnp.zeros_like(contrib_state)
    zero_norm = jnp.zeros_like(contrib_norm)
    prior_state, prior_norm = carried_in(
        (contrib_state, contrib_norm), CONTEXT, add_pair, (zero_state, zero_norm)
    )
    in_numer = jnp.einsum(
        "tsa,tshf,tahfd->tshd", selected, query_wide, prior_state, precision=precise
    )
    in_denom = jnp.einsum("tsa,tshf,tahf->tsh", selected, query_wide, prior_norm, precision=precise)
    block_rows = min(slot_count, 512)
    block_count = slot_count // block_rows

    def block_scores(block_index):
        row_start = block_index * block_rows
        query_rows = lax.dynamic_slice_in_dim(query_feat, row_start, block_rows, 1)
        slot_rows = lax.dynamic_slice_in_dim(slot_ids, row_start, block_rows, 0)
        segment_rows = lax.dynamic_slice_in_dim(segment, row_start, block_rows, 1)
        owner_rows = lax.dynamic_slice_in_dim(owner_branch, row_start, block_rows, 1)
        allowed = (slot_ids[None, None, :] <= slot_rows[None, :, None]) & (
            (segment[:, None, :] == segment_rows[:, :, None])
            | (segment[:, None, :] == 0)
            | (segment[:, None, :] == owner_rows[:, :, None])
        )
        allowed_wide = allowed[:, None].astype(jnp.float32)
        scores = (
            jnp.einsum("tihf,tjhf->thij", query_rows, key_feat, preferred_element_type=jnp.float32)
            * allowed_wide
        )
        return (scores, allowed_wide, query_rows)

    def local_forward(block_index):
        scores, allowed_wide, query_rows = block_scores(block_index)
        numerator = jnp.einsum("thij,tjhd->tihd", scores, value_wide, precision=precise)
        denominator = jnp.transpose(jnp.sum(scores, axis=3), (0, 2, 1))
        return (numerator, denominator)

    local_numer, local_denom = lax.map(local_forward, jnp.arange(block_count, dtype=jnp.int32))

    def unblock(stacked):
        return jnp.moveaxis(stacked, 0, 1).reshape((tree_count, slot_count) + stacked.shape[3:])

    numerator = unblock(local_numer) + in_numer
    denominator = unblock(local_denom) + in_denom
    safe_denom = jnp.maximum(denominator, 1.0)
    attended = numerator / safe_denom[..., None]
    attended_low = attended.astype(jnp.bfloat16).reshape(row_count, head_local * HEAD_DIM)
    attention_part = jnp.dot(attended_low, full_out, preferred_element_type=jnp.float32)
    attention_sum = lax.psum(attention_part.astype(jnp.bfloat16), TENSOR).astype(jnp.float32)
    resid_one = flat_in.astype(jnp.float32) + attention_sum
    normed_one, normal_one, inv_one = norm_forward(resid_one, gain_one, shift_one)
    normed_low = normed_one.astype(jnp.bfloat16)
    hidden_pre = jnp.dot(normed_low, full_up, preferred_element_type=jnp.float32)
    activated = jax.nn.gelu(hidden_pre, approximate=False).astype(jnp.bfloat16)
    ffn_part = jnp.dot(activated, full_down, preferred_element_type=jnp.float32)
    ffn_sum = lax.psum(ffn_part.astype(jnp.bfloat16), TENSOR).astype(jnp.float32)
    resid_two = normed_one + ffn_sum
    result, normal_two, inv_two = norm_forward(resid_two, gain_two, shift_two)
    layer_output = result.astype(jnp.bfloat16).reshape(tree_count, slot_count, model_width)
    valid_rows = (
        (slot_ids[None, :] < valid_count[:, None]).astype(jnp.float32).reshape(row_count, 1)
    )
    residual = (result - teacher.reshape(row_count, model_width).astype(jnp.float32)) * valid_rows
    loss_value = lax.psum(0.5 * jnp.sum(residual * residual), (FSDP, CONTEXT))
    grad_resid_two, second_gain_part, second_shift_part = norm_backward(
        residual, normal_two, inv_two, gain_two
    )
    grad_two_low = grad_resid_two.astype(jnp.bfloat16)
    down_part = jnp.dot(activated.T, grad_two_low, preferred_element_type=jnp.float32)
    grad_act = jnp.dot(grad_two_low, full_down.T, preferred_element_type=jnp.float32)
    cumulative = 0.5 * (1.0 + jax.scipy.special.erf(hidden_pre / math.sqrt(2.0)))
    density = jnp.exp(-0.5 * hidden_pre * hidden_pre) / math.sqrt(2.0 * math.pi)
    grad_pre = (grad_act * (cumulative + hidden_pre * density)).astype(jnp.bfloat16)
    up_part = jnp.dot(normed_low.T, grad_pre, preferred_element_type=jnp.float32)
    ffn_back = jnp.dot(grad_pre, full_up.T, preferred_element_type=jnp.float32)
    grad_normed_one = grad_resid_two + lax.psum(ffn_back.astype(jnp.bfloat16), TENSOR).astype(
        jnp.float32
    )
    grad_resid_one, first_gain_part, first_shift_part = norm_backward(
        grad_normed_one, normal_one, inv_one, gain_one
    )
    grad_one_low = grad_resid_one.astype(jnp.bfloat16)
    out_part = jnp.dot(attended_low.T, grad_one_low, preferred_element_type=jnp.float32)
    grad_attended = jnp.dot(grad_one_low, full_out.T, preferred_element_type=jnp.float32).astype(
        jnp.bfloat16
    )
    grad_attended = grad_attended.astype(jnp.float32).reshape(
        tree_count, slot_count, head_local, HEAD_DIM
    )
    grad_numer = grad_attended / safe_denom[..., None]
    grad_denom = jnp.where(
        denominator > 1.0, -jnp.sum(grad_attended * attended, axis=-1) / safe_denom, 0.0
    )
    grad_query = jnp.einsum(
        "tsa,tshd,tahfd->tshf", selected, grad_numer, prior_state, precision=precise
    ) + jnp.einsum("tsa,tsh,tahf->tshf", selected, grad_denom, prior_norm, precision=precise)
    grad_prior_state = jnp.einsum(
        "tsa,tshf,tshd->tahfd", selected, query_wide, grad_numer, precision=precise
    )
    grad_prior_norm = jnp.einsum(
        "tsa,tshf,tsh->tahf", selected, query_wide, grad_denom, precision=precise
    )
    grad_contrib_state, grad_contrib_norm = entering(
        (grad_prior_state, grad_prior_norm), CONTEXT, add_pair, (zero_state, zero_norm)
    )
    grad_key = jnp.einsum(
        "tsa,tshd,tahfd->tshf", in_segment, value_wide, grad_contrib_state, precision=precise
    ) + jnp.einsum("tsa,tahf->tshf", in_segment, grad_contrib_norm, precision=precise)
    grad_value = jnp.einsum(
        "tsa,tshf,tahfd->tshd", in_segment, key_wide, grad_contrib_state, precision=precise
    )

    def local_backward(carried, block_index):
        acc_key, acc_value = carried
        scores, allowed_wide, query_rows = block_scores(block_index)
        row_start = block_index * block_rows
        numer_rows = lax.dynamic_slice_in_dim(grad_numer, row_start, block_rows, 1)
        denom_rows = lax.dynamic_slice_in_dim(grad_denom, row_start, block_rows, 1)
        grad_scores = (
            jnp.einsum("tihd,tjhd->thij", numer_rows, value_wide, precision=precise)
            + jnp.transpose(denom_rows, (0, 2, 1))[:, :, :, None]
        ) * allowed_wide
        rows_grad = jnp.einsum("thij,tjhf->tihf", grad_scores, key_wide, precision=precise)
        acc_key = acc_key + jnp.einsum(
            "thij,tihf->tjhf", grad_scores, query_rows.astype(jnp.float32), precision=precise
        )
        acc_value = acc_value + jnp.einsum("thij,tihd->tjhd", scores, numer_rows, precision=precise)
        return ((acc_key, acc_value), rows_grad)

    (local_key, local_value), local_query = lax.scan(
        local_backward,
        (jnp.zeros_like(key_wide), jnp.zeros_like(value_wide)),
        jnp.arange(block_count, dtype=jnp.int32),
    )
    grad_query = grad_query + unblock(local_query)
    grad_key = grad_key + local_key
    grad_value = grad_value + local_value
    grad_query_low = (
        features_back(grad_query, query_pre, phase_angle)
        .astype(jnp.bfloat16)
        .reshape(row_count, -1)
    )
    grad_key_low = (
        features_back(grad_key, key_pre, phase_angle).astype(jnp.bfloat16).reshape(row_count, -1)
    )
    grad_value_low = grad_value.astype(jnp.bfloat16).reshape(row_count, -1)
    query_part = jnp.dot(flat_in.T, grad_query_low, preferred_element_type=jnp.float32)
    key_part = jnp.dot(flat_in.T, grad_key_low, preferred_element_type=jnp.float32)
    value_part = jnp.dot(flat_in.T, grad_value_low, preferred_element_type=jnp.float32)
    input_back = (
        jnp.dot(grad_query_low, full_query.T, preferred_element_type=jnp.float32)
        + jnp.dot(grad_key_low, full_key.T, preferred_element_type=jnp.float32)
        + jnp.dot(grad_value_low, full_value.T, preferred_element_type=jnp.float32)
    )
    input_grad = (
        grad_resid_one + lax.psum(input_back.astype(jnp.bfloat16), TENSOR).astype(jnp.float32)
    ).reshape(tree_count, slot_count, model_width)
    grad_parts = (
        query_part,
        key_part,
        value_part,
        out_part,
        up_part,
        down_part,
        first_gain_part,
        first_shift_part,
        second_gain_part,
        second_shift_part,
    )
    summed = (
        lax.psum(grad_parts[0].astype(jnp.bfloat16), CONTEXT).astype(jnp.float32),
        lax.psum(grad_parts[1].astype(jnp.bfloat16), CONTEXT).astype(jnp.float32),
        lax.psum(grad_parts[2].astype(jnp.bfloat16), CONTEXT).astype(jnp.float32),
        lax.psum(grad_parts[3].astype(jnp.bfloat16), CONTEXT).astype(jnp.float32),
        lax.psum(grad_parts[4].astype(jnp.bfloat16), CONTEXT).astype(jnp.float32),
        lax.psum(grad_parts[5].astype(jnp.bfloat16), CONTEXT).astype(jnp.float32),
        lax.psum(grad_parts[6].astype(jnp.bfloat16), CONTEXT).astype(jnp.float32),
        lax.psum(grad_parts[7].astype(jnp.bfloat16), CONTEXT).astype(jnp.float32),
        lax.psum(grad_parts[8].astype(jnp.bfloat16), CONTEXT).astype(jnp.float32),
        lax.psum(grad_parts[9].astype(jnp.bfloat16), CONTEXT).astype(jnp.float32),
    )
    reduced = (
        lax.psum_scatter(
            summed[0].astype(jnp.bfloat16), FSDP, scatter_dimension=0, tiled=True
        ).astype(jnp.float32),
        lax.psum_scatter(
            summed[1].astype(jnp.bfloat16), FSDP, scatter_dimension=0, tiled=True
        ).astype(jnp.float32),
        lax.psum_scatter(
            summed[2].astype(jnp.bfloat16), FSDP, scatter_dimension=0, tiled=True
        ).astype(jnp.float32),
        lax.psum_scatter(
            summed[3].astype(jnp.bfloat16), FSDP, scatter_dimension=1, tiled=True
        ).astype(jnp.float32),
        lax.psum_scatter(
            summed[4].astype(jnp.bfloat16), FSDP, scatter_dimension=0, tiled=True
        ).astype(jnp.float32),
        lax.psum_scatter(
            summed[5].astype(jnp.bfloat16), FSDP, scatter_dimension=1, tiled=True
        ).astype(jnp.float32),
        lax.psum_scatter(
            summed[6].astype(jnp.bfloat16), FSDP, scatter_dimension=0, tiled=True
        ).astype(jnp.float32),
        lax.psum_scatter(
            summed[7].astype(jnp.bfloat16), FSDP, scatter_dimension=0, tiled=True
        ).astype(jnp.float32),
        lax.psum_scatter(
            summed[8].astype(jnp.bfloat16), FSDP, scatter_dimension=0, tiled=True
        ).astype(jnp.float32),
        lax.psum_scatter(
            summed[9].astype(jnp.bfloat16), FSDP, scatter_dimension=0, tiled=True
        ).astype(jnp.float32),
    )
    return (
        layer_output,
        input_grad,
        loss_value,
        reduced[0],
        reduced[1],
        reduced[2],
        reduced[3],
        reduced[4],
        reduced[5],
        reduced[6],
        reduced[7],
        reduced[8],
        reduced[9],
    )


MESH_ID = pl.DeviceIdType.MESH
ROWS = 512
CORE, YY, XX, Z0, Z1, FIN = range(6)
FSDP, CONTEXT, TENSOR = "fsdp", "context", "tensor"
ST = 80


GATHER_ATTENTION = (
    (Z1, XX, Z0, YY),
    (Z0, YY, Z1, XX),
    (Z1, Z0, YY, XX),
    (Z1, Z0, XX, YY),
    (Z1, YY, XX, Z0),
    (Z0, YY, Z1, XX),
)
GATHER_UP = (
    (Z1, YY, XX, Z0),
    (Z0, YY, XX, Z1),
    (Z1, YY, Z0, XX),
)
GATHER_DOWN = (
    (Z0, Z1, XX, YY),
    (Z0, Z1, YY, XX),
    (YY, Z1, XX, Z0),
)
REDUCE_DOWN = (
    (Z0, XX, YY, Z1),
    (XX, Z0, YY, Z1),
    (Z0, XX, YY, Z1),
)
REDUCE_UP = (
    (XX, Z0, YY, Z1),
    (YY, Z0, Z1, XX),
    (Z0, XX, YY, Z1),
)
REDUCE_ATTENTION = (
    (XX, Z0, Z1, YY),
    (Z0, Z1, XX, YY),
    (XX, Z0, Z1, YY),
    (YY, Z0, XX, Z1),
    (Z0, XX, Z1, YY),
    (XX, Z0, YY, Z1),
)
GATE_U, GATE_D = 10.0, 16.0
HOLD_FORWARD, HOLD_BACKWARD, OUTPUT_STEP = False, 0, 0
UNIT_US, HOP_US, CORE_US = 3.28, 1.7, 0.3


class Plan:
    def __init__(self):
        self.now, self.free, self.flying = 0.0, {}, []
        self.holding, self.held = False, []

    def begin(self, piece):
        piece.at_stage = -1
        self.advance(piece)

    def load(self, stage, units):
        ends = []
        for link, us in self.cost(stage, units):
            ends.append(max(self.now, self.free.get(link, 0.0)) + us)
            self.free[link] = ends[-1]
        return max(ends) + HOP_US

    @staticmethod
    def cost(stage, units):
        if stage == CORE:
            return ((CORE, units * CORE_US),)
        us = units * UNIT_US
        if stage == Z1:
            return ((Z0, us), (Z1, 2 * us))
        return ((stage, us),)

    def advance(self, piece):
        piece.at_stage += 1
        if piece.at_stage < len(piece.order):
            stage = piece.order[piece.at_stage]
            if self.holding and stage in (XX, YY):
                self.held.append(piece)
                return
            piece.go(stage)
            self.flying.append((self.load(stage, piece.units[stage]), len(self.flying), piece))

    def take(self, until):
        if not self.flying:
            assert until < math.inf
            return False
        first = min(self.flying, key=lambda e: e[0])
        if first[0] > until:
            return False
        self.flying.remove(first)
        self.now = max(self.now, first[0])
        piece = first[2]
        piece.got(piece.order[piece.at_stage])
        self.advance(piece)
        return True

    def tick(self, us):
        self.now += us
        while self.take(self.now - 0.5):
            pass

    def hold(self):
        self.holding = True

    def release(self):
        self.holding = False
        held, self.held = self.held, []
        for piece in held:
            piece.at_stage -= 1
            self.advance(piece)

    def gate(self, until):
        while self.take(until):
            pass
        self.now = max(self.now, until)

    def need(self, pieces, stage=None):
        def short(p):
            done = p.at_stage
            return done < (len(p.order) if stage is None else p.order.index(stage) + 1)

        while any(short(p) for p in pieces):
            self.take(math.inf)


def fast_kernel(*refs, tree_len):
    (x_hbm, t_hbm, q_in, k_in, v_in, o_in, u_in, d_in, n_in, par, val,
     lo_hbm, ig_hbm, gout, small,
     G, NG, xv, qf, kf, vx, mk, mkT, cs, nl, att, n1, inv1, nlow, act, der, acc, glow, gT, nT,
     SR, PS, TTb, RR, dE, RX, W4, RC, RB, sm, smr, ss, rs, ls) = refs
    f = lax.axis_index(FSDP)
    c = lax.axis_index(CONTEXT)
    t = lax.axis_index(TENSOR)
    t1 = t + 1 - 2 * lax.rem(t, 2)
    t2 = lax.rem(t + 2, 4)
    t3 = lax.rem(t1 + 2, 4)
    f1 = f + 1 - 2 * lax.rem(f, 2)
    f2 = lax.rem(f + 2, 4)
    f3 = lax.rem(f1 + 2, 4)
    c1 = 1 - c
    tks = [t, t2, t1, t3]
    DEV = {CORE: {TENSOR: t1}, YY: {TENSOR: t2}, XX: {CONTEXT: c1}, Z0: {FSDP: f1}, Z1: {FSDP: f2}}
    D = 768
    counter = [0]

    def rcopy(src, dst, dev):
        i = counter[0]
        counter[0] += 1
        return pltpu.make_async_remote_copy(
            src_ref=src, dst_ref=dst, send_sem=ss.at[i], recv_sem=rs.at[i],
            device_id=DEV[dev], device_id_type=MESH_ID)

    lcounter = [0]

    def lcopy(src, dst):
        i = lcounter[0]
        lcounter[0] += 1
        return pltpu.make_async_copy(src, dst, ls.at[i])

    def start(cps):
        for cp in cps:
            cp.start()

    def wait_recv(cps):
        for cp in cps:
            cp.wait_recv()

    pending = []

    def send(cps):
        start(cps)
        pending.extend(cps)
        return cps

    def done(cp):
        pending[:] = [other for other in pending if other is not cp]

    f32, bf16 = jnp.float32, jnp.bfloat16

    def dot(a, b):
        return lax.dot_general(a, b, (((1,), (0,)), ((), ())), preferred_element_type=f32)

    def dot_nt(a, b):
        return lax.dot_general(a, b, (((1,), (1,)), ((), ())), preferred_element_type=f32)

    class Small:
        def __init__(self, stages, units, after=None):
            self.order = tuple(stages)
            self.stages, self.units, self.after = stages, units, after

        def go(self, stage):
            if self.after is not None:
                self.after(stage, False)
            send(self.stages[stage])

        def got(self, stage):
            wait_recv(self.stages[stage])
            if self.after is not None:
                self.after(stage, True)

    bar = pltpu.get_barrier_semaphore()
    for dev in DEV.values():
        pl.semaphore_signal(bar, inc=1, device_id=dev, device_id_type=MESH_ID)

    row0 = pl.multiple_of(t * ROWS, ROWS)
    lx = lcopy(x_hbm.at[0, pl.ds(row0, ROWS), :], xv)
    lt = lcopy(t_hbm.at[0, pl.ds(row0, ROWS), :], xv)
    lx2 = lcopy(x_hbm.at[0, pl.ds(row0, ROWS), :], nlow)
    tv = lob = xv
    igb, xT = nlow, nT
    own = [lcopy(w_in, G.at[m, t, f]) for m, w_in in ((1, u_in), (2, d_in))]
    lng = lcopy(n_in, NG.at[f])
    start([lx] + own + [lng])
    oT = jnp.transpose(o_in[...].astype(jnp.float32)).astype(jnp.bfloat16)
    for h in range(2):
        r = slice(h * 96, h * 96 + 96)
        own_a = G.at[0, t, f, h]
        own_a[:, 0:128] = q_in[r, 0:128]
        own_a[:, 128:256] = k_in[r, 0:128]
        own_a[:, 256:384] = v_in[r, 0:128]
        own_a[:, 384:512] = jnp.concatenate([q_in[r, 128:192], k_in[r, 128:192]], axis=1)
        own_a[:, 512:640] = jnp.concatenate([v_in[r, 128:192], oT[r, 128:192]], axis=1)
        own_a[:, 640:768] = oT[r, 0:128]
    for cp in own + [lng]:
        cp.wait()
    pl.semaphore_wait(bar, 5)

    far, near = {id(f): f2, id(f1): f3}, {id(f): f1, id(f2): f3}
    class Gather:
        def __init__(self, m, l0, n, order, split):
            self.lanes = slice(None) if n == D else pl.ds(l0, n)
            self.m, self.order = m, order
            self.ts, self.fs = [t], [f]
            self.h = c if split else None
            self.stages, self.units, self.share = {}, {}, n / D
            for stage in order:
                self.stages[stage] = self.build(stage)

        def at(self, ti, fi, h):
            hh = slice(None) if h is None else h
            return G.at[self.m, ti, fi, hh, slice(None), self.lanes]

        def build(self, stage):
            regs = []
            fl = [slice(None)] if len(self.fs) == 4 else self.fs
            if stage == XX:
                for ti in self.ts:
                    if ti is t:
                        others = [fi for fi in self.fs if fi is not f]
                        regs += [(ti, fi, c) for fi in others]
                    else:
                        regs += [(ti, fi, c) for fi in fl]
                self.h = None
            else:
                regs = [(ti, fi, self.h) for ti in self.ts for fi in fl]
                if stage == Z1:
                    self.fs = self.fs + [far[id(v)] for v in self.fs]
                if stage == Z0:
                    self.fs = self.fs + [near[id(v)] for v in self.fs]
                if stage == YY:
                    self.ts = self.ts + [t2]
                if stage == CORE:
                    self.ts = self.ts + [t1, t3]
            count = sum((4 if isinstance(fi, slice) else 1) * (2 if h is None else 1) for _, fi, h in regs)
            self.units[stage] = count * self.share
            return [rcopy(self.at(*r), self.at(*r), stage) for r in regs]

        def go(self, stage):
            send(self.stages[stage])

        def got(self, stage):
            wait_recv(self.stages[stage])

    gather_orders = (GATHER_ATTENTION, GATHER_UP, GATHER_DOWN)
    gat = [[Gather(m, j * (D // len(o)), D // len(o), order + (CORE,), True) for j, order in enumerate(o)]
           for m, o in enumerate(gather_orders)]
    norm_vectors = Small(
        {Z1: [rcopy(NG.at[f], NG.at[f], Z1)],
         Z0: [rcopy(NG.at[f], NG.at[f], Z0), rcopy(NG.at[f2], NG.at[f2], Z0)]}, {Z1: 0.03, Z0: 0.06})
    plan = Plan()
    for g in gat[0]:
        plan.begin(g)
    plan.begin(norm_vectors)

    lane = lax.broadcasted_iota(jnp.int32, (ROWS, 128), 1)
    low_half = lane < 64
    half_len, branch_len, leaf_len = tree_len // 2, tree_len // 16, tree_len // 32
    leaf_start = half_len + 4 * branch_len
    base_slot = c * (4 * ROWS) + t * ROWS

    def layout(slot):
        in_leaf = slot >= leaf_start
        in_branch = (slot >= half_len) & jnp.logical_not(in_leaf)
        bi = jnp.clip((slot - half_len) >> (branch_len.bit_length() - 1), 0, 3)
        li = jnp.clip((slot - leaf_start) >> (leaf_len.bit_length() - 1), 0, 7)
        lp = jnp.zeros_like(slot)
        for k in range(8):
            lp = jnp.where(li == k, par[0, k], lp)
        seg = jnp.where(in_leaf, 5 + li, jnp.where(in_branch, 1 + bi, 0))
        own_b = jnp.where(in_leaf, lp, jnp.where(in_branch, 1 + bi, 0))
        leaf_pos = half_len + jnp.where(lp > 0, branch_len, 0) + slot - leaf_start - li * leaf_len
        posn = jnp.where(in_leaf, leaf_pos, jnp.where(in_branch, slot - bi * branch_len, slot))
        return seg, own_b, posn

    slot_col = base_slot + lax.broadcasted_iota(jnp.int32, (ROWS, 128), 0)
    seg_c, own_c, pos_c = layout(slot_col)
    ang = 0.5 * math.pi * pos_c.astype(f32) / float(half_len + branch_len + leaf_len)
    cs[...] = jnp.where(low_half, jnp.cos(ang), jnp.sin(ang))
    slot_row = base_slot + lax.broadcasted_iota(jnp.int32, (8, ROWS), 1)
    seg_r8, own_r8, _ = layout(slot_row)
    seg_r, own_r, sl_r = seg_r8[0:1], own_r8[0:1], slot_row[0:1]
    for j in range(4):
        ls_ = slice(j * 128, j * 128 + 128)
        sr, orr, slr = seg_r[:, ls_], own_r[:, ls_], sl_r[:, ls_]
        ok = (slr <= slot_col) & ((sr == seg_c) | (sr == 0) | (sr == own_c))
        mk[:, ls_] = jnp.where(ok, 1.0, 0.0).astype(bf16)
        okT = (slot_col <= slr) & ((seg_c == sr) | (seg_c == 0) | (seg_c == orr))
        mkT[:, ls_] = jnp.where(okT, 1.0, 0.0).astype(bf16)
    lx.wait()

    plan.tick(4.0)
    plan.gate(GATE_U)
    for g in gat[1]:
        plan.begin(g)
    plan.gate(GATE_D)
    for g in gat[2]:
        plan.begin(g)

    def Gv(m, tk, l0, n):
        return G[m, tk, :, :, :, l0:l0 + n].reshape(D, n)

    def Gd(m, tk, n0, n):
        return G[m, tk, :, :, :, pl.ds(n0, n)].reshape(D, n)

    def qkv(tk):
        csv = cs[...]
        h = tk * 3

        def lo(p):
            return (jnp.where(low_half, p, pltpu.roll(p, 64, 1)) * csv).astype(bf16)

        def hi(p):
            return (jnp.where(low_half, pltpu.roll(p, 64, 1), p) * csv).astype(bf16)

        def vext(p, up):
            p = pltpu.roll(p, 64, 1) if up else p
            return jnp.where(low_half, p, jnp.where(lane == 64, 1.0, 0.0)).astype(bf16)

        a = jnp.maximum(dot(xv[...], Gv(0, tk, 0, 256)), 0.0)
        qf[h] = lo(a[:, :128])
        qf[h + 1] = hi(a[:, :128])
        kf[h] = lo(a[:, 128:])
        kf[h + 1] = hi(a[:, 128:])
        b = dot(xv[...], Gv(0, tk, 256, 256))
        vx[h] = vext(b[:, :128], False)
        vx[h + 1] = vext(b[:, :128], True)
        r = jnp.maximum(b[:, 128:], 0.0)
        qf[h + 2] = lo(r)
        kf[h + 2] = hi(r)
        vx[h + 2] = vext(dot(xv[...], Gv(0, tk, 512, 128)), False)
        for j in range(3):
            vT = jnp.transpose(vx[h + j].astype(f32)).astype(bf16)
            u0 = dot(vT[:ST, :256], kf[h + j, :256])
            u1 = dot(vT[:ST, 256:], kf[h + j, 256:])
            first = jnp.where(c == 0, u0 + u1, u0)
            dE[0, h + j] = first.astype(bf16)
            dE[1, h + j] = u1.astype(bf16)

    for g in gat[0]:
        plan.need([g], g.order[-2])
    qkv(tks[0])
    plan.tick(1.3)
    qkv(tks[1])
    plan.tick(1.3)
    plan.need(gat[0])
    if HOLD_FORWARD:
        plan.hold()
    qkv(tks[2])
    plan.tick(1.3)
    qkv(tks[3])
    plan.tick(1.3)

    core_id = lax.rem(t, 2)
    half = pl.ds(pl.multiple_of(core_id * 6, 6), 6)
    first_chip = t < 2
    fc0 = [rcopy(dE.at[0], SR.at[1], CORE)]
    fy0 = [rcopy(dE.at[1, half], SR.at[0, half], YY)]
    fx0 = [rcopy(TTb.at[half], PS.at[half], XX)]
    fo0 = [rcopy(SR.at[0, half], SR.at[2, half], CORE)]
    fy1 = [rcopy(dE.at[pl.ds(0, 2)], SR.at[pl.ds(0, 2)], YY)]
    fc1 = [rcopy(SR.at[pl.ds(0, 2)], SR.at[pl.ds(2, 2)], CORE)]
    fo1 = [rcopy(PS.at[half], PS.at[half], CORE)]

    def each_half(body):
        def one(i, _):
            body(core_id * 6 + i)
            return 0

        lax.fori_loop(0, 6, one, 0)

    def local_fwd(h, _):
        s = dot_nt(qf[h], kf[h]).astype(bf16) * mk[...]
        nl[h] = dot(s, vx[h])
        return 0

    @pl.when(c == 0)
    def _():
        start(fc0)

    @pl.when((c == 1) & first_chip)
    def _():
        start(fy1)

    units_due = plan.load(YY, 3.4)
    lax.fori_loop(0, 4, local_fwd, 0)
    plan.tick(2.1)

    @pl.when(c == 0)
    def _():
        for cp in fc0:
            cp.wait()

        def chip_sum(h):
            dE[1, h] = (dE[0, h].astype(f32) + SR[1, h].astype(f32)).astype(bf16)

        each_half(chip_sum)
        start(fy0)

    due = plan.load(YY, 0.85)
    lax.fori_loop(4, 9, local_fwd, 0)
    plan.tick(2.7)
    plan.gate(max(due, plan.now))

    @pl.when(c == 0)
    def _():
        for cp in fy0:
            cp.wait()

        def total(h):
            TTb[h] = (dE[1, h].astype(f32) + SR[0, h].astype(f32)).astype(bf16)

        each_half(total)
        start(fx0)
        start(fo0)

    due = plan.load(XX, 0.85) + 1.5
    plan.release()
    lax.fori_loop(9, 12, local_fwd, 0)
    plan.tick(1.6)
    plan.gate(max(units_due + 1.5, due, plan.now))

    @pl.when(c == 0)
    def _():
        for cp in fo0:
            cp.wait()
        for cp in fx0:
            cp.wait_send()

        def before(h, _):
            zero = jnp.zeros((ST, 128), f32)
            mine = h // 6 == core_id
            other = jnp.where(mine, SR[0, h].astype(f32), SR[2, h].astype(f32))
            p = jnp.where(t1 < t, SR[1, h].astype(f32), zero) + jnp.where(t2 < t, other, zero)
            PS[h] = p.astype(bf16)
            return 0

        lax.fori_loop(0, 12, before, 0)

    @pl.when(c == 1)
    def _():
        wait_recv(fx0)
        start(fo1)

    @pl.when((c == 1) & first_chip)
    def _():
        for cp in fy1:
            cp.wait_send()

    @pl.when((c == 1) & jnp.logical_not(first_chip))
    def _():
        wait_recv(fy1)
        start(fc1)
        for cp in fc1:
            cp.wait()

    @pl.when(c == 1)
    def _():
        for cp in fo1:
            cp.wait()

    is_leafdev = (c == 1) & (t >= 2)

    def leaf_parent(i):
        k = 4 * lax.rem(t, 2)
        v = par[0, i]
        w = par[0, 4 + i]
        return jnp.where(is_leafdev, jnp.where(k == 0, v, w), 0)

    low_base = jnp.where(t == 2, 0, 2)
    high_base = jnp.where(t == 2, 2, 0)

    def chunk_state(h, lp):
        s = PS[h].astype(f32)
        zero = jnp.zeros_like(s)
        s = s + jnp.where(lp == 1, SR[low_base, h].astype(f32), zero)
        s = s + jnp.where(lp == 2, SR[low_base + 1, h].astype(f32), zero)
        s = s + jnp.where(lp == 3, SR[high_base, h].astype(f32), zero)
        s = s + jnp.where(lp == 4, SR[high_base + 1, h].astype(f32), zero)
        s = s.astype(bf16)
        return jnp.concatenate([s, jnp.zeros((128 - ST, 128), bf16)], axis=0)

    lane_c = lax.broadcasted_iota(jnp.int32, (128, 128), 1)
    low_c = lane_c < 64
    zs = jnp.zeros((12, ST, 128), bf16)
    zh = jnp.zeros((6, ST, 128), bf16)
    rest = pl.ds(pl.multiple_of(6 - core_id * 6, 6), 6)

    @pl.when(c == 0)
    def _():
        SR[3] = zs
        SR[0, rest] = zh
        SR[2, half] = zh
        RR[5] = zs
        RR[3, rest] = zh
        RR[4, half] = zh
        RX[rest] = zh

    @pl.when(c == 1)
    def _():
        RX[...] = zs
        RR[3] = zs

    @pl.when((c == 1) & first_chip)
    def _():
        for i in range(4):
            SR[i] = zs

    @pl.when((c == 1) & jnp.logical_not(first_chip))
    def _():
        RR[4] = zs
        RR[5] = zs

    def prior_fwd(tt, _):
        for i in range(4):
            lp = leaf_parent(i)
            rows = pl.ds(i * 128, 128)
            outs = []
            for j in range(3):
                h = tt * 3 + j
                tot = nl[h, rows, :] + dot_nt(qf[h, rows, :], chunk_state(h, lp))
                den = jnp.broadcast_to(tot[:, 64:65], (128, 128))
                a = tot / jnp.maximum(den, 1.0)
                nl[h, rows, :] = jnp.where(low_c, a, den)
                outs.append(a)
            att[tt, rows, 0:128] = jnp.where(low_c, 0.0, pltpu.roll(outs[2], 64, 1)).astype(bf16)
            att[tt, rows, 128:256] = jnp.where(low_c, outs[0], pltpu.roll(outs[1], 64, 1)).astype(bf16)
        return 0

    lax.fori_loop(0, 4, prior_fwd, 0)
    plan.tick(4.5)

    acc[...] = xv[...].astype(f32)
    lt.start()

    def outp(tt, _):
        acc[...] += dot_nt(att[tt], Gv(0, tt, 512, 256))
        return 0

    lax.fori_loop(0, 4, outp, 0)
    plan.need([norm_vectors])
    ng = [NG[i].astype(f32) for i in range(4)]
    r1, r3 = pltpu.roll(ng[1], 64, 1), pltpu.roll(ng[3], 64, 1)
    gains = jnp.concatenate(
        [ng[0][:, :128], ng[0][:, 128:] + r1[:, :128], r1[:, 128:],
         ng[2][:, :128], ng[2][:, 128:] + r3[:, :128], r3[:, 128:]], axis=1)
    gain1, shift1, gain2, shift2 = (gains[i:i + 1] for i in range(4))
    RB_ = 32

    def norm1(i, _):
        rows = pl.ds(pl.multiple_of(i * RB_, RB_), RB_)
        r = acc[rows, :]
        cen = r - jnp.mean(r, axis=1, keepdims=True)
        inv = lax.rsqrt(jnp.mean(cen * cen, axis=1, keepdims=True) + norm_eps)
        nrm = cen * inv
        y = nrm * gain1 + shift1
        n1[rows, :] = nrm
        inv1[rows, :] = jnp.broadcast_to(inv, (RB_, 128))
        acc[rows, :] = y
        nlow[rows, :] = y.astype(bf16)
        return 0

    lax.fori_loop(0, ROWS // RB_, norm1, 0)
    for j in range(3):
        nT[j * 256:(j + 1) * 256, :] = jnp.transpose(nlow[:, j * 256:(j + 1) * 256])

    plan.tick(5.0)
    plan.need(gat[1])

    r2_ = 1.0 / math.sqrt(2.0)

    def ffn_up(tt, _):
        for n in range(3):
            hpre = dot(nlow[...], Gv(1, tt, n * 256, 256))
            cum = 0.5 * (1.0 + lax.erf(hpre * r2_))
            dens = jnp.exp(-0.5 * hpre * hpre) * (1.0 / math.sqrt(2.0 * math.pi))
            act[tt, :, n * 256:(n + 1) * 256] = (hpre * cum).astype(bf16)
            der[tt, :, n * 256:(n + 1) * 256] = (cum + hpre * dens).astype(bf16)
        return 0

    lax.fori_loop(0, 2, ffn_up, 0)
    plan.tick(2.2)
    lax.fori_loop(2, 4, ffn_up, 0)
    plan.tick(2.2)
    plan.need(gat[2])

    def ffn_down(tt, _):
        acc[...] += dot_nt(act[tt], Gv(2, tt, 0, D))
        return 0

    lax.fori_loop(0, 4, ffn_down, 0)
    plan.tick(3.0)

    lt.wait()
    vc = val[0]

    def norm2(i, carry):
        sg, sh, sl = carry
        rows = pl.ds(pl.multiple_of(i * RB_, RB_), RB_)
        r = acc[rows, :]
        cen = r - jnp.mean(r, axis=1, keepdims=True)
        inv = lax.rsqrt(jnp.mean(cen * cen, axis=1, keepdims=True) + norm_eps)
        nrm = cen * inv
        res = nrm * gain2 + shift2
        goal = tv[rows, :].astype(f32)
        lob[rows, :] = res.astype(bf16)
        slot = base_slot + i * RB_ + lax.broadcasted_iota(jnp.int32, (RB_, 1), 0)
        e = jnp.where(slot < vc, res - goal, 0.0)
        sc = e * gain2
        g = inv * (sc - jnp.mean(sc, axis=1, keepdims=True) - nrm * jnp.mean(sc * nrm, axis=1, keepdims=True))
        acc[rows, :] = g
        glow[rows, :] = g.astype(bf16)

        def fold(v):
            return jnp.sum(v.reshape(RB_ // 8, 8, D), axis=0)

        return (sg + fold(e * nrm), sh + fold(e), sl + fold(e * e))

    z8 = jnp.zeros((8, D), f32)
    sg, sh, sl = lax.fori_loop(0, ROWS // RB_, norm2, (z8, z8, z8))
    sm[0:1] = jnp.sum(sg, axis=0, keepdims=True)
    sm[1:2] = jnp.sum(sh, axis=0, keepdims=True)
    sm[2:3] = 0.5 * jnp.sum(sl, axis=0, keepdims=True)
    for j in range(3):
        gT[j * 256:(j + 1) * 256, :] = jnp.transpose(glow[:, j * 256:(j + 1) * 256])

    def rows_of(ti):
        return pl.ds(pl.multiple_of(ti * ROWS, ROWS), ROWS)

    lo_l = lcopy(lob, lo_hbm.at[rows_of(t)])
    lo_l.start()
    ticks = [0]

    def step(us):
        plan.tick(us)
        if ticks[0] == OUTPUT_STEP:
            plan.begin(lo_out)
        ticks[0] += 1

    lo_c = send([rcopy(lob, lo_hbm.at[rows_of(t)], CORE)])
    lo_out = Small({YY: [rcopy(lob, lo_hbm.at[rows_of(t)], YY)],
                    CORE: [rcopy(lo_hbm.at[rows_of(t2)], lo_hbm.at[rows_of(t2)], CORE)]}, {YY: 5.3, CORE: 5.3})
    step(5.0)
    lx2.start()

    class Reduce:
        def __init__(self, m, acc4, j, width, order, alloc):
            self.m, self.order, self.acc4 = m, order + (FIN,), acc4
            self.lanes = pl.ds(j * width, width)
            self.stages, self.units, self.share = {}, {}, width / D
            h, sl, fl = None, [0, 1], [f, f1, f2, f3]
            for name in order:
                full = len(fl) == 4
                fs = [slice(None)] if full else fl
                if name == XX:
                    src = [(s, fi, c1) for s in sl for fi in fs]
                    keep = [(s, fi, c) for s in sl for fi in fs]
                    h = c
                elif name == YY:
                    hs = ((0, 1) if full else (slice(None),)) if h is None else (h,)
                    src = [(1, fi, hh) for fi in fs for hh in hs]
                    keep = [(0, fi, hh) for fi in fs for hh in hs]
                    sl = [0]
                else:
                    hh = slice(None) if h is None else h
                    away = (f1, f3) if name == Z0 else (f2,)
                    fl = [f, f2] if name == Z0 else [f]
                    if name == Z0:
                        stay = (f, f2)
                    else:
                        stay = (f,)
                    src = [(s, fi, hh) for s in sl for fi in away]
                    keep = [(s, fi, hh) for s in sl for fi in stay]
                self.stage(name, src, keep, alloc)
            self.fin_dst = alloc(1).at[:, self.lanes]
            self.stages[FIN] = ([rcopy(self.at(0, f, c), self.fin_dst, XX)], None, None)
            self.units[FIN] = self.share

        def at(self, s, fi, h):
            return self.acc4.at[2 + s, fi, h, slice(None), self.lanes]

        def stage(self, name, src, keep, alloc):
            sizes = [4 if isinstance(fi, slice) else 2 if isinstance(h, slice) else 1 for _, fi, h in src]
            dsts = []
            for n in sizes:
                b = alloc(n)
                dsts.append(b.at[:, self.lanes] if n == 1 else b.at[:, :, self.lanes])
            self.units[name] = sum(sizes) * self.share
            cps = [rcopy(self.at(*r), d, name) for r, d in zip(src, dsts)]
            self.stages[name] = (cps, dsts, [self.at(*r) for r in keep])

        def go(self, name):
            send(self.stages[name][0])

        def got(self, name):
            cps, dsts, keep = self.stages[name]
            for cp in cps:
                cp.wait()
                done(cp)
            if name == FIN:
                lput(self.at(0, f, c), gout.at[self.m, c, slice(None), self.lanes])
                lput(self.fin_dst, gout.at[self.m, c1, slice(None), self.lanes])
                return
            for p, q in zip(dsts, keep):
                if len(q.shape) == 2:
                    q[...] = q[...] + p[...]
                else:
                    for i in range(q.shape[0]):
                        q[i] = q[i] + p[i]

    puts = []

    def lput(src, dst):
        cp = lcopy(src, dst)
        cp.start()
        puts.append(cp)

    def flat_alloc(ref):
        at = [0]

        def alloc(n):
            i = at[0]
            at[0] += n
            return ref.at[i] if n == 1 else ref.at[pl.ds(i, n)]

        return alloc

    def gather_alloc():
        free = {(a, i, b) for a in (2, 3) for i in range(4) for b in range(2)}
        groups = {
            4: [({(a, i, b) for i in range(4)}, G.at[1, a, :, b]) for a in (2, 3) for b in range(2)],
            2: [({(a, i, 0), (a, i, 1)}, G.at[1, a, i]) for a in (3, 2) for i in range(4)],
            1: [({(a, i, b)}, G.at[1, a, i, b]) for a in (3, 2) for i in range(4) for b in (1, 0)],
        }

        def alloc(n):
            for cells, ref in groups[n]:
                if cells <= free:
                    free.difference_update(cells)
                    return ref
            raise ValueError(n)

        return alloc

    def pieces(m, acc4, orders, alloc_of):
        width = D // len(orders)
        return [Reduce(m, acc4, j, width, order, alloc_of()) for j, order in enumerate(orders)]

    D4, U4, A4 = W4.at[0], W4.at[1], G.at[2]
    coreD = [rcopy(D4.at[j], RC.at[0, j], CORE) for j in range(2)]
    coreU = [rcopy(U4.at[j], RC.at[1, j], CORE) for j in range(2)]
    coreA = [rcopy(A4.at[j], G.at[1, j], CORE) for j in range(2)]
    redD = pieces(2, D4, REDUCE_DOWN, lambda: flat_alloc(RB.at[0]))
    redU = pieces(1, U4, REDUCE_UP, lambda: flat_alloc(RB.at[1]))
    redA = pieces(0, A4, REDUCE_ATTENTION, gather_alloc)

    def add_core(cps, acc4, rc):
        for cp in cps:
            cp.wait()
            done(cp)

        def one(i, _):
            for j in range(2):
                for h in range(2):
                    acc4[2 + j, i, h] = acc4[2 + j, i, h] + rc[j, i, h]
            return 0

        lax.fori_loop(0, 4, one, 0)

    def shard_of(kk):
        return jnp.where(kk == 0, t1, jnp.where(kk == 1, t3, jnp.where(kk == 2, t, t2)))

    def down_grad(kk, _):
        tk = shard_of(kk)
        for n in range(3):
            cols = slice(n * 256, n * 256 + 256)
            D4[kk, :, :, :, cols] = dot(gT[...], act[tk, :, cols]).reshape(4, 2, 96, 256).astype(bf16)
        return 0

    def up_back(kk, _):
        tk = shard_of(kk)

        def blk(n, _):
            n0 = pl.multiple_of(n * 256, 256)
            cols = pl.ds(n0, 256)
            g = (dot(glow[...], Gd(2, tk, n0, 256)) * der[tk, :, cols].astype(f32)).astype(bf16)
            der[tk, :, cols] = g
            U4[kk, :, :, :, cols] = dot(nT[...], g).reshape(4, 2, 96, 256).astype(bf16)
            return 0

        lax.fori_loop(0, 3, blk, 0)
        acc[...] += dot_nt(der[tk], Gv(1, tk, 0, D))
        return 0

    lax.fori_loop(0, 2, down_grad, 0)
    send(coreD)
    lax.fori_loop(2, 4, down_grad, 0)
    add_core(coreD, D4, RC.at[0])
    step(3.0)
    step(3.0)
    for r in redD:
        plan.begin(r)
    lax.fori_loop(0, 2, up_back, 0)
    send(coreU)
    step(7.0)
    lax.fori_loop(2, 4, up_back, 0)
    step(7.0)
    add_core(coreU, U4, RC.at[1])
    for r in redU:
        plan.begin(r)

    def norm1b(i, carry):
        sg, sh = carry
        rows = pl.ds(pl.multiple_of(i * RB_, RB_), RB_)
        e = acc[rows, :]
        nrm = n1[rows, :]
        inv = inv1[rows, 0:1]
        sc = e * gain1
        g = inv * (sc - jnp.mean(sc, axis=1, keepdims=True) - nrm * jnp.mean(sc * nrm, axis=1, keepdims=True))
        acc[rows, :] = g
        glow[rows, :] = g.astype(bf16)

        def fold(v):
            return jnp.sum(v.reshape(RB_ // 8, 8, D), axis=0)

        return (sg + fold(e * nrm), sh + fold(e))

    sg, sh = lax.fori_loop(0, ROWS // RB_, norm1b, (z8, z8))
    sm[3:4] = jnp.sum(sg, axis=0, keepdims=True)
    sm[4:5] = jnp.sum(sh, axis=0, keepdims=True)
    sm[5:8] = jnp.zeros((3, D), f32)
    for j in range(3):
        gT[j * 256:(j + 1) * 256, :] = jnp.transpose(glow[:, j * 256:(j + 1) * 256])

    lx2.wait()
    for j in range(3):
        xT[j * 256:(j + 1) * 256, :] = jnp.transpose(nlow[:, j * 256:(j + 1) * 256])
    step(3.0)

    links = (CORE, YY, XX, Z0, Z1)

    def sums_step(d, arrived):
        i = 2 * links.index(d)
        if arrived:
            sm[...] = sm[...] + smr[i + 1]
        else:
            smr[i] = sm[...]

    sums = Small({d: [rcopy(smr.at[2 * i], smr.at[2 * i + 1], d)] for i, d in enumerate(links)},
                 dict.fromkeys(links, 0.17), sums_step)

    for g in gat[1] + gat[2]:
        for cps in g.stages.values():
            for cp in cps:
                cp.wait_send()
                done(cp)
    plan.begin(sums)

    def gn_rows(tt, _):
        gae = dot(glow[...], G[0, tt, :, :, :, 512:768].reshape(D, 256)).astype(bf16).astype(f32)
        g2_ = pltpu.roll(gae[:, 0:128], 64, 1)
        g0_ = gae[:, 128:256]
        g1_ = pltpu.roll(g0_, 64, 1)
        for j, g in enumerate((g0_, g1_, g2_)):
            h = tt * 3 + j
            v = nl[h]
            g = jnp.where(low_half, g, 0.0)
            den = jnp.broadcast_to(v[:, 64:65], (ROWS, 128))
            safe = jnp.maximum(den, 1.0)
            s = jnp.sum(g * jnp.where(low_half, v, 0.0), axis=1, keepdims=True)
            gd_ = jnp.where(den > 1.0, -s / safe, 0.0)
            gn = jnp.where(low_half, g / safe, jnp.where(lane == 64, gd_, 0.0))
            nl[h] = gn
            gnT = jnp.transpose(gn).astype(bf16)
            parts = [dot(gnT[:ST, i * 128:(i + 1) * 128], qf[h, i * 128:(i + 1) * 128, :]) for i in range(4)]
            dE[2, h] = (parts[0] + parts[1] + parts[2] + parts[3]).astype(bf16)
            mine = jnp.where(t == 2, 1, 3)
            theirs = jnp.where(t == 2, 3, 1)
            for slot, b in ((0, theirs), (1, theirs + 1), (3, mine), (4, mine + 1)):
                tot = jnp.zeros((ST, 128), f32)
                for i in range(4):
                    tot = tot + jnp.where(leaf_parent(i) == b, parts[i], 0.0)
                dE[slot, h] = tot.astype(bf16)
        return 0

    if HOLD_BACKWARD == 1:
        plan.hold()
    lax.fori_loop(0, 2, gn_rows, 0)
    step(4.2)
    if HOLD_BACKWARD == 2:
        plan.hold()
    lax.fori_loop(2, 4, gn_rows, 0)
    step(4.2)

    bc0 = [rcopy(dE.at[2], RR.at[2], CORE)]
    bc1 = [rcopy(dE.at[pl.ds(0, 3)], RR.at[pl.ds(0, 3)], CORE)]
    bx1 = [rcopy(dE.at[2, half], RX.at[half], XX)]
    by1 = [rcopy(dE.at[pl.ds(3, 2)], RR.at[pl.ds(4, 2)], YY)]
    by0 = [rcopy(TTb.at[half], RR.at[3, half], YY)]
    bo0 = [rcopy(dE.at[3, half], RR.at[4, half], CORE)]

    @pl.when(c == 0)
    def _():
        start(bc0)

    @pl.when(c == 1)
    def _():
        start(bc1)

    dq = act

    def pair(y, feat):
        y = y * cs[...]
        fc = feat.astype(f32)
        fc = jnp.where(low_half, fc, pltpu.roll(fc, 64, 1))
        return jnp.where(fc > 0.0, y + pltpu.roll(y, 64, 1), 0.0).astype(bf16)

    def bwd_q(tt, _):
        for j in range(3):
            h = tt * 3 + j
            gn = nl[h].astype(bf16)
            dw = dot_nt(gn, vx[h]).astype(bf16) * mk[...]
            pri = [dot(gn[i * 128:(i + 1) * 128, :], chunk_state(h, leaf_parent(i))) for i in range(4)]
            gq = pair(dot(dw, kf[h]) + jnp.concatenate(pri, axis=0), qf[h])
            if j == 0:
                dq[tt, :, 0:64] = gq[:, 0:64]
            elif j == 1:
                dq[tt, :, 64:128] = gq[:, 64:128]
            else:
                dq[tt, :, 384:448] = gq[:, 0:64]
        return 0

    lax.fori_loop(0, 1, bwd_q, 0)
    step(1.8)

    @pl.when(c == 0)
    def _():
        for cp in bc0:
            cp.wait()

    @pl.when(c == 1)
    def _():
        for cp in bc1:
            cp.wait()

        def addup(h, _):
            dE[2, h] = (dE[2, h].astype(f32) + RR[2, h].astype(f32)).astype(bf16)
            dE[3, h] = (dE[3, h].astype(f32) + RR[0, h].astype(f32)).astype(bf16)
            dE[4, h] = (dE[4, h].astype(f32) + RR[1, h].astype(f32)).astype(bf16)
            return 0

        lax.fori_loop(0, 12, addup, 0)
        start(bx1)

    @pl.when((c == 1) & jnp.logical_not(first_chip))
    def _():
        start(by1)

    if HOLD_BACKWARD == 0:
        plan.hold()
    due = plan.load(XX, 0.85)
    units_due = plan.load(YY, 3.4)
    lax.fori_loop(1, 4, bwd_q, 0)
    step(5.3)
    plan.gate(max(due, plan.now))

    @pl.when(c == 0)
    def _():
        wait_recv(bx1)

        def message(h):
            zero = jnp.zeros((ST, 128), f32)
            later = dE[2, h].astype(f32) + RR[2, h].astype(f32)
            TTb[h] = (jnp.where(t >= 2, later, zero) + RX[h].astype(f32)).astype(bf16)

        each_half(message)
        start(by0)

    due = plan.load(YY, 0.85)
    plan.release()

    def out_grad(kk, _):
        tt = shard_of(kk)
        v = dot(gT[...], att[tt])
        A4[kk, :, :, :, 512:768] = v.reshape(4, 2, 96, 256).astype(bf16)
        return 0

    lax.fori_loop(0, 4, out_grad, 0)
    step(2.0)
    plan.gate(max(due, units_due, plan.now))

    @pl.when(c == 0)
    def _():
        for cp in by0:
            cp.wait()

        def common(h):
            dE[3, h] = (RX[h].astype(f32) + RR[3, h].astype(f32)).astype(bf16)

        each_half(common)
        start(bo0)
        for cp in bo0:
            cp.wait()

    @pl.when(c == 1)
    def _():
        for cp in bx1:
            cp.wait_send()

    @pl.when((c == 1) & first_chip)
    def _():
        wait_recv(by1)

    @pl.when((c == 1) & jnp.logical_not(first_chip))
    def _():
        for cp in by1:
            cp.wait_send()

    step(1.5)

    def later_states(h):
        zero = jnp.zeros((ST, 128), f32)
        shared = jnp.where(h // 6 == core_id, dE[3, h].astype(f32), RR[4, h].astype(f32))
        d = jnp.where(t1 > t, RR[2, h].astype(f32), zero) + shared
        pad = jnp.zeros((128 - ST, 128), bf16)
        out = []
        for u in range(2):
            b = jnp.where(t < 2, RR[4 + u, h].astype(f32), zero)
            out.append(jnp.concatenate([jnp.where(c == 0, d, b).astype(bf16), pad], axis=0))
        return out

    def bwd_kv(kk, _):
        tt = shard_of(kk)
        for j in range(3):
            h = tt * 3 + j
            gn = nl[h].astype(bf16)
            ds = later_states(h)
            wT = dot_nt(kf[h], qf[h]).astype(bf16) * mkT[...]
            dv = dot(wT, gn) + jnp.concatenate(
                [dot_nt(kf[h, u * 256:(u + 1) * 256, :], ds[u]) for u in range(2)], axis=0)
            dwT = dot_nt(vx[h], gn).astype(bf16) * mkT[...]
            dk = dot(dwT, qf[h]) + jnp.concatenate(
                [dot(vx[h, u * 256:(u + 1) * 256, :], ds[u]) for u in range(2)], axis=0)
            gk = pair(dk, kf[h])
            if j == 0:
                dq[tt, :, 128:192] = gk[:, 0:64]
                dq[tt, :, 256:320] = dv[:, 0:64].astype(bf16)
            elif j == 1:
                dq[tt, :, 192:256] = gk[:, 64:128]
                dq[tt, :, 320:384] = pltpu.roll(dv, 64, 1)[:, 64:128].astype(bf16)
            else:
                dq[tt, :, 448:512] = gk[:, 64:128]
                dq[tt, :, 512:640] = jnp.where(low_half, dv, 0.0).astype(bf16)

        def put(l0, n, v):
            A4[kk, :, :, :, l0:l0 + n] = v.reshape(4, 2, 96, n).astype(bf16)

        put(0, 256, dot(xT[...], dq[tt, :, 0:256]))
        put(256, 256, dot(xT[...], dq[tt, :, 256:512]))
        o2 = A4[kk, :, :, :, 512:640].reshape(D, 128).astype(f32)
        put(512, 128, dot(xT[...], dq[tt, :, 512:640]) + o2)
        return 0

    for p in range(2):
        lax.fori_loop(2 * p, 2 * p + 2, bwd_kv, 0)
        step(5.8)
        if p == 0:
            plan.need([sums])
            send(coreA)
    add_core(coreA, A4, G.at[1])
    for r in redA:
        plan.begin(r)

    if ticks[0] <= OUTPUT_STEP:
        plan.begin(lo_out)
    def inback(tt, _):
        acc[...] += dot_nt(dq[tt, :, 0:640], Gv(0, tt, 0, 640))
        return 0

    lax.fori_loop(0, 4, inback, 0)
    igb[...] = acc[...].astype(bf16)
    ig_l = lcopy(igb, ig_hbm.at[rows_of(t)])
    ig_l.start()
    ig_c = send([rcopy(igb, ig_hbm.at[rows_of(t)], CORE)])
    ig_out = Small({YY: [rcopy(igb, ig_hbm.at[rows_of(t)], YY)],
                    CORE: [rcopy(ig_hbm.at[rows_of(t2)], ig_hbm.at[rows_of(t2)], CORE)]}, {YY: 5.3, CORE: 5.3})
    plan.tick(4.5)
    plan.begin(ig_out)
    plan.need(redD + redU + redA + [lo_out, ig_out])
    small[...] = sm[...]
    wait_recv(lo_c + ig_c)
    for cp in pending:
        cp.wait_send()
    for cp in puts + [lo_l, ig_l]:
        cp.wait()
    assert counter[0] <= N_REMOTE and lcounter[0] <= N_LOCAL, (counter, lcounter)


N_REMOTE, N_LOCAL = 320, 40


def fast_shards(layer_input, teacher, query_weight, key_weight, value_weight, out_weight, up_weight,
                down_weight, first_gain, first_shift, second_gain, second_shift, parents, valid_count):
    f = lax.axis_index(FSDP)
    D = layer_input.shape[-1]
    sc = layer_input.shape[1]
    tree_len = sc * lax.axis_size(CONTEXT)
    bf16, f32 = jnp.bfloat16, jnp.float32
    norms = jnp.pad(jnp.stack([first_gain, first_shift, second_gain, second_shift]), ((0, 12), (0, 64)))
    V = pltpu.VMEM
    scratch = [
        V((3, 4, 4, 2, 96, D), bf16),
        V((4, 16, 256), bf16),
        V((ROWS, D), bf16),
        V((12, ROWS, 128), bf16),
        V((12, ROWS, 128), bf16),
        V((12, ROWS, 128), bf16),
        V((ROWS, ROWS), bf16),
        V((ROWS, ROWS), bf16),
        V((ROWS, 128), f32),
        V((12, ROWS, 128), f32),
        V((4, ROWS, 256), bf16),
        V((ROWS, D), f32),
        V((ROWS, 128), f32),
        V((ROWS, D), bf16),
        V((4, ROWS, D), bf16),
        V((4, ROWS, D), bf16),
        V((ROWS, D), f32),
        V((ROWS, D), bf16),
        V((D, ROWS), bf16),
        V((D, ROWS), bf16),
        V((4, 12, ST, 128), bf16),
        V((12, ST, 128), bf16),
        V((12, ST, 128), bf16),
        V((6, 12, ST, 128), bf16),
        V((5, 12, ST, 128), bf16),
        V((12, ST, 128), bf16),
        V((2, 4, 4, 2, 96, D), bf16),
        V((2, 2, 4, 2, 96, D), bf16),
        V((2, 16, 96, D), bf16),
        V((8, D), f32),
        V((10, 8, D), f32),
        pltpu.SemaphoreType.DMA((N_REMOTE,)),
        pltpu.SemaphoreType.DMA((N_REMOTE,)),
        pltpu.SemaphoreType.DMA((N_LOCAL,)),
    ]
    any_, smem, vmem = (pl.BlockSpec(memory_space=s) for s in (pl.ANY, pltpu.SMEM, pltpu.VMEM))
    lo, ig, gout, small = pl.pallas_call(
        functools.partial(fast_kernel, tree_len=tree_len),
        out_shape=[
            jax.ShapeDtypeStruct((sc, D), bf16),
            jax.ShapeDtypeStruct((sc, D), bf16),
            jax.ShapeDtypeStruct((3, 2, 96, D), bf16),
            jax.ShapeDtypeStruct((8, D), f32),
        ],
        in_specs=[any_, any_, vmem, vmem, vmem, vmem, any_, any_, any_, smem, smem],
        out_specs=[any_, any_, any_, vmem],
        scratch_shapes=scratch,
        compiler_params=pltpu.CompilerParams(
            collective_id=0, has_side_effects=True, vmem_limit_bytes=67043328),
        name="tree_layer",
    )(layer_input, teacher, query_weight, key_weight, value_weight, out_weight, up_weight.reshape(2, 96, D),
      down_weight.T.reshape(2, 96, D), norms, parents, valid_count)
    g = gout.reshape(3, 192, D).astype(f32)
    A = g[0]
    q_g = jnp.concatenate([A[:, 0:128], A[:, 384:448]], axis=1)
    k_g = jnp.concatenate([A[:, 128:256], A[:, 448:512]], axis=1)
    v_g = jnp.concatenate([A[:, 256:384], A[:, 512:576]], axis=1)
    o_g = jnp.concatenate([A[:, 640:768], A[:, 576:640]], axis=1).T
    mine = lax.dynamic_slice(small, (0, f * 192), (8, 192))
    return (lo[None], ig.astype(f32)[None], jnp.sum(small[2]), q_g, k_g, v_g, o_g, g[1], g[2].T,
            mine[3], mine[4], mine[0], mine[1])


def shards(*arrays):
    tree_count, slot_count, width = arrays[0].shape
    sizes = tuple(lax.axis_size(n) for n in (FSDP, CONTEXT, TENSOR))
    if (tree_count, slot_count, width) == (1, 2048, 768) and sizes == (4, 2, 4) and arrays[6].shape == (192, 768):
        return fast_shards(*arrays)
    return general_shards(*arrays)


def solution(mesh):
    return jax.shard_map(
        shards,
        mesh=mesh,
        in_specs=(
            P(FSDP, CONTEXT, None),
            P(FSDP, CONTEXT, None),
            P(FSDP, TENSOR),
            P(FSDP, TENSOR),
            P(FSDP, TENSOR),
            P(TENSOR, FSDP),
            P(FSDP, TENSOR),
            P(TENSOR, FSDP),
            P(FSDP),
            P(FSDP),
            P(FSDP),
            P(FSDP),
            P(FSDP, None),
            P(FSDP),
        ),
        out_specs=(
            P(FSDP, CONTEXT, None),
            P(FSDP, CONTEXT, None),
            P(),
            P(FSDP, TENSOR),
            P(FSDP, TENSOR),
            P(FSDP, TENSOR),
            P(TENSOR, FSDP),
            P(FSDP, TENSOR),
            P(TENSOR, FSDP),
            P(FSDP),
            P(FSDP),
            P(FSDP),
            P(FSDP),
        ),
        check_vma=False,
    )
```

```python
import functools
import math

import jax
import jax.numpy as jnp
from jax import lax
from jax.experimental import pallas as pl
from jax.experimental.pallas import tpu as pltpu
from jax.sharding import PartitionSpec as P

HEAD_DIM = 64


precise = lax.Precision.HIGHEST
norm_eps = 1e-05


def carried_in(array, axis, combine, identity):
    count, here = (lax.axis_size(axis), lax.axis_index(axis))
    everything = jax.tree.map(
        lambda part, kind: lax.all_gather(part.astype(kind), axis),
        array,
        (jnp.bfloat16, jnp.bfloat16),
    )
    start = jax.tree.map(
        lambda part, zero: jnp.broadcast_to(jnp.asarray(zero, part.dtype), part.shape),
        array,
        identity,
    )

    def carried_turn(k, before):
        reached = k < here
        new = combine(
            before, jax.tree.map(lambda part, own: part[k].astype(own.dtype), everything, array)
        )
        return jax.tree.map(lambda a, b: jnp.where(reached, a, b), new, before)

    return lax.fori_loop(0, count, carried_turn, start)


def entering(array, axis, combine, identity):
    count, here = (lax.axis_size(axis), lax.axis_index(axis))
    everything = jax.tree.map(
        lambda part, kind: lax.all_gather(part.astype(kind), axis),
        array,
        jax.tree.map(lambda a: jnp.bfloat16 if a.dtype == jnp.float32 else a.dtype, array),
    )
    start = jax.tree.map(
        lambda part, zero: jnp.broadcast_to(jnp.asarray(zero, part.dtype), part.shape),
        array,
        identity,
    )

    def entering_turn(k, before):
        at = count - 1 - k
        reached = at > here
        new = combine(
            before, jax.tree.map(lambda part, own: part[at].astype(own.dtype), everything, array)
        )
        return jax.tree.map(lambda a, b: jnp.where(reached, a, b), new, before)

    return lax.fori_loop(0, count, entering_turn, start)


def layout_of(slot_ids, parents_row, tree_len):
    half_len = tree_len // 2
    branch_len = tree_len // 16
    leaf_len = tree_len // 32
    leaf_start = half_len + 4 * branch_len
    in_branch = (slot_ids >= half_len) & (slot_ids < leaf_start)
    in_leaf = slot_ids >= leaf_start
    branch_index = jnp.clip((slot_ids - half_len) // branch_len, 0, 3)
    leaf_index = jnp.clip((slot_ids - leaf_start) // leaf_len, 0, 7)
    leaf_ids = jnp.arange(8, dtype=jnp.int32)
    leaf_parent = jnp.sum(
        jnp.where(leaf_index[:, None] == leaf_ids[None, :], parents_row[None, :], 0), axis=1
    )
    segment = jnp.where(in_leaf, 5 + leaf_index, jnp.where(in_branch, 1 + branch_index, 0))
    owner_branch = jnp.where(in_leaf, leaf_parent, jnp.where(in_branch, 1 + branch_index, 0))
    leaf_pos = (
        half_len
        + jnp.where(leaf_parent > 0, branch_len, 0)
        + slot_ids
        - leaf_start
        - leaf_index * leaf_len
    )
    branch_pos = slot_ids - branch_index * branch_len
    position = jnp.where(in_leaf, leaf_pos, jnp.where(in_branch, branch_pos, slot_ids))
    phase_angle = (
        0.5 * math.pi * position.astype(jnp.float32) / float(half_len + branch_len + leaf_len)
    )
    return (segment, owner_branch, phase_angle)


def features(pre_act, phase_angle):
    rectified = jnp.maximum(pre_act, 0.0)
    cosine = jnp.cos(phase_angle)[..., None, None]
    sine_part = jnp.sin(phase_angle)[..., None, None]
    return jnp.concatenate([rectified * cosine, rectified * sine_part], axis=-1)


def features_back(grad_feat, pre_act, phase_angle):
    half_dim = pre_act.shape[-1]
    cosine = jnp.cos(phase_angle)[..., None, None]
    sine_part = jnp.sin(phase_angle)[..., None, None]
    combined = grad_feat[..., :half_dim] * cosine + grad_feat[..., half_dim:] * sine_part
    return jnp.where(pre_act > 0.0, combined, 0.0)


def norm_forward(resid, gain_vec, shift_vec):
    row_mean = jnp.mean(resid, axis=-1, keepdims=True)
    centered = resid - row_mean
    inv_std = lax.rsqrt(jnp.mean(centered * centered, axis=-1, keepdims=True) + norm_eps)
    normal = centered * inv_std
    return (normal * gain_vec + shift_vec, normal, inv_std)


def norm_backward(grad_out, normal, inv_std, gain_vec):
    scaled = grad_out * gain_vec
    grad_in = inv_std * (
        scaled
        - jnp.mean(scaled, axis=-1, keepdims=True)
        - normal * jnp.mean(scaled * normal, axis=-1, keepdims=True)
    )
    return (grad_in, jnp.sum(grad_out * normal, axis=0), jnp.sum(grad_out, axis=0))


def add_pair(earlier, later):
    return (earlier[0] + later[0], earlier[1] + later[1])


def general_shards(
    layer_input,
    teacher,
    query_weight,
    key_weight,
    value_weight,
    out_weight,
    up_weight,
    down_weight,
    first_gain,
    first_shift,
    second_gain,
    second_shift,
    parents,
    valid_count,
):
    tree_count, slot_count, model_width = layer_input.shape
    ctx_size = lax.axis_size(CONTEXT)
    ctx_index = lax.axis_index(CONTEXT)
    tree_len = slot_count * ctx_size
    row_count = tree_count * slot_count
    (
        full_query,
        full_key,
        full_value,
        full_out,
        full_up,
        full_down,
        gain_one,
        shift_one,
        gain_two,
        shift_two,
    ) = (
        lax.all_gather(query_weight, FSDP, axis=0, tiled=True),
        lax.all_gather(key_weight, FSDP, axis=0, tiled=True),
        lax.all_gather(value_weight, FSDP, axis=0, tiled=True),
        lax.all_gather(out_weight, FSDP, axis=1, tiled=True),
        lax.all_gather(up_weight, FSDP, axis=0, tiled=True),
        lax.all_gather(down_weight, FSDP, axis=1, tiled=True),
        lax.all_gather(first_gain, FSDP, axis=0, tiled=True),
        lax.all_gather(first_shift, FSDP, axis=0, tiled=True),
        lax.all_gather(second_gain, FSDP, axis=0, tiled=True),
        lax.all_gather(second_shift, FSDP, axis=0, tiled=True),
    )
    gain_one = gain_one.astype(jnp.float32)
    shift_one = shift_one.astype(jnp.float32)
    gain_two = gain_two.astype(jnp.float32)
    shift_two = shift_two.astype(jnp.float32)
    head_local = full_query.shape[1] // HEAD_DIM
    flat_in = layer_input.reshape(row_count, model_width)
    slot_ids = ctx_index * slot_count + jnp.arange(slot_count, dtype=jnp.int32)

    def layout_here(parents_row):
        return layout_of(slot_ids, parents_row, tree_len)

    segment, owner_branch, phase_angle = jax.vmap(layout_here)(parents)

    def project(weight):
        return jnp.dot(flat_in, weight, preferred_element_type=jnp.float32).reshape(
            tree_count, slot_count, head_local, HEAD_DIM
        )

    query_pre = project(full_query)
    key_pre = project(full_key)
    values = project(full_value).astype(jnp.bfloat16)
    query_feat = features(query_pre, phase_angle).astype(jnp.bfloat16)
    key_feat = features(key_pre, phase_angle).astype(jnp.bfloat16)
    query_wide = query_feat.astype(jnp.float32)
    key_wide = key_feat.astype(jnp.float32)
    value_wide = values.astype(jnp.float32)
    state_ids = jnp.arange(5, dtype=jnp.int32)
    segment_hit = segment[:, :, None] == state_ids
    in_segment = segment_hit.astype(jnp.float32)
    selected = ((state_ids == 0) | (owner_branch[:, :, None] == state_ids)).astype(jnp.float32)
    masked_key = jnp.where(
        segment_hit[:, :, :, None, None], key_feat[:, :, None], jnp.zeros((), jnp.bfloat16)
    )
    contrib_state = jnp.einsum(
        "tsahf,tshd->tahfd", masked_key, values, preferred_element_type=jnp.float32
    )
    contrib_norm = jnp.einsum(
        "tsa,tshf->tahf",
        segment_hit.astype(jnp.bfloat16),
        key_feat,
        preferred_element_type=jnp.float32,
    )
    zero_state = jnp.zeros_like(contrib_state)
    zero_norm = jnp.zeros_like(contrib_norm)
    prior_state, prior_norm = carried_in(
        (contrib_state, contrib_norm), CONTEXT, add_pair, (zero_state, zero_norm)
    )
    in_numer = jnp.einsum(
        "tsa,tshf,tahfd->tshd", selected, query_wide, prior_state, precision=precise
    )
    in_denom = jnp.einsum("tsa,tshf,tahf->tsh", selected, query_wide, prior_norm, precision=precise)
    block_rows = min(slot_count, 512)
    block_count = slot_count // block_rows

    def block_scores(block_index):
        row_start = block_index * block_rows
        query_rows = lax.dynamic_slice_in_dim(query_feat, row_start, block_rows, 1)
        slot_rows = lax.dynamic_slice_in_dim(slot_ids, row_start, block_rows, 0)
        segment_rows = lax.dynamic_slice_in_dim(segment, row_start, block_rows, 1)
        owner_rows = lax.dynamic_slice_in_dim(owner_branch, row_start, block_rows, 1)
        allowed = (slot_ids[None, None, :] <= slot_rows[None, :, None]) & (
            (segment[:, None, :] == segment_rows[:, :, None])
            | (segment[:, None, :] == 0)
            | (segment[:, None, :] == owner_rows[:, :, None])
        )
        allowed_wide = allowed[:, None].astype(jnp.float32)
        scores = (
            jnp.einsum("tihf,tjhf->thij", query_rows, key_feat, preferred_element_type=jnp.float32)
            * allowed_wide
        )
        return (scores, allowed_wide, query_rows)

    def local_forward(block_index):
        scores, allowed_wide, query_rows = block_scores(block_index)
        numerator = jnp.einsum("thij,tjhd->tihd", scores, value_wide, precision=precise)
        denominator = jnp.transpose(jnp.sum(scores, axis=3), (0, 2, 1))
        return (numerator, denominator)

    local_numer, local_denom = lax.map(local_forward, jnp.arange(block_count, dtype=jnp.int32))

    def unblock(stacked):
        return jnp.moveaxis(stacked, 0, 1).reshape((tree_count, slot_count) + stacked.shape[3:])

    numerator = unblock(local_numer) + in_numer
    denominator = unblock(local_denom) + in_denom
    safe_denom = jnp.maximum(denominator, 1.0)
    attended = numerator / safe_denom[..., None]
    attended_low = attended.astype(jnp.bfloat16).reshape(row_count, head_local * HEAD_DIM)
    attention_part = jnp.dot(attended_low, full_out, preferred_element_type=jnp.float32)
    attention_sum = lax.psum(attention_part.astype(jnp.bfloat16), TENSOR).astype(jnp.float32)
    resid_one = flat_in.astype(jnp.float32) + attention_sum
    normed_one, normal_one, inv_one = norm_forward(resid_one, gain_one, shift_one)
    normed_low = normed_one.astype(jnp.bfloat16)
    hidden_pre = jnp.dot(normed_low, full_up, preferred_element_type=jnp.float32)
    activated = jax.nn.gelu(hidden_pre, approximate=False).astype(jnp.bfloat16)
    ffn_part = jnp.dot(activated, full_down, preferred_element_type=jnp.float32)
    ffn_sum = lax.psum(ffn_part.astype(jnp.bfloat16), TENSOR).astype(jnp.float32)
    resid_two = normed_one + ffn_sum
    result, normal_two, inv_two = norm_forward(resid_two, gain_two, shift_two)
    layer_output = result.astype(jnp.bfloat16).reshape(tree_count, slot_count, model_width)
    valid_rows = (
        (slot_ids[None, :] < valid_count[:, None]).astype(jnp.float32).reshape(row_count, 1)
    )
    residual = (result - teacher.reshape(row_count, model_width).astype(jnp.float32)) * valid_rows
    loss_value = lax.psum(0.5 * jnp.sum(residual * residual), (FSDP, CONTEXT))
    grad_resid_two, second_gain_part, second_shift_part = norm_backward(
        residual, normal_two, inv_two, gain_two
    )
    grad_two_low = grad_resid_two.astype(jnp.bfloat16)
    down_part = jnp.dot(activated.T, grad_two_low, preferred_element_type=jnp.float32)
    grad_act = jnp.dot(grad_two_low, full_down.T, preferred_element_type=jnp.float32)
    cumulative = 0.5 * (1.0 + jax.scipy.special.erf(hidden_pre / math.sqrt(2.0)))
    density = jnp.exp(-0.5 * hidden_pre * hidden_pre) / math.sqrt(2.0 * math.pi)
    grad_pre = (grad_act * (cumulative + hidden_pre * density)).astype(jnp.bfloat16)
    up_part = jnp.dot(normed_low.T, grad_pre, preferred_element_type=jnp.float32)
    ffn_back = jnp.dot(grad_pre, full_up.T, preferred_element_type=jnp.float32)
    grad_normed_one = grad_resid_two + lax.psum(ffn_back.astype(jnp.bfloat16), TENSOR).astype(
        jnp.float32
    )
    grad_resid_one, first_gain_part, first_shift_part = norm_backward(
        grad_normed_one, normal_one, inv_one, gain_one
    )
    grad_one_low = grad_resid_one.astype(jnp.bfloat16)
    out_part = jnp.dot(attended_low.T, grad_one_low, preferred_element_type=jnp.float32)
    grad_attended = jnp.dot(grad_one_low, full_out.T, preferred_element_type=jnp.float32).astype(
        jnp.bfloat16
    )
    grad_attended = grad_attended.astype(jnp.float32).reshape(
        tree_count, slot_count, head_local, HEAD_DIM
    )
    grad_numer = grad_attended / safe_denom[..., None]
    grad_denom = jnp.where(
        denominator > 1.0, -jnp.sum(grad_attended * attended, axis=-1) / safe_denom, 0.0
    )
    grad_query = jnp.einsum(
        "tsa,tshd,tahfd->tshf", selected, grad_numer, prior_state, precision=precise
    ) + jnp.einsum("tsa,tsh,tahf->tshf", selected, grad_denom, prior_norm, precision=precise)
    grad_prior_state = jnp.einsum(
        "tsa,tshf,tshd->tahfd", selected, query_wide, grad_numer, precision=precise
    )
    grad_prior_norm = jnp.einsum(
        "tsa,tshf,tsh->tahf", selected, query_wide, grad_denom, precision=precise
    )
    grad_contrib_state, grad_contrib_norm = entering(
        (grad_prior_state, grad_prior_norm), CONTEXT, add_pair, (zero_state, zero_norm)
    )
    grad_key = jnp.einsum(
        "tsa,tshd,tahfd->tshf", in_segment, value_wide, grad_contrib_state, precision=precise
    ) + jnp.einsum("tsa,tahf->tshf", in_segment, grad_contrib_norm, precision=precise)
    grad_value = jnp.einsum(
        "tsa,tshf,tahfd->tshd", in_segment, key_wide, grad_contrib_state, precision=precise
    )

    def local_backward(carried, block_index):
        acc_key, acc_value = carried
        scores, allowed_wide, query_rows = block_scores(block_index)
        row_start = block_index * block_rows
        numer_rows = lax.dynamic_slice_in_dim(grad_numer, row_start, block_rows, 1)
        denom_rows = lax.dynamic_slice_in_dim(grad_denom, row_start, block_rows, 1)
        grad_scores = (
            jnp.einsum("tihd,tjhd->thij", numer_rows, value_wide, precision=precise)
            + jnp.transpose(denom_rows, (0, 2, 1))[:, :, :, None]
        ) * allowed_wide
        rows_grad = jnp.einsum("thij,tjhf->tihf", grad_scores, key_wide, precision=precise)
        acc_key = acc_key + jnp.einsum(
            "thij,tihf->tjhf", grad_scores, query_rows.astype(jnp.float32), precision=precise
        )
        acc_value = acc_value + jnp.einsum("thij,tihd->tjhd", scores, numer_rows, precision=precise)
        return ((acc_key, acc_value), rows_grad)

    (local_key, local_value), local_query = lax.scan(
        local_backward,
        (jnp.zeros_like(key_wide), jnp.zeros_like(value_wide)),
        jnp.arange(block_count, dtype=jnp.int32),
    )
    grad_query = grad_query + unblock(local_query)
    grad_key = grad_key + local_key
    grad_value = grad_value + local_value
    grad_query_low = (
        features_back(grad_query, query_pre, phase_angle)
        .astype(jnp.bfloat16)
        .reshape(row_count, -1)
    )
    grad_key_low = (
        features_back(grad_key, key_pre, phase_angle).astype(jnp.bfloat16).reshape(row_count, -1)
    )
    grad_value_low = grad_value.astype(jnp.bfloat16).reshape(row_count, -1)
    query_part = jnp.dot(flat_in.T, grad_query_low, preferred_element_type=jnp.float32)
    key_part = jnp.dot(flat_in.T, grad_key_low, preferred_element_type=jnp.float32)
    value_part = jnp.dot(flat_in.T, grad_value_low, preferred_element_type=jnp.float32)
    input_back = (
        jnp.dot(grad_query_low, full_query.T, preferred_element_type=jnp.float32)
        + jnp.dot(grad_key_low, full_key.T, preferred_element_type=jnp.float32)
        + jnp.dot(grad_value_low, full_value.T, preferred_element_type=jnp.float32)
    )
    input_grad = (
        grad_resid_one + lax.psum(input_back.astype(jnp.bfloat16), TENSOR).astype(jnp.float32)
    ).reshape(tree_count, slot_count, model_width)
    grad_parts = (
        query_part,
        key_part,
        value_part,
        out_part,
        up_part,
        down_part,
        first_gain_part,
        first_shift_part,
        second_gain_part,
        second_shift_part,
    )
    summed = (
        lax.psum(grad_parts[0].astype(jnp.bfloat16), CONTEXT).astype(jnp.float32),
        lax.psum(grad_parts[1].astype(jnp.bfloat16), CONTEXT).astype(jnp.float32),
        lax.psum(grad_parts[2].astype(jnp.bfloat16), CONTEXT).astype(jnp.float32),
        lax.psum(grad_parts[3].astype(jnp.bfloat16), CONTEXT).astype(jnp.float32),
        lax.psum(grad_parts[4].astype(jnp.bfloat16), CONTEXT).astype(jnp.float32),
        lax.psum(grad_parts[5].astype(jnp.bfloat16), CONTEXT).astype(jnp.float32),
        lax.psum(grad_parts[6].astype(jnp.bfloat16), CONTEXT).astype(jnp.float32),
        lax.psum(grad_parts[7].astype(jnp.bfloat16), CONTEXT).astype(jnp.float32),
        lax.psum(grad_parts[8].astype(jnp.bfloat16), CONTEXT).astype(jnp.float32),
        lax.psum(grad_parts[9].astype(jnp.bfloat16), CONTEXT).astype(jnp.float32),
    )
    reduced = (
        lax.psum_scatter(
            summed[0].astype(jnp.bfloat16), FSDP, scatter_dimension=0, tiled=True
        ).astype(jnp.float32),
        lax.psum_scatter(
            summed[1].astype(jnp.bfloat16), FSDP, scatter_dimension=0, tiled=True
        ).astype(jnp.float32),
        lax.psum_scatter(
            summed[2].astype(jnp.bfloat16), FSDP, scatter_dimension=0, tiled=True
        ).astype(jnp.float32),
        lax.psum_scatter(
            summed[3].astype(jnp.bfloat16), FSDP, scatter_dimension=1, tiled=True
        ).astype(jnp.float32),
        lax.psum_scatter(
            summed[4].astype(jnp.bfloat16), FSDP, scatter_dimension=0, tiled=True
        ).astype(jnp.float32),
        lax.psum_scatter(
            summed[5].astype(jnp.bfloat16), FSDP, scatter_dimension=1, tiled=True
        ).astype(jnp.float32),
        lax.psum_scatter(
            summed[6].astype(jnp.bfloat16), FSDP, scatter_dimension=0, tiled=True
        ).astype(jnp.float32),
        lax.psum_scatter(
            summed[7].astype(jnp.bfloat16), FSDP, scatter_dimension=0, tiled=True
        ).astype(jnp.float32),
        lax.psum_scatter(
            summed[8].astype(jnp.bfloat16), FSDP, scatter_dimension=0, tiled=True
        ).astype(jnp.float32),
        lax.psum_scatter(
            summed[9].astype(jnp.bfloat16), FSDP, scatter_dimension=0, tiled=True
        ).astype(jnp.float32),
    )
    return (
        layer_output,
        input_grad,
        loss_value,
        reduced[0],
        reduced[1],
        reduced[2],
        reduced[3],
        reduced[4],
        reduced[5],
        reduced[6],
        reduced[7],
        reduced[8],
        reduced[9],
    )


MESH_ID = pl.DeviceIdType.MESH
ROWS = 512
CORE, YY, XX, Z0, Z1, FIN = range(6)
FSDP, CONTEXT, TENSOR = "fsdp", "context", "tensor"
ST = 80


GATHER_ATTENTION = (
    (Z0, Z1, XX, YY),
    (Z1, YY, XX, Z0),
    (Z1, YY, Z0, XX),
    (Z1, Z0, XX, YY),
    (Z1, Z0, YY, XX),
    (Z1, Z0, YY, XX),
)
GATHER_UP = (
    (Z1, YY, XX, Z0),
    (Z1, YY, Z0, XX),
    (Z1, Z0, XX, YY),
)
GATHER_DOWN = (
    (Z0, YY, Z1, XX),
    (YY, Z1, XX, Z0),
    (Z0, Z1, XX, YY),
)
REDUCE_DOWN = (
    (XX, YY, Z0, Z1),
    (XX, YY, Z0, Z1),
    (Z0, XX, YY, Z1),
)
REDUCE_UP = (
    (Z0, XX, Z1, YY),
    (Z0, XX, YY, Z1),
    (XX, YY, Z0, Z1),
)
REDUCE_ATTENTION = (
    (XX, Z0, Z1, YY),
    (XX, Z0, Z1, YY),
    (Z0, XX, Z1, YY),
    (YY, XX, Z0, Z1),
    (Z0, Z1, XX, YY),
    (XX, Z0, YY, Z1),
)
GATE_U, GATE_D = 8.0, 8.0
HOLD_FORWARD, HOLD_BACKWARD, OUTPUT_STEP = False, 2, 0
UNIT_US, HOP_US, CORE_US = 3.28, 1.7, 0.3


class Plan:
    def __init__(self):
        self.now, self.free, self.flying = 0.0, {}, []
        self.holding, self.held = False, []

    def begin(self, piece):
        piece.at_stage = -1
        self.advance(piece)

    def load(self, stage, units):
        ends = []
        for link, us in self.cost(stage, units):
            ends.append(max(self.now, self.free.get(link, 0.0)) + us)
            self.free[link] = ends[-1]
        return max(ends) + HOP_US

    @staticmethod
    def cost(stage, units):
        if stage == CORE:
            return ((CORE, units * CORE_US),)
        us = units * UNIT_US
        if stage == Z1:
            return ((Z0, us), (Z1, 2 * us))
        return ((stage, us),)

    def advance(self, piece):
        piece.at_stage += 1
        if piece.at_stage < len(piece.order):
            stage = piece.order[piece.at_stage]
            if self.holding and stage in (XX, YY):
                self.held.append(piece)
                return
            piece.go(stage)
            self.flying.append((self.load(stage, piece.units[stage]), len(self.flying), piece))

    def take(self, until):
        if not self.flying:
            assert until < math.inf
            return False
        first = min(self.flying, key=lambda e: e[0])
        if first[0] > until:
            return False
        self.flying.remove(first)
        self.now = max(self.now, first[0])
        piece = first[2]
        piece.got(piece.order[piece.at_stage])
        self.advance(piece)
        return True

    def tick(self, us):
        self.now += us
        while self.take(self.now - 0.5):
            pass

    def hold(self):
        self.holding = True

    def release(self):
        self.holding = False
        held, self.held = self.held, []
        for piece in held:
            piece.at_stage -= 1
            self.advance(piece)

    def gate(self, until):
        while self.take(until):
            pass
        self.now = max(self.now, until)

    def need(self, pieces, stage=None):
        def short(p):
            done = p.at_stage
            return done < (len(p.order) if stage is None else p.order.index(stage) + 1)

        while any(short(p) for p in pieces):
            self.take(math.inf)


def fast_kernel(*refs, tree_len):
    (x_hbm, t_hbm, q_in, k_in, v_in, o_in, u_in, d_in, g1_in, s1_in, g2_in, s2_in, par, val,
     lo_hbm, ig_hbm, gout, small,
     G, NG, xv, qf, kf, vx, mk, mkT, cs, nl, att, n1, inv1, nlow, act, der, acc, glow, gT, nT,
     SR, PS, TTb, RR, dE, RX, W4, RC, RB, sm, smr, ss, rs, ls) = refs
    f = lax.axis_index(FSDP)
    c = lax.axis_index(CONTEXT)
    t = lax.axis_index(TENSOR)
    t1 = t + 1 - 2 * lax.rem(t, 2)
    t2 = lax.rem(t + 2, 4)
    t3 = lax.rem(t1 + 2, 4)
    f1 = f + 1 - 2 * lax.rem(f, 2)
    f2 = lax.rem(f + 2, 4)
    f3 = lax.rem(f1 + 2, 4)
    c1 = 1 - c
    tks = [t, t2, t1, t3]
    DEV = {CORE: {TENSOR: t1}, YY: {TENSOR: t2}, XX: {CONTEXT: c1}, Z0: {FSDP: f1}, Z1: {FSDP: f2}}
    D = 768
    counter = [0]

    def rcopy(src, dst, dev):
        i = counter[0]
        counter[0] += 1
        return pltpu.make_async_remote_copy(
            src_ref=src, dst_ref=dst, send_sem=ss.at[i], recv_sem=rs.at[i],
            device_id=DEV[dev], device_id_type=MESH_ID)

    class Batch:
        def __init__(self, pairs, dev, units, width):
            i = counter[0]
            counter[0] += 1
            self.copies = [
                pltpu.make_async_remote_copy(
                    src_ref=a, dst_ref=b, send_sem=ss.at[i], recv_sem=rs.at[i],
                    device_id=DEV[dev], device_id_type=MESH_ID)
                for a, b in pairs]
            like = RB.at[0, pl.ds(0, units), slice(None), pl.ds(0, width)]
            self.sent = pltpu.make_async_copy(like, like, ss.at[i])
            self.come = pltpu.make_async_copy(like, like, rs.at[i])

        def start(self):
            for cp in self.copies:
                cp.start()

        def wait_send(self):
            self.sent.wait()

        def wait_recv(self):
            self.come.wait()

        def wait(self):
            self.wait_send()
            self.wait_recv()

    def rbatch(pairs, dev, units, width):
        if len(pairs) == 1:
            return [rcopy(*pairs[0], dev)]
        return [Batch(pairs, dev, units, width)]

    lcounter = [0]

    def lcopy(src, dst):
        i = lcounter[0]
        lcounter[0] += 1
        return pltpu.make_async_copy(src, dst, ls.at[i])

    def start(cps):
        for cp in cps:
            cp.start()

    def wait_recv(cps):
        for cp in cps:
            cp.wait_recv()

    pending = []

    def send(cps):
        start(cps)
        pending.extend(cps)
        return cps

    def done(cp):
        pending[:] = [other for other in pending if other is not cp]

    f32, bf16 = jnp.float32, jnp.bfloat16

    def dot(a, b):
        return lax.dot_general(a, b, (((1,), (0,)), ((), ())), preferred_element_type=f32)

    def dot_nt(a, b):
        return lax.dot_general(a, b, (((1,), (1,)), ((), ())), preferred_element_type=f32)

    class Small:
        def __init__(self, stages, units, after=None):
            self.order = tuple(stages)
            self.stages, self.units, self.after = stages, units, after

        def go(self, stage):
            if self.after is not None:
                self.after(stage, False)
            send(self.stages[stage])

        def got(self, stage):
            wait_recv(self.stages[stage])
            if self.after is not None:
                self.after(stage, True)

    bar = pltpu.get_barrier_semaphore()
    for dev in DEV.values():
        pl.semaphore_signal(bar, inc=1, device_id=dev, device_id_type=MESH_ID)

    def block_of(ti):
        return jnp.where(c == 0, ti, 2 * lax.rem(ti, 2) + ti // 2)

    row0 = pl.multiple_of(block_of(t) * ROWS, ROWS)
    lx = lcopy(x_hbm.at[0, pl.ds(row0, ROWS), :], xv)
    lt = lcopy(t_hbm.at[0, pl.ds(row0, ROWS), :], xv)
    lx2 = lcopy(x_hbm.at[0, pl.ds(row0, ROWS), :], nlow)
    tv = lob = xv
    igb, xT = nlow, nT
    own = [lcopy(w_in, G.at[m, t, f]) for m, w_in in ((1, u_in), (2, d_in))]
    start([lx] + own)
    oT = jnp.transpose(o_in[...].astype(jnp.float32)).astype(jnp.bfloat16)
    for h in range(2):
        r = slice(h * 96, h * 96 + 96)
        own_a = G.at[0, t, f, h]
        own_a[:, 0:128] = q_in[r, 0:128]
        own_a[:, 128:256] = k_in[r, 0:128]
        own_a[:, 256:384] = v_in[r, 0:128]
        own_a[:, 384:512] = jnp.concatenate([q_in[r, 128:192], k_in[r, 128:192]], axis=1)
        own_a[:, 512:640] = jnp.concatenate([v_in[r, 128:192], oT[r, 128:192]], axis=1)
        own_a[:, 640:768] = oT[r, 0:128]
    row = lax.broadcasted_iota(jnp.int32, (16, 192), 0)
    vectors = jnp.zeros((16, 192), jnp.float32)
    for i, v_ref in enumerate((g1_in, s1_in, g2_in, s2_in)):
        v = v_ref[...].astype(jnp.float32).reshape(1, 192)
        vectors = jnp.where(row == i, jnp.broadcast_to(v, (16, 192)), vectors)
    NG[f] = jnp.zeros((16, 256), jnp.bfloat16)
    NG[f, :, 0:192] = vectors.astype(jnp.bfloat16)
    for cp in own:
        cp.wait()
    pl.semaphore_wait(bar, 5)

    far, near = {id(f): f2, id(f1): f3}, {id(f): f1, id(f2): f3}
    class Gather:
        def __init__(self, m, l0, n, order, split):
            self.lanes = slice(None) if n == D else pl.ds(l0, n)
            self.m, self.order = m, order
            self.ts, self.fs = [t], [f]
            self.h = c if split else None
            self.stages, self.units, self.share, self.width = {}, {}, n / D, n
            for stage in order:
                self.stages[stage] = self.build(stage)

        def at(self, ti, fi, h):
            hh = slice(None) if h is None else h
            return G.at[self.m, ti, fi, hh, slice(None), self.lanes]

        def build(self, stage):
            regs = []
            fl = [slice(None)] if len(self.fs) == 4 else self.fs
            if stage == XX:
                for ti in self.ts:
                    if ti is t:
                        others = [fi for fi in self.fs if fi is not f]
                        regs += [(ti, fi, c) for fi in others]
                    else:
                        regs += [(ti, fi, c) for fi in fl]
                self.h = None
            else:
                regs = [(ti, fi, self.h) for ti in self.ts for fi in fl]
                if stage == Z1:
                    self.fs = self.fs + [far[id(v)] for v in self.fs]
                if stage == Z0:
                    self.fs = self.fs + [near[id(v)] for v in self.fs]
                if stage == YY:
                    self.ts = self.ts + [t2]
                if stage == CORE:
                    self.ts = self.ts + [t1, t3]
            count = sum((4 if isinstance(fi, slice) else 1) * (2 if h is None else 1) for _, fi, h in regs)
            self.units[stage] = count * self.share
            return rbatch([(self.at(*r), self.at(*r)) for r in regs], stage, count, self.width)

        def go(self, stage):
            send(self.stages[stage])

        def got(self, stage):
            wait_recv(self.stages[stage])

    gather_orders = (GATHER_ATTENTION, GATHER_UP, GATHER_DOWN)
    gat = [[Gather(m, j * (D // len(o)), D // len(o), order + (CORE,), True) for j, order in enumerate(o)]
           for m, o in enumerate(gather_orders)]
    norm_vectors = Small(
        {Z1: [rcopy(NG.at[f], NG.at[f], Z1)],
         Z0: [rcopy(NG.at[f], NG.at[f], Z0), rcopy(NG.at[f2], NG.at[f2], Z0)]}, {Z1: 0.03, Z0: 0.06})
    plan = Plan()
    for g in gat[0][:5]:
        plan.begin(g)
    plan.begin(norm_vectors)

    lane = lax.broadcasted_iota(jnp.int32, (ROWS, 128), 1)
    low_half = lane < 64
    half_len, branch_len, leaf_len = tree_len // 2, tree_len // 16, tree_len // 32
    leaf_start = half_len + 4 * branch_len
    base_slot = c * (4 * ROWS) + block_of(t) * ROWS

    def layout(slot):
        in_leaf = slot >= leaf_start
        in_branch = (slot >= half_len) & jnp.logical_not(in_leaf)
        bi = jnp.clip((slot - half_len) >> (branch_len.bit_length() - 1), 0, 3)
        li = jnp.clip((slot - leaf_start) >> (leaf_len.bit_length() - 1), 0, 7)
        lp = jnp.zeros_like(slot)
        for k in range(8):
            lp = jnp.where(li == k, par[0, k], lp)
        seg = jnp.where(in_leaf, 5 + li, jnp.where(in_branch, 1 + bi, 0))
        own_b = jnp.where(in_leaf, lp, jnp.where(in_branch, 1 + bi, 0))
        leaf_pos = half_len + jnp.where(lp > 0, branch_len, 0) + slot - leaf_start - li * leaf_len
        posn = jnp.where(in_leaf, leaf_pos, jnp.where(in_branch, slot - bi * branch_len, slot))
        return seg, own_b, posn

    slot_col = base_slot + lax.broadcasted_iota(jnp.int32, (ROWS, 128), 0)
    seg_c, own_c, pos_c = layout(slot_col)
    ang = 0.5 * math.pi * pos_c.astype(f32) / float(half_len + branch_len + leaf_len)
    cs[...] = jnp.where(low_half, jnp.cos(ang), jnp.sin(ang))
    slot_row = base_slot + lax.broadcasted_iota(jnp.int32, (8, ROWS), 1)
    seg_r8, own_r8, _ = layout(slot_row)
    seg_r, own_r, sl_r = seg_r8[0:1], own_r8[0:1], slot_row[0:1]
    for j in range(4):
        ls_ = slice(j * 128, j * 128 + 128)
        sr, orr, slr = seg_r[:, ls_], own_r[:, ls_], sl_r[:, ls_]
        ok = (slr <= slot_col) & ((sr == seg_c) | (sr == 0) | (sr == own_c))
        mk[:, ls_] = jnp.where(ok, 1.0, 0.0).astype(bf16)
        okT = (slot_col <= slr) & ((seg_c == sr) | (seg_c == 0) | (seg_c == orr))
        mkT[:, ls_] = jnp.where(okT, 1.0, 0.0).astype(bf16)
    lx.wait()

    plan.tick(4.0)
    plan.gate(GATE_U)
    for g in gat[0][5:] + gat[1]:
        plan.begin(g)
    plan.gate(GATE_D)
    for g in gat[2]:
        plan.begin(g)

    def Gv(m, tk, l0, n):
        return G[m, tk, :, :, :, l0:l0 + n].reshape(D, n)

    def Gd(m, tk, n0, n):
        return G[m, tk, :, :, :, pl.ds(n0, n)].reshape(D, n)

    def from_low(p):
        return (jnp.where(low_half, p, pltpu.roll(p, 64, 1)) * cs[...]).astype(bf16)

    def from_high(p):
        return (jnp.where(low_half, pltpu.roll(p, 64, 1), p) * cs[...]).astype(bf16)

    def vext(p, up):
        p = pltpu.roll(p, 64, 1) if up else p
        return jnp.where(low_half, p, jnp.where(lane == 64, 1.0, 0.0)).astype(bf16)

    def project_kv(tk):
        h = tk * 3
        a = dot(xv[...], Gv(0, tk, 128, 256))
        k01 = jnp.maximum(a[:, :128], 0.0)
        kf[h] = from_low(k01)
        kf[h + 1] = from_high(k01)
        vx[h] = vext(a[:, 128:], False)
        vx[h + 1] = vext(a[:, 128:], True)
        b = dot(xv[...], Gv(0, tk, 384, 256))
        r = jnp.maximum(b[:, :128], 0.0)
        qf[h + 2] = from_low(r)
        kf[h + 2] = from_high(r)
        vx[h + 2] = vext(b[:, 128:], False)
        for j in range(3):
            vT = jnp.transpose(vx[h + j].astype(f32)).astype(bf16)
            u0 = dot(vT[:ST, :256], kf[h + j, :256])
            u1 = dot(vT[:ST, 256:], kf[h + j, 256:])
            first = jnp.where(c == 0, u0 + u1, u0)
            dE[0, h + j] = first.astype(bf16)
            dE[1, h + j] = u1.astype(bf16)

    def project_q(tk, _):
        q01 = jnp.maximum(dot(xv[...], Gv(0, tk, 0, 128)), 0.0)
        qf[tk * 3] = from_low(q01)
        qf[tk * 3 + 1] = from_high(q01)
        return 0

    first_needed, last_needed = gat[0][1:5], gat[0][:1]
    for g in first_needed:
        plan.need([g], g.order[-2])
    project_kv(tks[0])
    plan.tick(1.1)
    project_kv(tks[1])
    plan.tick(1.1)
    plan.need(first_needed)
    if HOLD_FORWARD:
        plan.hold()
    project_kv(tks[2])
    plan.tick(1.1)
    project_kv(tks[3])
    plan.tick(1.1)

    core_id = lax.rem(t, 2)
    half = pl.ds(pl.multiple_of(core_id * 6, 6), 6)
    has_leaves = (c == 1) & (core_id == 1)
    has_branches = (c == 1) & (core_id == 0)
    fc0 = [rcopy(dE.at[0], SR.at[1], CORE)]
    fy0 = [rcopy(dE.at[1, half], SR.at[0, half], YY)]
    fx0 = [rcopy(TTb.at[half], PS.at[half], XX)]
    fo0 = [rcopy(SR.at[0, half], SR.at[2, half], CORE)]
    fy1 = [rcopy(dE.at[pl.ds(0, 2)], SR.at[pl.ds(0, 2)], YY)]
    fn1 = [rcopy(dE.at[pl.ds(0, 2)], SR.at[pl.ds(0, 2)], CORE)]
    fc1 = [rcopy(SR.at[pl.ds(0, 2)], SR.at[pl.ds(2, 2)], CORE)]
    fo1 = [rcopy(PS.at[half], PS.at[half], CORE)]

    def each_half(body):
        def one(i, _):
            body(core_id * 6 + i)
            return 0

        lax.fori_loop(0, 6, one, 0)

    def local_fwd(h, _):
        s = dot_nt(qf[h], kf[h]).astype(bf16) * mk[...]
        nl[h] = dot(s, vx[h])
        return 0

    @pl.when(c == 0)
    def _():
        start(fc0)

    @pl.when(has_branches)
    def _():
        start(fy1)
        start(fn1)

    units_due = plan.load(YY, 1.7)
    plan.need(last_needed)
    lax.fori_loop(0, 4, project_q, 0)
    plan.tick(1.8)

    @pl.when(c == 0)
    def _():
        for cp in fc0:
            cp.wait()

        def chip_sum(h):
            dE[1, h] = (dE[0, h].astype(f32) + SR[1, h].astype(f32)).astype(bf16)

        each_half(chip_sum)
        start(fy0)

    due = plan.load(YY, 0.85)
    lax.fori_loop(0, 7, local_fwd, 0)
    plan.tick(3.7)
    plan.gate(max(due, plan.now))

    @pl.when(c == 0)
    def _():
        for cp in fy0:
            cp.wait()

        def total(h):
            TTb[h] = (dE[1, h].astype(f32) + SR[0, h].astype(f32)).astype(bf16)

        each_half(total)
        start(fx0)
        start(fo0)

    due = plan.load(XX, 0.85) + 1.5
    plan.release()
    lax.fori_loop(7, 12, local_fwd, 0)
    plan.tick(2.7)
    plan.gate(max(units_due + 1.5, due, plan.now))

    @pl.when(c == 0)
    def _():
        for cp in fo0:
            cp.wait()
        for cp in fx0:
            cp.wait_send()

        def before(h, _):
            zero = jnp.zeros((ST, 128), f32)
            mine = h // 6 == core_id
            other = jnp.where(mine, SR[0, h].astype(f32), SR[2, h].astype(f32))
            p = jnp.where(t1 < t, SR[1, h].astype(f32), zero) + jnp.where(t2 < t, other, zero)
            PS[h] = p.astype(bf16)
            return 0

        lax.fori_loop(0, 12, before, 0)

    @pl.when(c == 1)
    def _():
        wait_recv(fx0)
        start(fo1)

    @pl.when(has_branches)
    def _():
        for cp in fy1:
            cp.wait()
        start(fc1)
        for cp in fn1 + fc1:
            cp.wait_send()

    @pl.when(has_leaves)
    def _():
        wait_recv(fn1 + fc1)

    @pl.when(c == 1)
    def _():
        for cp in fo1:
            cp.wait()


    def leaf_parent(i):
        return jnp.where(has_leaves, jnp.where(t < 2, par[0, i], par[0, 4 + i]), 0)

    low_base = jnp.where(t < 2, 0, 2)
    high_base = jnp.where(t < 2, 2, 0)

    def chunk_state(h, lp):
        s = PS[h].astype(f32)
        zero = jnp.zeros_like(s)
        s = s + jnp.where(lp == 1, SR[low_base, h].astype(f32), zero)
        s = s + jnp.where(lp == 2, SR[low_base + 1, h].astype(f32), zero)
        s = s + jnp.where(lp == 3, SR[high_base, h].astype(f32), zero)
        s = s + jnp.where(lp == 4, SR[high_base + 1, h].astype(f32), zero)
        s = s.astype(bf16)
        return jnp.concatenate([s, jnp.zeros((128 - ST, 128), bf16)], axis=0)

    lane_c = lax.broadcasted_iota(jnp.int32, (128, 128), 1)
    low_c = lane_c < 64
    zs = jnp.zeros((12, ST, 128), bf16)
    zh = jnp.zeros((6, ST, 128), bf16)
    rest = pl.ds(pl.multiple_of(6 - core_id * 6, 6), 6)

    @pl.when(c == 0)
    def _():
        SR[3] = zs
        SR[0, rest] = zh
        SR[2, half] = zh
        RR[1, rest] = zh
        RR[2, half] = zh
        RR[3] = zs
        RX[rest] = zh

    @pl.when(c == 1)
    def _():
        RX[...] = zs
        RR[1] = zs

    @pl.when(has_branches)
    def _():
        SR[2] = zs
        SR[3] = zs

    def prior_fwd(tt, _):
        for i in range(4):
            lp = leaf_parent(i)
            rows = pl.ds(i * 128, 128)
            outs = []
            for j in range(3):
                h = tt * 3 + j
                tot = nl[h, rows, :] + dot_nt(qf[h, rows, :], chunk_state(h, lp))
                den = jnp.broadcast_to(tot[:, 64:65], (128, 128))
                a = tot / jnp.maximum(den, 1.0)
                nl[h, rows, :] = jnp.where(low_c, a, den)
                outs.append(a)
            att[tt, rows, 0:128] = jnp.where(low_c, 0.0, pltpu.roll(outs[2], 64, 1)).astype(bf16)
            att[tt, rows, 128:256] = jnp.where(low_c, outs[0], pltpu.roll(outs[1], 64, 1)).astype(bf16)
        return 0

    lax.fori_loop(0, 4, prior_fwd, 0)
    plan.tick(4.5)
    plan.need(gat[0])

    acc[...] = xv[...].astype(f32)
    lt.start()

    def outp(tt, _):
        acc[...] += dot_nt(att[tt], Gv(0, tt, 512, 256))
        return 0

    lax.fori_loop(0, 4, outp, 0)
    plan.need([norm_vectors])
    ng = [NG[i].astype(f32) for i in range(4)]
    r1, r3 = pltpu.roll(ng[1], 64, 1), pltpu.roll(ng[3], 64, 1)
    gains = jnp.concatenate(
        [ng[0][:, :128], ng[0][:, 128:] + r1[:, :128], r1[:, 128:],
         ng[2][:, :128], ng[2][:, 128:] + r3[:, :128], r3[:, 128:]], axis=1)
    gain1, shift1, gain2, shift2 = (gains[i:i + 1] for i in range(4))
    RB_ = 32

    def norm1(i, _):
        rows = pl.ds(pl.multiple_of(i * RB_, RB_), RB_)
        r = acc[rows, :]
        cen = r - jnp.mean(r, axis=1, keepdims=True)
        inv = lax.rsqrt(jnp.mean(cen * cen, axis=1, keepdims=True) + norm_eps)
        nrm = cen * inv
        y = nrm * gain1 + shift1
        n1[rows, :] = nrm
        inv1[rows, :] = jnp.broadcast_to(inv, (RB_, 128))
        acc[rows, :] = y
        nlow[rows, :] = y.astype(bf16)
        return 0

    lax.fori_loop(0, ROWS // RB_, norm1, 0)
    for j in range(3):
        nT[j * 256:(j + 1) * 256, :] = jnp.transpose(nlow[:, j * 256:(j + 1) * 256])

    plan.tick(5.0)
    plan.need(gat[1])

    r2_ = 1.0 / math.sqrt(2.0)

    def ffn_up(tt, _):
        for n in range(3):
            hpre = dot(nlow[...], Gv(1, tt, n * 256, 256))
            cum = 0.5 * (1.0 + lax.erf(hpre * r2_))
            dens = jnp.exp(-0.5 * hpre * hpre) * (1.0 / math.sqrt(2.0 * math.pi))
            act[tt, :, n * 256:(n + 1) * 256] = (hpre * cum).astype(bf16)
            der[tt, :, n * 256:(n + 1) * 256] = (cum + hpre * dens).astype(bf16)
        return 0

    lax.fori_loop(0, 2, ffn_up, 0)
    plan.tick(2.2)
    lax.fori_loop(2, 4, ffn_up, 0)
    plan.tick(2.2)
    plan.need(gat[2])

    def ffn_down(tt, _):
        acc[...] += dot_nt(act[tt], Gv(2, tt, 0, D))
        return 0

    lax.fori_loop(0, 4, ffn_down, 0)
    plan.tick(3.0)

    lt.wait()
    vc = val[0]

    def norm2(i, carry):
        sg, sh, sl = carry
        rows = pl.ds(pl.multiple_of(i * RB_, RB_), RB_)
        r = acc[rows, :]
        cen = r - jnp.mean(r, axis=1, keepdims=True)
        inv = lax.rsqrt(jnp.mean(cen * cen, axis=1, keepdims=True) + norm_eps)
        nrm = cen * inv
        res = nrm * gain2 + shift2
        goal = tv[rows, :].astype(f32)
        lob[rows, :] = res.astype(bf16)
        slot = base_slot + i * RB_ + lax.broadcasted_iota(jnp.int32, (RB_, 1), 0)
        e = jnp.where(slot < vc, res - goal, 0.0)
        sc = e * gain2
        g = inv * (sc - jnp.mean(sc, axis=1, keepdims=True) - nrm * jnp.mean(sc * nrm, axis=1, keepdims=True))
        acc[rows, :] = g
        glow[rows, :] = g.astype(bf16)

        def fold(v):
            return jnp.sum(v.reshape(RB_ // 8, 8, D), axis=0)

        return (sg + fold(e * nrm), sh + fold(e), sl + fold(e * e))

    z8 = jnp.zeros((8, D), f32)
    sg, sh, sl = lax.fori_loop(0, ROWS // RB_, norm2, (z8, z8, z8))
    sm[0:1] = jnp.sum(sg, axis=0, keepdims=True)
    sm[1:2] = jnp.sum(sh, axis=0, keepdims=True)
    sm[2:3] = 0.5 * jnp.sum(sl, axis=0, keepdims=True)
    for j in range(3):
        gT[j * 256:(j + 1) * 256, :] = jnp.transpose(glow[:, j * 256:(j + 1) * 256])

    def rows_of(ti):
        return pl.ds(pl.multiple_of(block_of(ti) * ROWS, ROWS), ROWS)

    lo_l = lcopy(lob, lo_hbm.at[rows_of(t)])
    lo_l.start()
    ticks = [0]

    def step(us):
        plan.tick(us)
        if ticks[0] == OUTPUT_STEP:
            plan.begin(lo_out)
        ticks[0] += 1

    lo_c = send([rcopy(lob, lo_hbm.at[rows_of(t)], CORE)])
    lo_out = Small({YY: [rcopy(lob, lo_hbm.at[rows_of(t)], YY)],
                    CORE: [rcopy(lo_hbm.at[rows_of(t2)], lo_hbm.at[rows_of(t2)], CORE)]}, {YY: 5.3, CORE: 5.3})
    step(5.0)
    lx2.start()

    class Reduce:
        def __init__(self, m, acc4, j, width, order, alloc):
            self.m, self.order, self.acc4 = m, order + (FIN,), acc4
            self.lanes = pl.ds(j * width, width)
            self.stages, self.units, self.share, self.width = {}, {}, width / D, width
            h, sl, fl = None, [0, 1], [f, f1, f2, f3]
            for name in order:
                full = len(fl) == 4
                fs = [slice(None)] if full else fl
                if name == XX:
                    src = [(s, fi, c1) for s in sl for fi in fs]
                    keep = [(s, fi, c) for s in sl for fi in fs]
                    h = c
                elif name == YY:
                    hs = ((0, 1) if full else (slice(None),)) if h is None else (h,)
                    src = [(1, fi, hh) for fi in fs for hh in hs]
                    keep = [(0, fi, hh) for fi in fs for hh in hs]
                    sl = [0]
                else:
                    hh = slice(None) if h is None else h
                    away = (f1, f3) if name == Z0 else (f2,)
                    fl = [f, f2] if name == Z0 else [f]
                    if name == Z0:
                        stay = (f, f2)
                    else:
                        stay = (f,)
                    src = [(s, fi, hh) for s in sl for fi in away]
                    keep = [(s, fi, hh) for s in sl for fi in stay]
                self.stage(name, src, keep, alloc)
            self.fin_dst = alloc(1).at[:, self.lanes]
            self.stages[FIN] = ([rcopy(self.at(0, f, c), self.fin_dst, XX)], None, None)
            self.units[FIN] = self.share

        def at(self, s, fi, h):
            return self.acc4.at[2 + s, fi, h, slice(None), self.lanes]

        def stage(self, name, src, keep, alloc):
            sizes = [4 if isinstance(fi, slice) else 2 if isinstance(h, slice) else 1 for _, fi, h in src]
            dsts = []
            for n in sizes:
                b = alloc(n)
                dsts.append(b.at[:, self.lanes] if n == 1 else b.at[:, :, self.lanes])
            self.units[name] = sum(sizes) * self.share
            cps = rbatch([(self.at(*r), d) for r, d in zip(src, dsts)], name, sum(sizes), self.width)
            self.stages[name] = (cps, dsts, [self.at(*r) for r in keep])

        def go(self, name):
            send(self.stages[name][0])

        def got(self, name):
            cps, dsts, keep = self.stages[name]
            for cp in cps:
                cp.wait()
                done(cp)
            if name == FIN:
                lput(self.at(0, f, c), gout.at[self.m, c, slice(None), self.lanes])
                lput(self.fin_dst, gout.at[self.m, c1, slice(None), self.lanes])
                return
            for p, q in zip(dsts, keep):
                if len(q.shape) == 2:
                    q[...] = q[...] + p[...]
                else:
                    for i in range(q.shape[0]):
                        q[i] = q[i] + p[i]

    puts = []

    def lput(src, dst):
        cp = lcopy(src, dst)
        cp.start()
        puts.append(cp)

    def flat_alloc(ref):
        at = [0]

        def alloc(n):
            i = at[0]
            at[0] += n
            return ref.at[i] if n == 1 else ref.at[pl.ds(i, n)]

        return alloc

    def gather_alloc():
        free = {(a, i, b) for a in (2, 3) for i in range(4) for b in range(2)}
        groups = {
            4: [({(a, i, b) for i in range(4)}, G.at[1, a, :, b]) for a in (2, 3) for b in range(2)],
            2: [({(a, i, 0), (a, i, 1)}, G.at[1, a, i]) for a in (3, 2) for i in range(4)],
            1: [({(a, i, b)}, G.at[1, a, i, b]) for a in (3, 2) for i in range(4) for b in (1, 0)],
        }

        def alloc(n):
            for cells, ref in groups[n]:
                if cells <= free:
                    free.difference_update(cells)
                    return ref
            raise ValueError(n)

        return alloc

    def pieces(m, acc4, orders, alloc_of):
        width = D // len(orders)
        return [Reduce(m, acc4, j, width, order, alloc_of()) for j, order in enumerate(orders)]

    D4, U4, A4 = W4.at[0], W4.at[1], G.at[2]
    coreD = [rcopy(D4.at[j], RC.at[0, j], CORE) for j in range(2)]
    coreU = [rcopy(U4.at[j], RC.at[1, j], CORE) for j in range(2)]
    coreA = [rcopy(A4.at[j], G.at[1, j], CORE) for j in range(2)]
    redD = pieces(2, D4, REDUCE_DOWN, lambda: flat_alloc(RB.at[0]))
    redU = pieces(1, U4, REDUCE_UP, lambda: flat_alloc(RB.at[1]))
    redA = pieces(0, A4, REDUCE_ATTENTION, gather_alloc)

    def add_core(cps, acc4, rc):
        for cp in cps:
            cp.wait()
            done(cp)

        def one(i, _):
            for j in range(2):
                for h in range(2):
                    acc4[2 + j, i, h] = acc4[2 + j, i, h] + rc[j, i, h]
            return 0

        lax.fori_loop(0, 4, one, 0)

    def shard_of(kk):
        return jnp.where(kk == 0, t1, jnp.where(kk == 1, t3, jnp.where(kk == 2, t, t2)))

    def down_grad(kk, _):
        tk = shard_of(kk)
        for n in range(3):
            cols = slice(n * 256, n * 256 + 256)
            D4[kk, :, :, :, cols] = dot(gT[...], act[tk, :, cols]).reshape(4, 2, 96, 256).astype(bf16)
        return 0

    def up_back(kk, _):
        tk = shard_of(kk)

        def blk(n, _):
            n0 = pl.multiple_of(n * 256, 256)
            cols = pl.ds(n0, 256)
            g = (dot(glow[...], Gd(2, tk, n0, 256)) * der[tk, :, cols].astype(f32)).astype(bf16)
            der[tk, :, cols] = g
            U4[kk, :, :, :, cols] = dot(nT[...], g).reshape(4, 2, 96, 256).astype(bf16)
            return 0

        lax.fori_loop(0, 3, blk, 0)
        acc[...] += dot_nt(der[tk], Gv(1, tk, 0, D))
        return 0

    lax.fori_loop(0, 2, down_grad, 0)
    send(coreD)
    lax.fori_loop(2, 4, down_grad, 0)
    add_core(coreD, D4, RC.at[0])
    step(3.0)
    step(3.0)
    for r in redD:
        plan.begin(r)
    lax.fori_loop(0, 2, up_back, 0)
    send(coreU)
    step(7.0)
    lax.fori_loop(2, 4, up_back, 0)
    step(7.0)
    add_core(coreU, U4, RC.at[1])
    for r in redU:
        plan.begin(r)

    def norm1b(i, carry):
        sg, sh = carry
        rows = pl.ds(pl.multiple_of(i * RB_, RB_), RB_)
        e = acc[rows, :]
        nrm = n1[rows, :]
        inv = inv1[rows, 0:1]
        sc = e * gain1
        g = inv * (sc - jnp.mean(sc, axis=1, keepdims=True) - nrm * jnp.mean(sc * nrm, axis=1, keepdims=True))
        acc[rows, :] = g
        glow[rows, :] = g.astype(bf16)

        def fold(v):
            return jnp.sum(v.reshape(RB_ // 8, 8, D), axis=0)

        return (sg + fold(e * nrm), sh + fold(e))

    sg, sh = lax.fori_loop(0, ROWS // RB_, norm1b, (z8, z8))
    sm[3:4] = jnp.sum(sg, axis=0, keepdims=True)
    sm[4:5] = jnp.sum(sh, axis=0, keepdims=True)
    sm[5:8] = jnp.zeros((3, D), f32)
    for j in range(3):
        gT[j * 256:(j + 1) * 256, :] = jnp.transpose(glow[:, j * 256:(j + 1) * 256])

    lx2.wait()
    for j in range(3):
        xT[j * 256:(j + 1) * 256, :] = jnp.transpose(nlow[:, j * 256:(j + 1) * 256])
    step(3.0)

    links = (CORE, YY, XX, Z0, Z1)

    def sums_step(d, arrived):
        i = 2 * links.index(d)
        if arrived:
            sm[...] = sm[...] + smr[i + 1]
        else:
            smr[i] = sm[...]

    sums = Small({d: [rcopy(smr.at[2 * i], smr.at[2 * i + 1], d)] for i, d in enumerate(links)},
                 dict.fromkeys(links, 0.17), sums_step)

    for g in gat[1] + gat[2]:
        for cps in g.stages.values():
            for cp in cps:
                cp.wait_send()
                done(cp)
    plan.begin(sums)

    def gn_rows(tt, _):
        gae = dot(glow[...], G[0, tt, :, :, :, 512:768].reshape(D, 256)).astype(bf16).astype(f32)
        g2_ = pltpu.roll(gae[:, 0:128], 64, 1)
        g0_ = gae[:, 128:256]
        g1_ = pltpu.roll(g0_, 64, 1)
        for j, g in enumerate((g0_, g1_, g2_)):
            h = tt * 3 + j
            v = nl[h]
            g = jnp.where(low_half, g, 0.0)
            den = jnp.broadcast_to(v[:, 64:65], (ROWS, 128))
            safe = jnp.maximum(den, 1.0)
            s = jnp.sum(g * jnp.where(low_half, v, 0.0), axis=1, keepdims=True)
            gd_ = jnp.where(den > 1.0, -s / safe, 0.0)
            gn = jnp.where(low_half, g / safe, jnp.where(lane == 64, gd_, 0.0))
            nl[h] = gn
            gnT = jnp.transpose(gn).astype(bf16)
            parts = [dot(gnT[:ST, i * 128:(i + 1) * 128], qf[h, i * 128:(i + 1) * 128, :]) for i in range(4)]
            dE[2, h] = (parts[0] + parts[1] + parts[2] + parts[3]).astype(bf16)
            near = jnp.where(t < 2, 1, 3)
            away = jnp.where(t < 2, 3, 1)
            for slot, b in ((0, away), (1, away + 1), (3, near), (4, near + 1)):
                tot = jnp.zeros((ST, 128), f32)
                for i in range(4):
                    tot = tot + jnp.where(leaf_parent(i) == b, parts[i], 0.0)
                dE[slot, h] = tot.astype(bf16)
        return 0

    if HOLD_BACKWARD == 1:
        plan.hold()
    lax.fori_loop(0, 2, gn_rows, 0)
    step(4.2)
    if HOLD_BACKWARD == 2:
        plan.hold()
    lax.fori_loop(2, 4, gn_rows, 0)
    step(4.2)

    bc = [rcopy(dE.at[2], RR.at[0], CORE)]
    bx1 = [rcopy(dE.at[2, half], RX.at[half], XX)]
    by1 = [rcopy(dE.at[pl.ds(0, 2)], RR.at[pl.ds(2, 2)], YY)]
    bn1 = [rcopy(dE.at[pl.ds(3, 2)], RR.at[pl.ds(2, 2)], CORE)]
    by0 = [rcopy(TTb.at[half], RR.at[1, half], YY)]
    bo0 = [rcopy(dE.at[3, half], RR.at[2, half], CORE)]
    start(bc)

    @pl.when(has_leaves)
    def _():
        start(by1)

    dq = act

    def pair(y, feat):
        y = y * cs[...]
        fc = feat.astype(f32)
        fc = jnp.where(low_half, fc, pltpu.roll(fc, 64, 1))
        return jnp.where(fc > 0.0, y + pltpu.roll(y, 64, 1), 0.0).astype(bf16)

    def bwd_q(tt, _):
        for j in range(3):
            h = tt * 3 + j
            gn = nl[h].astype(bf16)
            dw = dot_nt(gn, vx[h]).astype(bf16) * mk[...]
            pri = [dot(gn[i * 128:(i + 1) * 128, :], chunk_state(h, leaf_parent(i))) for i in range(4)]
            gq = pair(dot(dw, kf[h]) + jnp.concatenate(pri, axis=0), qf[h])
            if j == 0:
                dq[tt, :, 0:64] = gq[:, 0:64]
            elif j == 1:
                dq[tt, :, 64:128] = gq[:, 64:128]
            else:
                dq[tt, :, 384:448] = gq[:, 0:64]
        return 0

    lax.fori_loop(0, 1, bwd_q, 0)
    step(1.8)

    for cp in bc:
        cp.wait()

    @pl.when(c == 1)
    def _():
        def addup(h):
            dE[2, h] = dE[2, h] + RR[0, h]

        each_half(addup)
        start(bx1)

    if HOLD_BACKWARD == 0:
        plan.hold()
    due = plan.load(XX, 0.85)
    units_due = plan.load(YY, 1.7)
    lax.fori_loop(1, 4, bwd_q, 0)
    step(5.3)
    plan.gate(max(due, plan.now))

    @pl.when(c == 0)
    def _():
        wait_recv(bx1)

        def message(h):
            zero = jnp.zeros((ST, 128), f32)
            later = dE[2, h].astype(f32) + RR[0, h].astype(f32)
            TTb[h] = (jnp.where(t >= 2, later, zero) + RX[h].astype(f32)).astype(bf16)

        each_half(message)
        start(by0)

    due = plan.load(YY, 0.85)
    plan.release()

    def out_grad(kk, _):
        tt = shard_of(kk)
        v = dot(gT[...], att[tt])
        A4[kk, :, :, :, 512:768] = v.reshape(4, 2, 96, 256).astype(bf16)
        return 0

    lax.fori_loop(0, 4, out_grad, 0)
    step(2.0)
    plan.gate(max(due, units_due, plan.now))

    @pl.when(c == 0)
    def _():
        for cp in by0:
            cp.wait()

        def common(h):
            dE[3, h] = (RX[h].astype(f32) + RR[1, h].astype(f32)).astype(bf16)

        each_half(common)
        start(bo0)
        for cp in bo0:
            cp.wait()

    @pl.when(c == 1)
    def _():
        for cp in bx1:
            cp.wait_send()

    @pl.when(has_leaves)
    def _():
        for cp in by1:
            cp.wait()

        def meet(h, _):
            dE[3, h] = dE[3, h] + RR[2, h]
            dE[4, h] = dE[4, h] + RR[3, h]
            return 0

        lax.fori_loop(0, 12, meet, 0)
        start(bn1)
        for cp in bn1:
            cp.wait_send()

    @pl.when(has_branches)
    def _():
        wait_recv(bn1)

    step(1.5)

    def later_states(h):
        zero = jnp.zeros((ST, 128), f32)
        shared = jnp.where(h // 6 == core_id, dE[3, h].astype(f32), RR[2, h].astype(f32))
        d = jnp.where(t1 > t, RR[0, h].astype(f32), zero) + shared
        pad = jnp.zeros((128 - ST, 128), bf16)
        out = []
        for u in range(2):
            b = jnp.where(has_branches, RR[2 + u, h].astype(f32), zero)
            out.append(jnp.concatenate([jnp.where(c == 0, d, b).astype(bf16), pad], axis=0))
        return out

    def bwd_kv(kk, _):
        tt = shard_of(kk)
        for j in range(3):
            h = tt * 3 + j
            gn = nl[h].astype(bf16)
            ds = later_states(h)
            wT = dot_nt(kf[h], qf[h]).astype(bf16) * mkT[...]
            dv = dot(wT, gn) + jnp.concatenate(
                [dot_nt(kf[h, u * 256:(u + 1) * 256, :], ds[u]) for u in range(2)], axis=0)
            dwT = dot_nt(vx[h], gn).astype(bf16) * mkT[...]
            dk = dot(dwT, qf[h]) + jnp.concatenate(
                [dot(vx[h, u * 256:(u + 1) * 256, :], ds[u]) for u in range(2)], axis=0)
            gk = pair(dk, kf[h])
            if j == 0:
                dq[tt, :, 128:192] = gk[:, 0:64]
                dq[tt, :, 256:320] = dv[:, 0:64].astype(bf16)
            elif j == 1:
                dq[tt, :, 192:256] = gk[:, 64:128]
                dq[tt, :, 320:384] = pltpu.roll(dv, 64, 1)[:, 64:128].astype(bf16)
            else:
                dq[tt, :, 448:512] = gk[:, 64:128]
                dq[tt, :, 512:640] = jnp.where(low_half, dv, 0.0).astype(bf16)

        def put(l0, n, v):
            A4[kk, :, :, :, l0:l0 + n] = v.reshape(4, 2, 96, n).astype(bf16)

        put(0, 256, dot(xT[...], dq[tt, :, 0:256]))
        put(256, 256, dot(xT[...], dq[tt, :, 256:512]))
        o2 = A4[kk, :, :, :, 512:640].reshape(D, 128).astype(f32)
        put(512, 128, dot(xT[...], dq[tt, :, 512:640]) + o2)
        return 0

    for p in range(2):
        lax.fori_loop(2 * p, 2 * p + 2, bwd_kv, 0)
        step(5.8)
        if p == 0:
            plan.need([sums])
            send(coreA)
    add_core(coreA, A4, G.at[1])
    for r in redA:
        plan.begin(r)

    if ticks[0] <= OUTPUT_STEP:
        plan.begin(lo_out)
    def inback(tt, _):
        acc[...] += dot_nt(dq[tt, :, 0:640], Gv(0, tt, 0, 640))
        return 0

    lax.fori_loop(0, 4, inback, 0)
    igb[...] = acc[...].astype(bf16)
    ig_l = lcopy(igb, ig_hbm.at[rows_of(t)])
    ig_l.start()
    ig_c = send([rcopy(igb, ig_hbm.at[rows_of(t)], CORE)])

    def ig_step(stage, arrived):
        if stage == YY and arrived:
            lput(der.at[0], ig_hbm.at[rows_of(t2)])

    ig_out = Small({YY: [rcopy(igb, der.at[0], YY)],
                    CORE: [rcopy(der.at[0], ig_hbm.at[rows_of(t2)], CORE)]}, {YY: 5.3, CORE: 5.3}, ig_step)
    plan.tick(4.5)
    plan.begin(ig_out)
    plan.need(redD + redU + redA + [lo_out, ig_out])
    small[...] = sm[...]
    wait_recv(lo_c + ig_c)
    for cp in pending:
        cp.wait_send()
    for cp in puts + [lo_l, ig_l]:
        cp.wait()
    assert counter[0] <= N_REMOTE and lcounter[0] <= N_LOCAL, (counter, lcounter)


N_REMOTE, N_LOCAL = 168, 40


def fast_shards(layer_input, teacher, query_weight, key_weight, value_weight, out_weight, up_weight,
                down_weight, first_gain, first_shift, second_gain, second_shift, parents, valid_count):
    f = lax.axis_index(FSDP)
    D = layer_input.shape[-1]
    sc = layer_input.shape[1]
    tree_len = sc * lax.axis_size(CONTEXT)
    bf16, f32 = jnp.bfloat16, jnp.float32
    V = pltpu.VMEM
    scratch = [
        V((3, 4, 4, 2, 96, D), bf16),
        V((4, 16, 256), bf16),
        V((ROWS, D), bf16),
        V((12, ROWS, 128), bf16),
        V((12, ROWS, 128), bf16),
        V((12, ROWS, 128), bf16),
        V((ROWS, ROWS), bf16),
        V((ROWS, ROWS), bf16),
        V((ROWS, 128), f32),
        V((12, ROWS, 128), f32),
        V((4, ROWS, 256), bf16),
        V((ROWS, D), f32),
        V((ROWS, 128), f32),
        V((ROWS, D), bf16),
        V((4, ROWS, D), bf16),
        V((4, ROWS, D), bf16),
        V((ROWS, D), f32),
        V((ROWS, D), bf16),
        V((D, ROWS), bf16),
        V((D, ROWS), bf16),
        V((4, 12, ST, 128), bf16),
        V((12, ST, 128), bf16),
        V((12, ST, 128), bf16),
        V((4, 12, ST, 128), bf16),
        V((5, 12, ST, 128), bf16),
        V((12, ST, 128), bf16),
        V((2, 4, 4, 2, 96, D), bf16),
        V((2, 2, 4, 2, 96, D), bf16),
        V((2, 16, 96, D), bf16),
        V((8, D), f32),
        V((10, 8, D), f32),
        pltpu.SemaphoreType.DMA((N_REMOTE,)),
        pltpu.SemaphoreType.DMA((N_REMOTE,)),
        pltpu.SemaphoreType.DMA((N_LOCAL,)),
    ]
    any_, smem, vmem = (pl.BlockSpec(memory_space=s) for s in (pl.ANY, pltpu.SMEM, pltpu.VMEM))
    lo, ig, gout, small = pl.pallas_call(
        functools.partial(fast_kernel, tree_len=tree_len),
        out_shape=[
            jax.ShapeDtypeStruct((sc, D), bf16),
            jax.ShapeDtypeStruct((sc, D), bf16),
            jax.ShapeDtypeStruct((3, 2, 96, D), bf16),
            jax.ShapeDtypeStruct((8, D), f32),
        ],
        in_specs=[any_, any_, vmem, vmem, vmem, vmem, any_, any_, vmem, vmem, vmem, vmem, smem, smem],
        out_specs=[any_, any_, any_, vmem],
        scratch_shapes=scratch,
        compiler_params=pltpu.CompilerParams(
            collective_id=0, has_side_effects=True, vmem_limit_bytes=67043328),
        name="tree_layer",
    )(layer_input, teacher, query_weight, key_weight, value_weight, out_weight, up_weight.reshape(2, 96, D),
      down_weight.T.reshape(2, 96, D), first_gain, first_shift, second_gain, second_shift, parents, valid_count)
    sq, wide, vec = (jax.ShapeDtypeStruct(n, f32) for n in ((192, 192), (192, D), (192,)))

    def whole(a):
        return pl.BlockSpec(a.shape, lambda i: (0,) * len(a.shape))

    outs = pl.pallas_call(
        unpack_kernel,
        grid=(4,),
        in_specs=[whole(gout), whole(small), pl.BlockSpec((ROWS, D), lambda i: (i, 0))],
        out_specs=[whole(a) for a in (sq, sq, sq, sq, wide, wide, vec, vec, vec, vec)]
        + [pl.BlockSpec((1, 1), lambda i: (0, 0)), pl.BlockSpec((ROWS, D), lambda i: (i, 0))],
        out_shape=[sq, sq, sq, sq, wide, wide, vec, vec, vec, vec,
                   jax.ShapeDtypeStruct((1, 1), f32), jax.ShapeDtypeStruct((sc, D), f32)],
        name="unpack",
    )(gout, small, ig)
    q_g, k_g, v_g, o_g, up_g, down_t, g1_g, s1_g, g2_g, s2_g, loss, ig_wide = outs
    return (lo[None], ig_wide[None], loss.reshape(()), q_g, k_g, v_g, o_g, up_g, down_t.T,
            g1_g, s1_g, g2_g, s2_g)


def unpack_kernel(gout, small, ig, q_g, k_g, v_g, o_g, up_g, down_t, g1_g, s1_g, g2_g, s2_g, loss, ig_wide):
    f32 = jnp.float32
    ig_wide[...] = ig[...].astype(f32)

    @pl.when(pl.program_id(0) == 0)
    def _():
        a = gout[0].reshape(192, 768).astype(f32)
        q_g[:, 0:128] = a[:, 0:128]
        q_g[:, 128:192] = a[:, 384:448]
        k_g[:, 0:128] = a[:, 128:256]
        k_g[:, 128:192] = pltpu.roll(a[:, 384:512], 64, 1)[:, 0:64]
        v_g[:, 0:128] = a[:, 256:384]
        v_g[:, 128:192] = a[:, 512:576]
        o_t = jnp.concatenate([a[:, 640:768], pltpu.roll(a[:, 512:640], 64, 1)], axis=1)
        o_g[...] = jnp.transpose(o_t)[0:192, :]
        up_g[...] = gout[1].reshape(192, 768).astype(f32)
        down_t[...] = gout[2].reshape(192, 768).astype(f32)
        f = lax.axis_index(FSDP)
        total = small[...]
        mine = jnp.where(f == 0, total[:, 0:256], total[:, 384:640])
        odd = jnp.where(f == 1, total[:, 128:384], total[:, 512:768])
        mine = jnp.where(f - 2 * (f // 2) == 1, pltpu.roll(odd, 192, 1), mine)[:, 0:192]
        for i, out in ((3, g1_g), (4, s1_g), (0, g2_g), (1, s2_g)):
            out[...] = mine[i]
        loss[...] = jnp.sum(total[2:3], axis=1, keepdims=True)


def shards(*arrays):
    tree_count, slot_count, width = arrays[0].shape
    sizes = tuple(lax.axis_size(n) for n in (FSDP, CONTEXT, TENSOR))
    if (tree_count, slot_count, width) == (1, 2048, 768) and sizes == (4, 2, 4) and arrays[6].shape == (192, 768):
        return fast_shards(*arrays)
    return general_shards(*arrays)


def solution(mesh):
    return jax.shard_map(
        shards,
        mesh=mesh,
        in_specs=(
            P(FSDP, CONTEXT, None),
            P(FSDP, CONTEXT, None),
            P(FSDP, TENSOR),
            P(FSDP, TENSOR),
            P(FSDP, TENSOR),
            P(TENSOR, FSDP),
            P(FSDP, TENSOR),
            P(TENSOR, FSDP),
            P(FSDP),
            P(FSDP),
            P(FSDP),
            P(FSDP),
            P(FSDP, None),
            P(FSDP),
        ),
        out_specs=(
            P(FSDP, CONTEXT, None),
            P(FSDP, CONTEXT, None),
            P(),
            P(FSDP, TENSOR),
            P(FSDP, TENSOR),
            P(FSDP, TENSOR),
            P(TENSOR, FSDP),
            P(FSDP, TENSOR),
            P(TENSOR, FSDP),
            P(FSDP),
            P(FSDP),
            P(FSDP),
            P(FSDP),
        ),
        check_vma=False,
    )
```

```python
import functools
import math

import jax
import jax.numpy as jnp
from jax import lax
from jax.experimental import pallas as pl
from jax.experimental.pallas import tpu as pltpu
from jax.sharding import PartitionSpec as P

HEAD_DIM = 64


precise = lax.Precision.HIGHEST
norm_eps = 1e-05


def carried_in(array, axis, combine, identity):
    count, here = (lax.axis_size(axis), lax.axis_index(axis))
    everything = jax.tree.map(
        lambda part, kind: lax.all_gather(part.astype(kind), axis),
        array,
        (jnp.bfloat16, jnp.bfloat16),
    )
    start = jax.tree.map(
        lambda part, zero: jnp.broadcast_to(jnp.asarray(zero, part.dtype), part.shape),
        array,
        identity,
    )

    def carried_turn(k, before):
        reached = k < here
        new = combine(
            before, jax.tree.map(lambda part, own: part[k].astype(own.dtype), everything, array)
        )
        return jax.tree.map(lambda a, b: jnp.where(reached, a, b), new, before)

    return lax.fori_loop(0, count, carried_turn, start)


def entering(array, axis, combine, identity):
    count, here = (lax.axis_size(axis), lax.axis_index(axis))
    everything = jax.tree.map(
        lambda part, kind: lax.all_gather(part.astype(kind), axis),
        array,
        jax.tree.map(lambda a: jnp.bfloat16 if a.dtype == jnp.float32 else a.dtype, array),
    )
    start = jax.tree.map(
        lambda part, zero: jnp.broadcast_to(jnp.asarray(zero, part.dtype), part.shape),
        array,
        identity,
    )

    def entering_turn(k, before):
        at = count - 1 - k
        reached = at > here
        new = combine(
            before, jax.tree.map(lambda part, own: part[at].astype(own.dtype), everything, array)
        )
        return jax.tree.map(lambda a, b: jnp.where(reached, a, b), new, before)

    return lax.fori_loop(0, count, entering_turn, start)


def layout_of(slot_ids, parents_row, tree_len):
    half_len = tree_len // 2
    branch_len = tree_len // 16
    leaf_len = tree_len // 32
    leaf_start = half_len + 4 * branch_len
    in_branch = (slot_ids >= half_len) & (slot_ids < leaf_start)
    in_leaf = slot_ids >= leaf_start
    branch_index = jnp.clip((slot_ids - half_len) // branch_len, 0, 3)
    leaf_index = jnp.clip((slot_ids - leaf_start) // leaf_len, 0, 7)
    leaf_ids = jnp.arange(8, dtype=jnp.int32)
    leaf_parent = jnp.sum(
        jnp.where(leaf_index[:, None] == leaf_ids[None, :], parents_row[None, :], 0), axis=1
    )
    segment = jnp.where(in_leaf, 5 + leaf_index, jnp.where(in_branch, 1 + branch_index, 0))
    owner_branch = jnp.where(in_leaf, leaf_parent, jnp.where(in_branch, 1 + branch_index, 0))
    leaf_pos = (
        half_len
        + jnp.where(leaf_parent > 0, branch_len, 0)
        + slot_ids
        - leaf_start
        - leaf_index * leaf_len
    )
    branch_pos = slot_ids - branch_index * branch_len
    position = jnp.where(in_leaf, leaf_pos, jnp.where(in_branch, branch_pos, slot_ids))
    phase_angle = (
        0.5 * math.pi * position.astype(jnp.float32) / float(half_len + branch_len + leaf_len)
    )
    return (segment, owner_branch, phase_angle)


def features(pre_act, phase_angle):
    rectified = jnp.maximum(pre_act, 0.0)
    cosine = jnp.cos(phase_angle)[..., None, None]
    sine_part = jnp.sin(phase_angle)[..., None, None]
    return jnp.concatenate([rectified * cosine, rectified * sine_part], axis=-1)


def features_back(grad_feat, pre_act, phase_angle):
    half_dim = pre_act.shape[-1]
    cosine = jnp.cos(phase_angle)[..., None, None]
    sine_part = jnp.sin(phase_angle)[..., None, None]
    combined = grad_feat[..., :half_dim] * cosine + grad_feat[..., half_dim:] * sine_part
    return jnp.where(pre_act > 0.0, combined, 0.0)


def norm_forward(resid, gain_vec, shift_vec):
    row_mean = jnp.mean(resid, axis=-1, keepdims=True)
    centered = resid - row_mean
    inv_std = lax.rsqrt(jnp.mean(centered * centered, axis=-1, keepdims=True) + norm_eps)
    normal = centered * inv_std
    return (normal * gain_vec + shift_vec, normal, inv_std)


def norm_backward(grad_out, normal, inv_std, gain_vec):
    scaled = grad_out * gain_vec
    grad_in = inv_std * (
        scaled
        - jnp.mean(scaled, axis=-1, keepdims=True)
        - normal * jnp.mean(scaled * normal, axis=-1, keepdims=True)
    )
    return (grad_in, jnp.sum(grad_out * normal, axis=0), jnp.sum(grad_out, axis=0))


def add_pair(earlier, later):
    return (earlier[0] + later[0], earlier[1] + later[1])


def general_shards(
    layer_input,
    teacher,
    query_weight,
    key_weight,
    value_weight,
    out_weight,
    up_weight,
    down_weight,
    first_gain,
    first_shift,
    second_gain,
    second_shift,
    parents,
    valid_count,
):
    tree_count, slot_count, model_width = layer_input.shape
    ctx_size = lax.axis_size(CONTEXT)
    ctx_index = lax.axis_index(CONTEXT)
    tree_len = slot_count * ctx_size
    row_count = tree_count * slot_count
    (
        full_query,
        full_key,
        full_value,
        full_out,
        full_up,
        full_down,
        gain_one,
        shift_one,
        gain_two,
        shift_two,
    ) = (
        lax.all_gather(query_weight, FSDP, axis=0, tiled=True),
        lax.all_gather(key_weight, FSDP, axis=0, tiled=True),
        lax.all_gather(value_weight, FSDP, axis=0, tiled=True),
        lax.all_gather(out_weight, FSDP, axis=1, tiled=True),
        lax.all_gather(up_weight, FSDP, axis=0, tiled=True),
        lax.all_gather(down_weight, FSDP, axis=1, tiled=True),
        lax.all_gather(first_gain, FSDP, axis=0, tiled=True),
        lax.all_gather(first_shift, FSDP, axis=0, tiled=True),
        lax.all_gather(second_gain, FSDP, axis=0, tiled=True),
        lax.all_gather(second_shift, FSDP, axis=0, tiled=True),
    )
    gain_one = gain_one.astype(jnp.float32)
    shift_one = shift_one.astype(jnp.float32)
    gain_two = gain_two.astype(jnp.float32)
    shift_two = shift_two.astype(jnp.float32)
    head_local = full_query.shape[1] // HEAD_DIM
    flat_in = layer_input.reshape(row_count, model_width)
    slot_ids = ctx_index * slot_count + jnp.arange(slot_count, dtype=jnp.int32)

    def layout_here(parents_row):
        return layout_of(slot_ids, parents_row, tree_len)

    segment, owner_branch, phase_angle = jax.vmap(layout_here)(parents)

    def project(weight):
        return jnp.dot(flat_in, weight, preferred_element_type=jnp.float32).reshape(
            tree_count, slot_count, head_local, HEAD_DIM
        )

    query_pre = project(full_query)
    key_pre = project(full_key)
    values = project(full_value).astype(jnp.bfloat16)
    query_feat = features(query_pre, phase_angle).astype(jnp.bfloat16)
    key_feat = features(key_pre, phase_angle).astype(jnp.bfloat16)
    query_wide = query_feat.astype(jnp.float32)
    key_wide = key_feat.astype(jnp.float32)
    value_wide = values.astype(jnp.float32)
    state_ids = jnp.arange(5, dtype=jnp.int32)
    segment_hit = segment[:, :, None] == state_ids
    in_segment = segment_hit.astype(jnp.float32)
    selected = ((state_ids == 0) | (owner_branch[:, :, None] == state_ids)).astype(jnp.float32)
    masked_key = jnp.where(
        segment_hit[:, :, :, None, None], key_feat[:, :, None], jnp.zeros((), jnp.bfloat16)
    )
    contrib_state = jnp.einsum(
        "tsahf,tshd->tahfd", masked_key, values, preferred_element_type=jnp.float32
    )
    contrib_norm = jnp.einsum(
        "tsa,tshf->tahf",
        segment_hit.astype(jnp.bfloat16),
        key_feat,
        preferred_element_type=jnp.float32,
    )
    zero_state = jnp.zeros_like(contrib_state)
    zero_norm = jnp.zeros_like(contrib_norm)
    prior_state, prior_norm = carried_in(
        (contrib_state, contrib_norm), CONTEXT, add_pair, (zero_state, zero_norm)
    )
    in_numer = jnp.einsum(
        "tsa,tshf,tahfd->tshd", selected, query_wide, prior_state, precision=precise
    )
    in_denom = jnp.einsum("tsa,tshf,tahf->tsh", selected, query_wide, prior_norm, precision=precise)
    block_rows = min(slot_count, 512)
    block_count = slot_count // block_rows

    def block_scores(block_index):
        row_start = block_index * block_rows
        query_rows = lax.dynamic_slice_in_dim(query_feat, row_start, block_rows, 1)
        slot_rows = lax.dynamic_slice_in_dim(slot_ids, row_start, block_rows, 0)
        segment_rows = lax.dynamic_slice_in_dim(segment, row_start, block_rows, 1)
        owner_rows = lax.dynamic_slice_in_dim(owner_branch, row_start, block_rows, 1)
        allowed = (slot_ids[None, None, :] <= slot_rows[None, :, None]) & (
            (segment[:, None, :] == segment_rows[:, :, None])
            | (segment[:, None, :] == 0)
            | (segment[:, None, :] == owner_rows[:, :, None])
        )
        allowed_wide = allowed[:, None].astype(jnp.float32)
        scores = (
            jnp.einsum("tihf,tjhf->thij", query_rows, key_feat, preferred_element_type=jnp.float32)
            * allowed_wide
        )
        return (scores, allowed_wide, query_rows)

    def local_forward(block_index):
        scores, allowed_wide, query_rows = block_scores(block_index)
        numerator = jnp.einsum("thij,tjhd->tihd", scores, value_wide, precision=precise)
        denominator = jnp.transpose(jnp.sum(scores, axis=3), (0, 2, 1))
        return (numerator, denominator)

    local_numer, local_denom = lax.map(local_forward, jnp.arange(block_count, dtype=jnp.int32))

    def unblock(stacked):
        return jnp.moveaxis(stacked, 0, 1).reshape((tree_count, slot_count) + stacked.shape[3:])

    numerator = unblock(local_numer) + in_numer
    denominator = unblock(local_denom) + in_denom
    safe_denom = jnp.maximum(denominator, 1.0)
    attended = numerator / safe_denom[..., None]
    attended_low = attended.astype(jnp.bfloat16).reshape(row_count, head_local * HEAD_DIM)
    attention_part = jnp.dot(attended_low, full_out, preferred_element_type=jnp.float32)
    attention_sum = lax.psum(attention_part.astype(jnp.bfloat16), TENSOR).astype(jnp.float32)
    resid_one = flat_in.astype(jnp.float32) + attention_sum
    normed_one, normal_one, inv_one = norm_forward(resid_one, gain_one, shift_one)
    normed_low = normed_one.astype(jnp.bfloat16)
    hidden_pre = jnp.dot(normed_low, full_up, preferred_element_type=jnp.float32)
    activated = jax.nn.gelu(hidden_pre, approximate=False).astype(jnp.bfloat16)
    ffn_part = jnp.dot(activated, full_down, preferred_element_type=jnp.float32)
    ffn_sum = lax.psum(ffn_part.astype(jnp.bfloat16), TENSOR).astype(jnp.float32)
    resid_two = normed_one + ffn_sum
    result, normal_two, inv_two = norm_forward(resid_two, gain_two, shift_two)
    layer_output = result.astype(jnp.bfloat16).reshape(tree_count, slot_count, model_width)
    valid_rows = (
        (slot_ids[None, :] < valid_count[:, None]).astype(jnp.float32).reshape(row_count, 1)
    )
    residual = (result - teacher.reshape(row_count, model_width).astype(jnp.float32)) * valid_rows
    loss_value = lax.psum(0.5 * jnp.sum(residual * residual), (FSDP, CONTEXT))
    grad_resid_two, second_gain_part, second_shift_part = norm_backward(
        residual, normal_two, inv_two, gain_two
    )
    grad_two_low = grad_resid_two.astype(jnp.bfloat16)
    down_part = jnp.dot(activated.T, grad_two_low, preferred_element_type=jnp.float32)
    grad_act = jnp.dot(grad_two_low, full_down.T, preferred_element_type=jnp.float32)
    cumulative = 0.5 * (1.0 + jax.scipy.special.erf(hidden_pre / math.sqrt(2.0)))
    density = jnp.exp(-0.5 * hidden_pre * hidden_pre) / math.sqrt(2.0 * math.pi)
    grad_pre = (grad_act * (cumulative + hidden_pre * density)).astype(jnp.bfloat16)
    up_part = jnp.dot(normed_low.T, grad_pre, preferred_element_type=jnp.float32)
    ffn_back = jnp.dot(grad_pre, full_up.T, preferred_element_type=jnp.float32)
    grad_normed_one = grad_resid_two + lax.psum(ffn_back.astype(jnp.bfloat16), TENSOR).astype(
        jnp.float32
    )
    grad_resid_one, first_gain_part, first_shift_part = norm_backward(
        grad_normed_one, normal_one, inv_one, gain_one
    )
    grad_one_low = grad_resid_one.astype(jnp.bfloat16)
    out_part = jnp.dot(attended_low.T, grad_one_low, preferred_element_type=jnp.float32)
    grad_attended = jnp.dot(grad_one_low, full_out.T, preferred_element_type=jnp.float32).astype(
        jnp.bfloat16
    )
    grad_attended = grad_attended.astype(jnp.float32).reshape(
        tree_count, slot_count, head_local, HEAD_DIM
    )
    grad_numer = grad_attended / safe_denom[..., None]
    grad_denom = jnp.where(
        denominator > 1.0, -jnp.sum(grad_attended * attended, axis=-1) / safe_denom, 0.0
    )
    grad_query = jnp.einsum(
        "tsa,tshd,tahfd->tshf", selected, grad_numer, prior_state, precision=precise
    ) + jnp.einsum("tsa,tsh,tahf->tshf", selected, grad_denom, prior_norm, precision=precise)
    grad_prior_state = jnp.einsum(
        "tsa,tshf,tshd->tahfd", selected, query_wide, grad_numer, precision=precise
    )
    grad_prior_norm = jnp.einsum(
        "tsa,tshf,tsh->tahf", selected, query_wide, grad_denom, precision=precise
    )
    grad_contrib_state, grad_contrib_norm = entering(
        (grad_prior_state, grad_prior_norm), CONTEXT, add_pair, (zero_state, zero_norm)
    )
    grad_key = jnp.einsum(
        "tsa,tshd,tahfd->tshf", in_segment, value_wide, grad_contrib_state, precision=precise
    ) + jnp.einsum("tsa,tahf->tshf", in_segment, grad_contrib_norm, precision=precise)
    grad_value = jnp.einsum(
        "tsa,tshf,tahfd->tshd", in_segment, key_wide, grad_contrib_state, precision=precise
    )

    def local_backward(carried, block_index):
        acc_key, acc_value = carried
        scores, allowed_wide, query_rows = block_scores(block_index)
        row_start = block_index * block_rows
        numer_rows = lax.dynamic_slice_in_dim(grad_numer, row_start, block_rows, 1)
        denom_rows = lax.dynamic_slice_in_dim(grad_denom, row_start, block_rows, 1)
        grad_scores = (
            jnp.einsum("tihd,tjhd->thij", numer_rows, value_wide, precision=precise)
            + jnp.transpose(denom_rows, (0, 2, 1))[:, :, :, None]
        ) * allowed_wide
        rows_grad = jnp.einsum("thij,tjhf->tihf", grad_scores, key_wide, precision=precise)
        acc_key = acc_key + jnp.einsum(
            "thij,tihf->tjhf", grad_scores, query_rows.astype(jnp.float32), precision=precise
        )
        acc_value = acc_value + jnp.einsum("thij,tihd->tjhd", scores, numer_rows, precision=precise)
        return ((acc_key, acc_value), rows_grad)

    (local_key, local_value), local_query = lax.scan(
        local_backward,
        (jnp.zeros_like(key_wide), jnp.zeros_like(value_wide)),
        jnp.arange(block_count, dtype=jnp.int32),
    )
    grad_query = grad_query + unblock(local_query)
    grad_key = grad_key + local_key
    grad_value = grad_value + local_value
    grad_query_low = (
        features_back(grad_query, query_pre, phase_angle)
        .astype(jnp.bfloat16)
        .reshape(row_count, -1)
    )
    grad_key_low = (
        features_back(grad_key, key_pre, phase_angle).astype(jnp.bfloat16).reshape(row_count, -1)
    )
    grad_value_low = grad_value.astype(jnp.bfloat16).reshape(row_count, -1)
    query_part = jnp.dot(flat_in.T, grad_query_low, preferred_element_type=jnp.float32)
    key_part = jnp.dot(flat_in.T, grad_key_low, preferred_element_type=jnp.float32)
    value_part = jnp.dot(flat_in.T, grad_value_low, preferred_element_type=jnp.float32)
    input_back = (
        jnp.dot(grad_query_low, full_query.T, preferred_element_type=jnp.float32)
        + jnp.dot(grad_key_low, full_key.T, preferred_element_type=jnp.float32)
        + jnp.dot(grad_value_low, full_value.T, preferred_element_type=jnp.float32)
    )
    input_grad = (
        grad_resid_one + lax.psum(input_back.astype(jnp.bfloat16), TENSOR).astype(jnp.float32)
    ).reshape(tree_count, slot_count, model_width)
    grad_parts = (
        query_part,
        key_part,
        value_part,
        out_part,
        up_part,
        down_part,
        first_gain_part,
        first_shift_part,
        second_gain_part,
        second_shift_part,
    )
    summed = (
        lax.psum(grad_parts[0].astype(jnp.bfloat16), CONTEXT).astype(jnp.float32),
        lax.psum(grad_parts[1].astype(jnp.bfloat16), CONTEXT).astype(jnp.float32),
        lax.psum(grad_parts[2].astype(jnp.bfloat16), CONTEXT).astype(jnp.float32),
        lax.psum(grad_parts[3].astype(jnp.bfloat16), CONTEXT).astype(jnp.float32),
        lax.psum(grad_parts[4].astype(jnp.bfloat16), CONTEXT).astype(jnp.float32),
        lax.psum(grad_parts[5].astype(jnp.bfloat16), CONTEXT).astype(jnp.float32),
        lax.psum(grad_parts[6].astype(jnp.bfloat16), CONTEXT).astype(jnp.float32),
        lax.psum(grad_parts[7].astype(jnp.bfloat16), CONTEXT).astype(jnp.float32),
        lax.psum(grad_parts[8].astype(jnp.bfloat16), CONTEXT).astype(jnp.float32),
        lax.psum(grad_parts[9].astype(jnp.bfloat16), CONTEXT).astype(jnp.float32),
    )
    reduced = (
        lax.psum_scatter(
            summed[0].astype(jnp.bfloat16), FSDP, scatter_dimension=0, tiled=True
        ).astype(jnp.float32),
        lax.psum_scatter(
            summed[1].astype(jnp.bfloat16), FSDP, scatter_dimension=0, tiled=True
        ).astype(jnp.float32),
        lax.psum_scatter(
            summed[2].astype(jnp.bfloat16), FSDP, scatter_dimension=0, tiled=True
        ).astype(jnp.float32),
        lax.psum_scatter(
            summed[3].astype(jnp.bfloat16), FSDP, scatter_dimension=1, tiled=True
        ).astype(jnp.float32),
        lax.psum_scatter(
            summed[4].astype(jnp.bfloat16), FSDP, scatter_dimension=0, tiled=True
        ).astype(jnp.float32),
        lax.psum_scatter(
            summed[5].astype(jnp.bfloat16), FSDP, scatter_dimension=1, tiled=True
        ).astype(jnp.float32),
        lax.psum_scatter(
            summed[6].astype(jnp.bfloat16), FSDP, scatter_dimension=0, tiled=True
        ).astype(jnp.float32),
        lax.psum_scatter(
            summed[7].astype(jnp.bfloat16), FSDP, scatter_dimension=0, tiled=True
        ).astype(jnp.float32),
        lax.psum_scatter(
            summed[8].astype(jnp.bfloat16), FSDP, scatter_dimension=0, tiled=True
        ).astype(jnp.float32),
        lax.psum_scatter(
            summed[9].astype(jnp.bfloat16), FSDP, scatter_dimension=0, tiled=True
        ).astype(jnp.float32),
    )
    return (
        layer_output,
        input_grad,
        loss_value,
        reduced[0],
        reduced[1],
        reduced[2],
        reduced[3],
        reduced[4],
        reduced[5],
        reduced[6],
        reduced[7],
        reduced[8],
        reduced[9],
    )


MESH_ID = pl.DeviceIdType.MESH
ROWS = 512
CORE, YY, XX, Z0, Z1, FIN = range(6)
FSDP, CONTEXT, TENSOR = "fsdp", "context", "tensor"
ST = 80


GATHER_ATTENTION = (
    (Z1, YY, Z0, XX),
    (Z1, Z0, XX, YY),
    (Z0, YY, Z1, XX),
    (Z0, Z1, YY, XX),
    (Z1, XX, Z0, YY),
    (YY, Z1, XX, Z0),
)
GATHER_UP = (
    (Z1, Z0, XX, YY),
    (Z1, YY, XX, Z0),
    (Z0, YY, Z1, XX),
)
GATHER_DOWN = (
    (Z0, Z1, XX, YY),
    (Z1, XX, YY, Z0),
    (YY, Z0, Z1, XX),
)
REDUCE_DOWN = (
    (XX, YY, Z0, Z1),
    (Z0, XX, Z1, YY),
    (Z0, XX, YY, Z1),
)
REDUCE_UP = (
    (YY, Z0, Z1, XX),
    (XX, YY, Z0, Z1),
    (Z0, XX, YY, Z1),
)
REDUCE_ATTENTION = (
    (Z0, XX, Z1, YY),
    (Z0, XX, Z1, YY),
    (XX, Z0, Z1, YY),
    (YY, Z0, XX, Z1),
    (Z0, XX, YY, Z1),
    (XX, Z0, YY, Z1),
)
GATE_U, GATE_D = 4.0, 10.0
HOLD_FORWARD, HOLD_BACKWARD, OUTPUT_STEP = False, 0, 0
UNIT_US, HOP_US, CORE_US = 3.28, 1.7, 0.3


class Plan:
    def __init__(self):
        self.now, self.free, self.flying = 0.0, {}, []
        self.holding, self.held = False, []

    def begin(self, piece):
        piece.at_stage = -1
        self.advance(piece)

    def load(self, stage, units):
        ends = []
        for link, us in self.cost(stage, units):
            ends.append(max(self.now, self.free.get(link, 0.0)) + us)
            self.free[link] = ends[-1]
        return max(ends) + HOP_US

    @staticmethod
    def cost(stage, units):
        if stage == CORE:
            return ((CORE, units * CORE_US),)
        us = units * UNIT_US
        if stage == Z1:
            return ((Z0, us), (Z1, 2 * us))
        return ((stage, us),)

    def advance(self, piece):
        piece.at_stage += 1
        if piece.at_stage < len(piece.order):
            stage = piece.order[piece.at_stage]
            if self.holding and stage in (XX, YY):
                self.held.append(piece)
                return
            piece.go(stage)
            self.flying.append((self.load(stage, piece.units[stage]), len(self.flying), piece))

    def take(self, until):
        if not self.flying:
            assert until < math.inf
            return False
        first = min(self.flying, key=lambda e: e[0])
        if first[0] > until:
            return False
        self.flying.remove(first)
        self.now = max(self.now, first[0])
        piece = first[2]
        piece.got(piece.order[piece.at_stage])
        self.advance(piece)
        return True

    def tick(self, us):
        self.now += us
        while self.take(self.now - 0.5):
            pass

    def hold(self):
        self.holding = True

    def release(self):
        self.holding = False
        held, self.held = self.held, []
        for piece in held:
            piece.at_stage -= 1
            self.advance(piece)

    def gate(self, until):
        while self.take(until):
            pass
        self.now = max(self.now, until)

    def need(self, pieces, stage=None):
        def short(p):
            done = p.at_stage
            return done < (len(p.order) if stage is None else p.order.index(stage) + 1)

        while any(short(p) for p in pieces):
            self.take(math.inf)


def fast_kernel(*refs, tree_len):
    (x_hbm, t_hbm, q_in, k_in, v_in, o_in, u_in, d_in, g1_in, s1_in, g2_in, s2_in, par, val,
     lo_hbm, ig_hbm, gout, small,
     G, NG, xv, qf, kf, vx, mk, mkT, cs, nl, att, n1, inv1, nlow, act, der, acc, glow, gT, nT,
     SR, PS, TTb, RR, dE, RX, W4, RC, RB, sm, smr, ss, rs, ls) = refs
    f = lax.axis_index(FSDP)
    c = lax.axis_index(CONTEXT)
    t = lax.axis_index(TENSOR)
    t1 = t + 1 - 2 * lax.rem(t, 2)
    t2 = lax.rem(t + 2, 4)
    t3 = lax.rem(t1 + 2, 4)
    f1 = f + 1 - 2 * lax.rem(f, 2)
    f2 = lax.rem(f + 2, 4)
    f3 = lax.rem(f1 + 2, 4)
    c1 = 1 - c
    tks = [t, t2, t1, t3]
    DEV = {CORE: {TENSOR: t1}, YY: {TENSOR: t2}, XX: {CONTEXT: c1}, Z0: {FSDP: f1}, Z1: {FSDP: f2}}
    D = 768
    counter = [0]

    def rcopy(src, dst, dev):
        i = counter[0]
        counter[0] += 1
        return pltpu.make_async_remote_copy(
            src_ref=src, dst_ref=dst, send_sem=ss.at[i], recv_sem=rs.at[i],
            device_id=DEV[dev], device_id_type=MESH_ID)

    class Batch:
        def __init__(self, pairs, dev, units, width):
            i = counter[0]
            counter[0] += 1
            self.copies = [
                pltpu.make_async_remote_copy(
                    src_ref=a, dst_ref=b, send_sem=ss.at[i], recv_sem=rs.at[i],
                    device_id=DEV[dev], device_id_type=MESH_ID)
                for a, b in pairs]
            like = RB.at[0, pl.ds(0, units), slice(None), pl.ds(0, width)]
            self.sent = pltpu.make_async_copy(like, like, ss.at[i])
            self.come = pltpu.make_async_copy(like, like, rs.at[i])

        def start(self):
            for cp in self.copies:
                cp.start()

        def wait_send(self):
            self.sent.wait()

        def wait_recv(self):
            self.come.wait()

        def wait(self):
            self.wait_send()
            self.wait_recv()

    def rbatch(pairs, dev, units, width):
        if len(pairs) == 1:
            return [rcopy(*pairs[0], dev)]
        return [Batch(pairs, dev, units, width)]

    lcounter = [0]

    def lcopy(src, dst):
        i = lcounter[0]
        lcounter[0] += 1
        return pltpu.make_async_copy(src, dst, ls.at[i])

    def start(cps):
        for cp in cps:
            cp.start()

    def wait_recv(cps):
        for cp in cps:
            cp.wait_recv()

    pending = []

    def send(cps):
        start(cps)
        pending.extend(cps)
        return cps

    def done(cp):
        pending[:] = [other for other in pending if other is not cp]

    f32, bf16 = jnp.float32, jnp.bfloat16

    def dot(a, b):
        return lax.dot_general(a, b, (((1,), (0,)), ((), ())), preferred_element_type=f32)

    def dot_nt(a, b):
        return lax.dot_general(a, b, (((1,), (1,)), ((), ())), preferred_element_type=f32)

    class Small:
        def __init__(self, stages, units, after=None):
            self.order = tuple(stages)
            self.stages, self.units, self.after = stages, units, after

        def go(self, stage):
            if self.after is not None:
                self.after(stage, False)
            send(self.stages[stage])

        def got(self, stage):
            wait_recv(self.stages[stage])
            if self.after is not None:
                self.after(stage, True)

    bar = pltpu.get_barrier_semaphore()
    for dev in DEV.values():
        pl.semaphore_signal(bar, inc=1, device_id=dev, device_id_type=MESH_ID)

    def block_of(ti):
        return jnp.where(c == 0, ti, 2 * lax.rem(ti, 2) + ti // 2)

    row0 = pl.multiple_of(block_of(t) * ROWS, ROWS)
    lx = lcopy(x_hbm.at[0, pl.ds(row0, ROWS), :], xv)
    lt = lcopy(t_hbm.at[0, pl.ds(row0, ROWS), :], xv)
    lx2 = lcopy(x_hbm.at[0, pl.ds(row0, ROWS), :], nlow)
    tv = lob = xv
    igb, xT = nlow, nT
    own = [lcopy(w_in, G.at[m, t, f]) for m, w_in in ((1, u_in), (2, d_in))]
    start([lx] + own)
    oT = jnp.transpose(o_in[...].astype(jnp.float32)).astype(jnp.bfloat16)
    for h in range(2):
        r = slice(h * 96, h * 96 + 96)
        own_a = G.at[0, t, f, h]
        own_a[:, 0:128] = q_in[r, 0:128]
        own_a[:, 128:256] = k_in[r, 0:128]
        own_a[:, 256:384] = v_in[r, 0:128]
        own_a[:, 384:512] = jnp.concatenate([q_in[r, 128:192], k_in[r, 128:192]], axis=1)
        own_a[:, 512:640] = jnp.concatenate([v_in[r, 128:192], oT[r, 128:192]], axis=1)
        own_a[:, 640:768] = oT[r, 0:128]
    row = lax.broadcasted_iota(jnp.int32, (16, 192), 0)
    vectors = jnp.zeros((16, 192), jnp.float32)
    for i, v_ref in enumerate((g1_in, s1_in, g2_in, s2_in)):
        v = v_ref[...].astype(jnp.float32).reshape(1, 192)
        vectors = jnp.where(row == i, jnp.broadcast_to(v, (16, 192)), vectors)
    NG[f] = jnp.zeros((16, 256), jnp.bfloat16)
    NG[f, :, 0:192] = vectors.astype(jnp.bfloat16)
    for cp in own:
        cp.wait()
    pl.semaphore_wait(bar, 5)

    far, near = {id(f): f2, id(f1): f3}, {id(f): f1, id(f2): f3}
    class Gather:
        def __init__(self, m, l0, n, order, split):
            self.lanes = slice(None) if n == D else pl.ds(l0, n)
            self.m, self.order = m, order
            self.ts, self.fs = [t], [f]
            self.h = c if split else None
            self.stages, self.units, self.share, self.width = {}, {}, n / D, n
            for stage in order:
                self.stages[stage] = self.build(stage)

        def at(self, ti, fi, h):
            hh = slice(None) if h is None else h
            return G.at[self.m, ti, fi, hh, slice(None), self.lanes]

        def build(self, stage):
            regs = []
            fl = [slice(None)] if len(self.fs) == 4 else self.fs
            if stage == XX:
                for ti in self.ts:
                    if ti is t:
                        others = [fi for fi in self.fs if fi is not f]
                        regs += [(ti, fi, c) for fi in others]
                    else:
                        regs += [(ti, fi, c) for fi in fl]
                self.h = None
            else:
                regs = [(ti, fi, self.h) for ti in self.ts for fi in fl]
                if stage == Z1:
                    self.fs = self.fs + [far[id(v)] for v in self.fs]
                if stage == Z0:
                    self.fs = self.fs + [near[id(v)] for v in self.fs]
                if stage == YY:
                    self.ts = self.ts + [t2]
                if stage == CORE:
                    self.ts = self.ts + [t1, t3]
            count = sum((4 if isinstance(fi, slice) else 1) * (2 if h is None else 1) for _, fi, h in regs)
            self.units[stage] = count * self.share
            return rbatch([(self.at(*r), self.at(*r)) for r in regs], stage, count, self.width)

        def go(self, stage):
            send(self.stages[stage])

        def got(self, stage):
            wait_recv(self.stages[stage])

    gather_orders = (GATHER_ATTENTION, GATHER_UP, GATHER_DOWN)
    gat = [[Gather(m, j * (D // len(o)), D // len(o), order + (CORE,), True) for j, order in enumerate(o)]
           for m, o in enumerate(gather_orders)]
    norm_vectors = Small(
        {Z1: [rcopy(NG.at[f], NG.at[f], Z1)],
         Z0: [rcopy(NG.at[f], NG.at[f], Z0), rcopy(NG.at[f2], NG.at[f2], Z0)]}, {Z1: 0.03, Z0: 0.06})
    plan = Plan()
    for g in gat[0][:5]:
        plan.begin(g)
    plan.begin(norm_vectors)

    lane = lax.broadcasted_iota(jnp.int32, (ROWS, 128), 1)
    low_half = lane < 64
    half_len, branch_len, leaf_len = tree_len // 2, tree_len // 16, tree_len // 32
    leaf_start = half_len + 4 * branch_len
    base_slot = c * (4 * ROWS) + block_of(t) * ROWS

    def layout(slot):
        in_leaf = slot >= leaf_start
        in_branch = (slot >= half_len) & jnp.logical_not(in_leaf)
        bi = jnp.clip((slot - half_len) >> (branch_len.bit_length() - 1), 0, 3)
        li = jnp.clip((slot - leaf_start) >> (leaf_len.bit_length() - 1), 0, 7)
        lp = jnp.zeros_like(slot)
        for k in range(8):
            lp = jnp.where(li == k, par[0, k], lp)
        seg = jnp.where(in_leaf, 5 + li, jnp.where(in_branch, 1 + bi, 0))
        own_b = jnp.where(in_leaf, lp, jnp.where(in_branch, 1 + bi, 0))
        leaf_pos = half_len + jnp.where(lp > 0, branch_len, 0) + slot - leaf_start - li * leaf_len
        posn = jnp.where(in_leaf, leaf_pos, jnp.where(in_branch, slot - bi * branch_len, slot))
        return seg, own_b, posn

    slot_col = base_slot + lax.broadcasted_iota(jnp.int32, (ROWS, 128), 0)
    seg_c, own_c, pos_c = layout(slot_col)
    ang = 0.5 * math.pi * pos_c.astype(f32) / float(half_len + branch_len + leaf_len)
    cs[...] = jnp.where(low_half, jnp.cos(ang), jnp.sin(ang))
    slot_row = base_slot + lax.broadcasted_iota(jnp.int32, (8, ROWS), 1)
    seg_r8, own_r8, _ = layout(slot_row)
    seg_r, own_r, sl_r = seg_r8[0:1], own_r8[0:1], slot_row[0:1]
    for j in range(4):
        ls_ = slice(j * 128, j * 128 + 128)
        sr, orr, slr = seg_r[:, ls_], own_r[:, ls_], sl_r[:, ls_]
        ok = (slr <= slot_col) & ((sr == seg_c) | (sr == 0) | (sr == own_c))
        mk[:, ls_] = jnp.where(ok, 1.0, 0.0).astype(bf16)
        okT = (slot_col <= slr) & ((seg_c == sr) | (seg_c == 0) | (seg_c == orr))
        mkT[:, ls_] = jnp.where(okT, 1.0, 0.0).astype(bf16)
    lx.wait()

    plan.tick(4.0)
    plan.gate(GATE_U)
    for g in gat[0][5:] + gat[1]:
        plan.begin(g)
    plan.gate(GATE_D)
    for g in gat[2]:
        plan.begin(g)

    def Gv(m, tk, l0, n):
        return G[m, tk, :, :, :, l0:l0 + n].reshape(D, n)

    def Gd(m, tk, n0, n):
        return G[m, tk, :, :, :, pl.ds(n0, n)].reshape(D, n)

    def from_low(p):
        return (jnp.where(low_half, p, pltpu.roll(p, 64, 1)) * cs[...]).astype(bf16)

    def from_high(p):
        return (jnp.where(low_half, pltpu.roll(p, 64, 1), p) * cs[...]).astype(bf16)

    def vext(p, up):
        p = pltpu.roll(p, 64, 1) if up else p
        return jnp.where(low_half, p, jnp.where(lane == 64, 1.0, 0.0)).astype(bf16)

    def project_kv(tk):
        h = tk * 3
        a = dot(xv[...], Gv(0, tk, 128, 256))
        k01 = jnp.maximum(a[:, :128], 0.0)
        kf[h] = from_low(k01)
        kf[h + 1] = from_high(k01)
        vx[h] = vext(a[:, 128:], False)
        vx[h + 1] = vext(a[:, 128:], True)
        b = dot(xv[...], Gv(0, tk, 384, 256))
        r = jnp.maximum(b[:, :128], 0.0)
        qf[h + 2] = from_low(r)
        kf[h + 2] = from_high(r)
        vx[h + 2] = vext(b[:, 128:], False)
        for j in range(3):
            vT = jnp.transpose(vx[h + j].astype(f32)).astype(bf16)
            u0 = dot(vT[:ST, :256], kf[h + j, :256])
            u1 = dot(vT[:ST, 256:], kf[h + j, 256:])
            first = jnp.where(c == 0, u0 + u1, u0)
            dE[0, h + j] = first.astype(bf16)
            dE[1, h + j] = u1.astype(bf16)

    def project_q(tk, _):
        q01 = jnp.maximum(dot(xv[...], Gv(0, tk, 0, 128)), 0.0)
        qf[tk * 3] = from_low(q01)
        qf[tk * 3 + 1] = from_high(q01)
        return 0

    first_needed, last_needed = gat[0][1:5], gat[0][:1]
    for g in first_needed:
        plan.need([g], g.order[-2])
    project_kv(tks[0])
    plan.tick(1.1)
    project_kv(tks[1])
    plan.tick(1.1)
    plan.need(first_needed)
    if HOLD_FORWARD:
        plan.hold()
    project_kv(tks[2])
    plan.tick(1.1)
    project_kv(tks[3])
    plan.tick(1.1)

    core_id = lax.rem(t, 2)
    half = pl.ds(pl.multiple_of(core_id * 6, 6), 6)
    has_leaves = (c == 1) & (core_id == 1)
    has_branches = (c == 1) & (core_id == 0)
    fc0 = [rcopy(dE.at[0], SR.at[1], CORE)]
    fy0 = [rcopy(dE.at[1, half], SR.at[0, half], YY)]
    fx0 = [rcopy(TTb.at[half], PS.at[half], XX)]
    fo0 = [rcopy(SR.at[0, half], SR.at[2, half], CORE)]
    fy1 = [rcopy(dE.at[pl.ds(0, 2)], SR.at[pl.ds(0, 2)], YY)]
    fn1 = [rcopy(dE.at[pl.ds(0, 2)], SR.at[pl.ds(0, 2)], CORE)]
    fc1 = [rcopy(SR.at[pl.ds(0, 2)], SR.at[pl.ds(2, 2)], CORE)]
    fo1 = [rcopy(PS.at[half], PS.at[half], CORE)]

    def each_half(body):
        def one(i, _):
            body(core_id * 6 + i)
            return 0

        lax.fori_loop(0, 6, one, 0)

    def local_fwd(h, _):
        s = dot_nt(qf[h], kf[h]).astype(bf16) * mk[...]
        nl[h] = dot(s, vx[h])
        return 0

    @pl.when(c == 0)
    def _():
        start(fc0)

    @pl.when(has_branches)
    def _():
        start(fy1)
        start(fn1)

    units_due = plan.load(YY, 1.7)
    plan.need(last_needed)
    lax.fori_loop(0, 4, project_q, 0)
    plan.tick(1.8)

    @pl.when(c == 0)
    def _():
        for cp in fc0:
            cp.wait()

        def chip_sum(h):
            dE[1, h] = (dE[0, h].astype(f32) + SR[1, h].astype(f32)).astype(bf16)

        each_half(chip_sum)
        start(fy0)

    due = plan.load(YY, 0.85)
    lax.fori_loop(0, 7, local_fwd, 0)
    plan.tick(3.7)
    plan.gate(max(due, plan.now))

    @pl.when(c == 0)
    def _():
        for cp in fy0:
            cp.wait()

        def total(h):
            TTb[h] = (dE[1, h].astype(f32) + SR[0, h].astype(f32)).astype(bf16)

        each_half(total)
        start(fx0)
        start(fo0)

    due = plan.load(XX, 0.85) + 1.5
    plan.release()
    lax.fori_loop(7, 12, local_fwd, 0)
    plan.tick(2.7)
    plan.gate(max(units_due + 1.5, due, plan.now))

    @pl.when(c == 0)
    def _():
        for cp in fo0:
            cp.wait()
        for cp in fx0:
            cp.wait_send()

        def before(h, _):
            zero = jnp.zeros((ST, 128), f32)
            mine = h // 6 == core_id
            other = jnp.where(mine, SR[0, h].astype(f32), SR[2, h].astype(f32))
            p = jnp.where(t1 < t, SR[1, h].astype(f32), zero) + jnp.where(t2 < t, other, zero)
            PS[h] = p.astype(bf16)
            return 0

        lax.fori_loop(0, 12, before, 0)

    @pl.when(c == 1)
    def _():
        wait_recv(fx0)
        start(fo1)

    @pl.when(has_branches)
    def _():
        for cp in fy1:
            cp.wait()
        start(fc1)
        for cp in fn1 + fc1:
            cp.wait_send()

    @pl.when(has_leaves)
    def _():
        wait_recv(fn1 + fc1)

    @pl.when(c == 1)
    def _():
        for cp in fo1:
            cp.wait()


    def leaf_parent(i):
        return jnp.where(has_leaves, jnp.where(t < 2, par[0, i], par[0, 4 + i]), 0)

    low_base = jnp.where(t < 2, 0, 2)
    high_base = jnp.where(t < 2, 2, 0)

    def chunk_state(h, lp):
        s = PS[h].astype(f32)
        zero = jnp.zeros_like(s)
        s = s + jnp.where(lp == 1, SR[low_base, h].astype(f32), zero)
        s = s + jnp.where(lp == 2, SR[low_base + 1, h].astype(f32), zero)
        s = s + jnp.where(lp == 3, SR[high_base, h].astype(f32), zero)
        s = s + jnp.where(lp == 4, SR[high_base + 1, h].astype(f32), zero)
        s = s.astype(bf16)
        return jnp.concatenate([s, jnp.zeros((128 - ST, 128), bf16)], axis=0)

    lane_c = lax.broadcasted_iota(jnp.int32, (128, 128), 1)
    low_c = lane_c < 64
    zs = jnp.zeros((12, ST, 128), bf16)
    zh = jnp.zeros((6, ST, 128), bf16)
    rest = pl.ds(pl.multiple_of(6 - core_id * 6, 6), 6)

    @pl.when(c == 0)
    def _():
        SR[3] = zs
        SR[0, rest] = zh
        SR[2, half] = zh
        RR[1, rest] = zh
        RR[2, half] = zh
        RR[3] = zs
        RX[rest] = zh

    @pl.when(c == 1)
    def _():
        RX[...] = zs
        RR[1] = zs

    @pl.when(has_branches)
    def _():
        SR[2] = zs
        SR[3] = zs

    def prior_fwd(tt, _):
        for i in range(4):
            lp = leaf_parent(i)
            rows = pl.ds(i * 128, 128)
            outs = []
            for j in range(3):
                h = tt * 3 + j
                tot = nl[h, rows, :] + dot_nt(qf[h, rows, :], chunk_state(h, lp))
                den = jnp.broadcast_to(tot[:, 64:65], (128, 128))
                a = tot / jnp.maximum(den, 1.0)
                nl[h, rows, :] = jnp.where(low_c, a, den)
                outs.append(a)
            att[tt, rows, 0:128] = jnp.where(low_c, 0.0, pltpu.roll(outs[2], 64, 1)).astype(bf16)
            att[tt, rows, 128:256] = jnp.where(low_c, outs[0], pltpu.roll(outs[1], 64, 1)).astype(bf16)
        return 0

    lax.fori_loop(0, 4, prior_fwd, 0)
    plan.tick(4.5)
    plan.need(gat[0])

    acc[...] = xv[...].astype(f32)
    lt.start()

    def outp(tt, _):
        acc[...] += dot_nt(att[tt], Gv(0, tt, 512, 256))
        return 0

    lax.fori_loop(0, 4, outp, 0)
    plan.need([norm_vectors])
    ng = [NG[i].astype(f32) for i in range(4)]
    r1, r3 = pltpu.roll(ng[1], 64, 1), pltpu.roll(ng[3], 64, 1)
    gains = jnp.concatenate(
        [ng[0][:, :128], ng[0][:, 128:] + r1[:, :128], r1[:, 128:],
         ng[2][:, :128], ng[2][:, 128:] + r3[:, :128], r3[:, 128:]], axis=1)
    gain1, shift1, gain2, shift2 = (gains[i:i + 1] for i in range(4))
    RB_ = 128

    def norm1(i, _):
        rows = pl.ds(pl.multiple_of(i * RB_, RB_), RB_)
        r = acc[rows, :]
        cen = r - jnp.mean(r, axis=1, keepdims=True)
        inv = lax.rsqrt(jnp.mean(cen * cen, axis=1, keepdims=True) + norm_eps)
        nrm = cen * inv
        y = nrm * gain1 + shift1
        n1[rows, :] = nrm
        inv1[rows, :] = jnp.broadcast_to(inv, (RB_, 128))
        acc[rows, :] = y
        nlow[rows, :] = y.astype(bf16)
        return 0

    lax.fori_loop(0, ROWS // RB_, norm1, 0)
    for j in range(3):
        nT[j * 256:(j + 1) * 256, :] = jnp.transpose(nlow[:, j * 256:(j + 1) * 256])

    plan.tick(3.5)
    plan.need(gat[1])

    r2_ = 1.0 / math.sqrt(2.0)

    def ffn_up(tt, _):
        for n in range(3):
            hpre = dot(nlow[...], Gv(1, tt, n * 256, 256))
            cum = 0.5 * (1.0 + lax.erf(hpre * r2_))
            dens = jnp.exp(-0.5 * hpre * hpre) * (1.0 / math.sqrt(2.0 * math.pi))
            act[tt, :, n * 256:(n + 1) * 256] = (hpre * cum).astype(bf16)
            der[tt, :, n * 256:(n + 1) * 256] = (cum + hpre * dens).astype(bf16)
        return 0

    lax.fori_loop(0, 2, ffn_up, 0)
    plan.tick(2.2)
    lax.fori_loop(2, 4, ffn_up, 0)
    plan.tick(2.2)
    plan.need(gat[2])

    def ffn_down(tt, _):
        acc[...] += dot_nt(act[tt], Gv(2, tt, 0, D))
        return 0

    lax.fori_loop(0, 4, ffn_down, 0)
    plan.tick(3.0)

    lt.wait()
    vc = val[0]

    def norm2(i, carry):
        sg, sh, sl = carry
        rows = pl.ds(pl.multiple_of(i * RB_, RB_), RB_)
        r = acc[rows, :]
        cen = r - jnp.mean(r, axis=1, keepdims=True)
        inv = lax.rsqrt(jnp.mean(cen * cen, axis=1, keepdims=True) + norm_eps)
        nrm = cen * inv
        res = nrm * gain2 + shift2
        goal = tv[rows, :].astype(f32)
        lob[rows, :] = res.astype(bf16)
        slot = base_slot + i * RB_ + lax.broadcasted_iota(jnp.int32, (RB_, 1), 0)
        e = jnp.where(slot < vc, res - goal, 0.0)
        sc = e * gain2
        g = inv * (sc - jnp.mean(sc, axis=1, keepdims=True) - nrm * jnp.mean(sc * nrm, axis=1, keepdims=True))
        acc[rows, :] = g
        glow[rows, :] = g.astype(bf16)

        def fold(v):
            return jnp.sum(v.reshape(RB_ // 8, 8, D), axis=0)

        return (sg + fold(e * nrm), sh + fold(e), sl + fold(e * e))

    z8 = jnp.zeros((8, D), f32)
    sg, sh, sl = lax.fori_loop(0, ROWS // RB_, norm2, (z8, z8, z8))
    sm[0:1] = jnp.sum(sg, axis=0, keepdims=True)
    sm[1:2] = jnp.sum(sh, axis=0, keepdims=True)
    sm[2:3] = 0.5 * jnp.sum(sl, axis=0, keepdims=True)
    for j in range(3):
        gT[j * 256:(j + 1) * 256, :] = jnp.transpose(glow[:, j * 256:(j + 1) * 256])

    def rows_of(ti):
        return pl.ds(pl.multiple_of(block_of(ti) * ROWS, ROWS), ROWS)

    lo_l = lcopy(lob, lo_hbm.at[rows_of(t)])
    lo_l.start()
    ticks = [0]

    def step(us):
        plan.tick(us)
        if ticks[0] == OUTPUT_STEP:
            plan.begin(lo_out)
        ticks[0] += 1

    lo_c = send([rcopy(lob, lo_hbm.at[rows_of(t)], CORE)])
    lo_out = Small({YY: [rcopy(lob, lo_hbm.at[rows_of(t)], YY)],
                    CORE: [rcopy(lo_hbm.at[rows_of(t2)], lo_hbm.at[rows_of(t2)], CORE)]}, {YY: 5.3, CORE: 5.3})
    step(3.2)
    lx2.start()

    class Reduce:
        def __init__(self, m, acc4, j, width, order, alloc):
            self.m, self.order, self.acc4 = m, order + (FIN,), acc4
            self.lanes = pl.ds(j * width, width)
            self.stages, self.units, self.share, self.width = {}, {}, width / D, width
            h, sl, fl = None, [0, 1], [f, f1, f2, f3]
            for name in order:
                full = len(fl) == 4
                fs = [slice(None)] if full else fl
                if name == XX:
                    src = [(s, fi, c1) for s in sl for fi in fs]
                    keep = [(s, fi, c) for s in sl for fi in fs]
                    h = c
                elif name == YY:
                    hs = ((0, 1) if full else (slice(None),)) if h is None else (h,)
                    src = [(1, fi, hh) for fi in fs for hh in hs]
                    keep = [(0, fi, hh) for fi in fs for hh in hs]
                    sl = [0]
                else:
                    hh = slice(None) if h is None else h
                    away = (f1, f3) if name == Z0 else (f2,)
                    fl = [f, f2] if name == Z0 else [f]
                    if name == Z0:
                        stay = (f, f2)
                    else:
                        stay = (f,)
                    src = [(s, fi, hh) for s in sl for fi in away]
                    keep = [(s, fi, hh) for s in sl for fi in stay]
                self.stage(name, src, keep, alloc)
            self.fin_dst = alloc(1).at[:, self.lanes]
            self.stages[FIN] = ([rcopy(self.at(0, f, c), self.fin_dst, XX)], None, None)
            self.units[FIN] = self.share

        def at(self, s, fi, h):
            return self.acc4.at[2 + s, fi, h, slice(None), self.lanes]

        def stage(self, name, src, keep, alloc):
            sizes = [4 if isinstance(fi, slice) else 2 if isinstance(h, slice) else 1 for _, fi, h in src]
            dsts = []
            for n in sizes:
                b = alloc(n)
                dsts.append(b.at[:, self.lanes] if n == 1 else b.at[:, :, self.lanes])
            self.units[name] = sum(sizes) * self.share
            cps = rbatch([(self.at(*r), d) for r, d in zip(src, dsts)], name, sum(sizes), self.width)
            self.stages[name] = (cps, dsts, [self.at(*r) for r in keep])

        def go(self, name):
            send(self.stages[name][0])

        def got(self, name):
            cps, dsts, keep = self.stages[name]
            for cp in cps:
                cp.wait()
                done(cp)
            if name == FIN:
                lput(self.at(0, f, c), gout.at[self.m, c, slice(None), self.lanes])
                lput(self.fin_dst, gout.at[self.m, c1, slice(None), self.lanes])
                return
            for p, q in zip(dsts, keep):
                if len(q.shape) == 2:
                    q[...] = q[...] + p[...]
                else:
                    for i in range(q.shape[0]):
                        q[i] = q[i] + p[i]

    puts = []

    def lput(src, dst):
        cp = lcopy(src, dst)
        cp.start()
        puts.append(cp)

    def flat_alloc(ref):
        at = [0]

        def alloc(n):
            i = at[0]
            at[0] += n
            return ref.at[i] if n == 1 else ref.at[pl.ds(i, n)]

        return alloc

    def gather_alloc():
        free = {(a, i, b) for a in (2, 3) for i in range(4) for b in range(2)}
        groups = {
            4: [({(a, i, b) for i in range(4)}, G.at[1, a, :, b]) for a in (2, 3) for b in range(2)],
            2: [({(a, i, 0), (a, i, 1)}, G.at[1, a, i]) for a in (3, 2) for i in range(4)],
            1: [({(a, i, b)}, G.at[1, a, i, b]) for a in (3, 2) for i in range(4) for b in (1, 0)],
        }

        def alloc(n):
            for cells, ref in groups[n]:
                if cells <= free:
                    free.difference_update(cells)
                    return ref
            raise ValueError(n)

        return alloc

    def pieces(m, acc4, orders, alloc_of):
        width = D // len(orders)
        return [Reduce(m, acc4, j, width, order, alloc_of()) for j, order in enumerate(orders)]

    D4, U4, A4 = W4.at[0], W4.at[1], G.at[2]
    coreD = [rcopy(D4.at[j], RC.at[0, j], CORE) for j in range(2)]
    coreU = [rcopy(U4.at[j], RC.at[1, j], CORE) for j in range(2)]
    coreA = [rcopy(A4.at[j], G.at[1, j], CORE) for j in range(2)]
    redD = pieces(2, D4, REDUCE_DOWN, lambda: flat_alloc(RB.at[0]))
    redU = pieces(1, U4, REDUCE_UP, lambda: flat_alloc(RB.at[1]))
    redA = pieces(0, A4, REDUCE_ATTENTION, gather_alloc)

    def add_core(cps, acc4, rc):
        for cp in cps:
            cp.wait()
            done(cp)

        def one(i, _):
            for j in range(2):
                for h in range(2):
                    acc4[2 + j, i, h] = acc4[2 + j, i, h] + rc[j, i, h]
            return 0

        lax.fori_loop(0, 4, one, 0)

    def shard_of(kk):
        return jnp.where(kk == 0, t1, jnp.where(kk == 1, t3, jnp.where(kk == 2, t, t2)))

    def down_grad(kk, _):
        tk = shard_of(kk)
        for n in range(3):
            cols = slice(n * 256, n * 256 + 256)
            D4[kk, :, :, :, cols] = dot(gT[...], act[tk, :, cols]).reshape(4, 2, 96, 256).astype(bf16)
        return 0

    def up_back(kk, _):
        tk = shard_of(kk)

        for n in range(3):
            n0 = n * 256
            cols = pl.ds(n0, 256)
            g = (dot(glow[...], Gd(2, tk, n0, 256)) * der[tk, :, cols].astype(f32)).astype(bf16)
            der[tk, :, cols] = g
            U4[kk, :, :, :, cols] = dot(nT[...], g).reshape(4, 2, 96, 256).astype(bf16)

        acc[...] += dot_nt(der[tk], Gv(1, tk, 0, D))
        return 0

    lax.fori_loop(0, 2, down_grad, 0)
    send(coreD)
    lax.fori_loop(2, 4, down_grad, 0)
    add_core(coreD, D4, RC.at[0])
    step(3.0)
    step(3.0)
    for r in redD:
        plan.begin(r)
    lax.fori_loop(0, 2, up_back, 0)
    send(coreU)
    step(5.3)
    lax.fori_loop(2, 4, up_back, 0)
    step(5.3)
    add_core(coreU, U4, RC.at[1])
    step(1.0)
    for r in redU:
        plan.begin(r)

    def norm1b(i, carry):
        sg, sh = carry
        rows = pl.ds(pl.multiple_of(i * RB_, RB_), RB_)
        e = acc[rows, :]
        nrm = n1[rows, :]
        inv = inv1[rows, 0:1]
        sc = e * gain1
        g = inv * (sc - jnp.mean(sc, axis=1, keepdims=True) - nrm * jnp.mean(sc * nrm, axis=1, keepdims=True))
        acc[rows, :] = g
        glow[rows, :] = g.astype(bf16)

        def fold(v):
            return jnp.sum(v.reshape(RB_ // 8, 8, D), axis=0)

        return (sg + fold(e * nrm), sh + fold(e))

    sg, sh = lax.fori_loop(0, ROWS // RB_, norm1b, (z8, z8))
    sm[3:4] = jnp.sum(sg, axis=0, keepdims=True)
    sm[4:5] = jnp.sum(sh, axis=0, keepdims=True)
    sm[5:8] = jnp.zeros((3, D), f32)
    for j in range(3):
        gT[j * 256:(j + 1) * 256, :] = jnp.transpose(glow[:, j * 256:(j + 1) * 256])

    lx2.wait()
    for j in range(3):
        xT[j * 256:(j + 1) * 256, :] = jnp.transpose(nlow[:, j * 256:(j + 1) * 256])
    step(3.0)

    links = (CORE, YY, XX, Z0, Z1)

    def sums_step(d, arrived):
        i = 2 * links.index(d)
        if arrived:
            sm[...] = sm[...] + smr[i + 1]
        else:
            smr[i] = sm[...]

    sums = Small({d: [rcopy(smr.at[2 * i], smr.at[2 * i + 1], d)] for i, d in enumerate(links)},
                 dict.fromkeys(links, 0.17), sums_step)

    for g in gat[1] + gat[2]:
        for cps in g.stages.values():
            for cp in cps:
                cp.wait_send()
                done(cp)
    plan.begin(sums)

    def gn_rows(tt, _):
        gae = dot(glow[...], G[0, tt, :, :, :, 512:768].reshape(D, 256)).astype(bf16).astype(f32)
        g2_ = pltpu.roll(gae[:, 0:128], 64, 1)
        g0_ = gae[:, 128:256]
        g1_ = pltpu.roll(g0_, 64, 1)
        for j, g in enumerate((g0_, g1_, g2_)):
            h = tt * 3 + j
            v = nl[h]
            g = jnp.where(low_half, g, 0.0)
            den = jnp.broadcast_to(v[:, 64:65], (ROWS, 128))
            safe = jnp.maximum(den, 1.0)
            s = jnp.sum(g * jnp.where(low_half, v, 0.0), axis=1, keepdims=True)
            gd_ = jnp.where(den > 1.0, -s / safe, 0.0)
            gn = jnp.where(low_half, g / safe, jnp.where(lane == 64, gd_, 0.0))
            nl[h] = gn
            gnT = jnp.transpose(gn).astype(bf16)
            parts = [dot(gnT[:ST, i * 128:(i + 1) * 128], qf[h, i * 128:(i + 1) * 128, :]) for i in range(4)]
            dE[2, h] = (parts[0] + parts[1] + parts[2] + parts[3]).astype(bf16)
            near = jnp.where(t < 2, 1, 3)
            away = jnp.where(t < 2, 3, 1)
            for slot, b in ((0, away), (1, away + 1), (3, near), (4, near + 1)):
                tot = jnp.zeros((ST, 128), f32)
                for i in range(4):
                    tot = tot + jnp.where(leaf_parent(i) == b, parts[i], 0.0)
                dE[slot, h] = tot.astype(bf16)
        return 0

    if HOLD_BACKWARD == 1:
        plan.hold()
    lax.fori_loop(0, 2, gn_rows, 0)
    step(4.2)
    if HOLD_BACKWARD == 2:
        plan.hold()
    lax.fori_loop(2, 4, gn_rows, 0)
    step(4.2)

    bc = [rcopy(dE.at[2], RR.at[0], CORE)]
    bx1 = [rcopy(dE.at[2, half], RX.at[half], XX)]
    by1 = [rcopy(dE.at[pl.ds(0, 2)], RR.at[pl.ds(2, 2)], YY)]
    bn1 = [rcopy(dE.at[pl.ds(3, 2)], RR.at[pl.ds(2, 2)], CORE)]
    by0 = [rcopy(TTb.at[half], RR.at[1, half], YY)]
    bo0 = [rcopy(dE.at[3, half], RR.at[2, half], CORE)]
    start(bc)

    @pl.when(has_leaves)
    def _():
        start(by1)

    dq = act

    def pair(y, feat):
        y = y * cs[...]
        fc = feat.astype(f32)
        fc = jnp.where(low_half, fc, pltpu.roll(fc, 64, 1))
        return jnp.where(fc > 0.0, y + pltpu.roll(y, 64, 1), 0.0).astype(bf16)

    def bwd_q(tt, _):
        for j in range(3):
            h = tt * 3 + j
            gn = nl[h].astype(bf16)
            dw = dot_nt(gn, vx[h]).astype(bf16) * mk[...]
            pri = [dot(gn[i * 128:(i + 1) * 128, :], chunk_state(h, leaf_parent(i))) for i in range(4)]
            gq = pair(dot(dw, kf[h]) + jnp.concatenate(pri, axis=0), qf[h])
            if j == 0:
                dq[tt, :, 0:64] = gq[:, 0:64]
            elif j == 1:
                dq[tt, :, 64:128] = gq[:, 64:128]
            else:
                dq[tt, :, 384:448] = gq[:, 0:64]
        return 0

    lax.fori_loop(0, 1, bwd_q, 0)
    step(1.8)

    for cp in bc:
        cp.wait()

    @pl.when(c == 1)
    def _():
        def addup(h):
            dE[2, h] = dE[2, h] + RR[0, h]

        each_half(addup)
        start(bx1)

    if HOLD_BACKWARD == 0:
        plan.hold()
    due = plan.load(XX, 0.85)
    units_due = plan.load(YY, 1.7)
    lax.fori_loop(1, 4, bwd_q, 0)
    step(5.3)
    plan.gate(max(due, plan.now))

    @pl.when(c == 0)
    def _():
        wait_recv(bx1)

        def message(h):
            zero = jnp.zeros((ST, 128), f32)
            later = dE[2, h].astype(f32) + RR[0, h].astype(f32)
            TTb[h] = (jnp.where(t >= 2, later, zero) + RX[h].astype(f32)).astype(bf16)

        each_half(message)
        start(by0)

    due = plan.load(YY, 0.85)
    plan.release()

    def out_grad(kk, _):
        tt = shard_of(kk)
        v = dot(gT[...], att[tt])
        A4[kk, :, :, :, 512:768] = v.reshape(4, 2, 96, 256).astype(bf16)
        return 0

    lax.fori_loop(0, 4, out_grad, 0)
    step(2.0)
    plan.gate(max(due, units_due, plan.now))

    @pl.when(c == 0)
    def _():
        for cp in by0:
            cp.wait()

        def common(h):
            dE[3, h] = (RX[h].astype(f32) + RR[1, h].astype(f32)).astype(bf16)

        each_half(common)
        start(bo0)
        for cp in bo0:
            cp.wait()

    @pl.when(c == 1)
    def _():
        for cp in bx1:
            cp.wait_send()

    @pl.when(has_leaves)
    def _():
        for cp in by1:
            cp.wait()

        def meet(h, _):
            dE[3, h] = dE[3, h] + RR[2, h]
            dE[4, h] = dE[4, h] + RR[3, h]
            return 0

        lax.fori_loop(0, 12, meet, 0)
        start(bn1)
        for cp in bn1:
            cp.wait_send()

    @pl.when(has_branches)
    def _():
        wait_recv(bn1)

    step(1.5)

    def later_states(h):
        zero = jnp.zeros((ST, 128), f32)
        shared = jnp.where(h // 6 == core_id, dE[3, h].astype(f32), RR[2, h].astype(f32))
        d = jnp.where(t1 > t, RR[0, h].astype(f32), zero) + shared
        pad = jnp.zeros((128 - ST, 128), bf16)
        out = []
        for u in range(2):
            b = jnp.where(has_branches, RR[2 + u, h].astype(f32), zero)
            out.append(jnp.concatenate([jnp.where(c == 0, d, b).astype(bf16), pad], axis=0))
        return out

    def bwd_kv(kk, _):
        tt = shard_of(kk)
        for j in range(3):
            h = tt * 3 + j
            gn = nl[h].astype(bf16)
            ds = later_states(h)
            wT = dot_nt(kf[h], qf[h]).astype(bf16) * mkT[...]
            dv = dot(wT, gn) + jnp.concatenate(
                [dot_nt(kf[h, u * 256:(u + 1) * 256, :], ds[u]) for u in range(2)], axis=0)
            dwT = dot_nt(vx[h], gn).astype(bf16) * mkT[...]
            dk = dot(dwT, qf[h]) + jnp.concatenate(
                [dot(vx[h, u * 256:(u + 1) * 256, :], ds[u]) for u in range(2)], axis=0)
            gk = pair(dk, kf[h])
            if j == 0:
                dq[tt, :, 128:192] = gk[:, 0:64]
                dq[tt, :, 256:320] = dv[:, 0:64].astype(bf16)
            elif j == 1:
                dq[tt, :, 192:256] = gk[:, 64:128]
                dq[tt, :, 320:384] = pltpu.roll(dv, 64, 1)[:, 64:128].astype(bf16)
            else:
                dq[tt, :, 448:512] = gk[:, 64:128]
                dq[tt, :, 512:640] = jnp.where(low_half, dv, 0.0).astype(bf16)

        def put(l0, n, v):
            A4[kk, :, :, :, l0:l0 + n] = v.reshape(4, 2, 96, n).astype(bf16)

        put(0, 256, dot(xT[...], dq[tt, :, 0:256]))
        put(256, 256, dot(xT[...], dq[tt, :, 256:512]))
        o2 = A4[kk, :, :, :, 512:640].reshape(D, 128).astype(f32)
        put(512, 128, dot(xT[...], dq[tt, :, 512:640]) + o2)
        return 0

    for p in range(2):
        lax.fori_loop(2 * p, 2 * p + 2, bwd_kv, 0)
        step(5.8)
        if p == 0:
            plan.need([sums])
            send(coreA)
    add_core(coreA, A4, G.at[1])
    step(1.0)
    for r in redA:
        plan.begin(r)

    if ticks[0] <= OUTPUT_STEP:
        plan.begin(lo_out)
    def inback(tt, _):
        acc[...] += dot_nt(dq[tt, :, 0:640], Gv(0, tt, 0, 640))
        return 0

    lax.fori_loop(0, 4, inback, 0)
    igb[...] = acc[...].astype(bf16)
    ig_l = lcopy(igb, ig_hbm.at[rows_of(t)])
    ig_l.start()
    ig_c = send([rcopy(igb, ig_hbm.at[rows_of(t)], CORE)])

    def ig_step(stage, arrived):
        if stage == YY and arrived:
            lput(der.at[0], ig_hbm.at[rows_of(t2)])

    ig_out = Small({YY: [rcopy(igb, der.at[0], YY)],
                    CORE: [rcopy(der.at[0], ig_hbm.at[rows_of(t2)], CORE)]}, {YY: 5.3, CORE: 5.3}, ig_step)
    plan.tick(4.5)
    plan.begin(ig_out)
    plan.need(redD + redU + redA + [lo_out, ig_out])
    small[...] = sm[...]
    wait_recv(lo_c + ig_c)
    for cp in pending:
        cp.wait_send()
    for cp in puts + [lo_l, ig_l]:
        cp.wait()
    assert counter[0] <= N_REMOTE and lcounter[0] <= N_LOCAL, (counter, lcounter)


N_REMOTE, N_LOCAL = 168, 40


def fast_shards(layer_input, teacher, query_weight, key_weight, value_weight, out_weight, up_weight,
                down_weight, first_gain, first_shift, second_gain, second_shift, parents, valid_count):
    f = lax.axis_index(FSDP)
    D = layer_input.shape[-1]
    sc = layer_input.shape[1]
    tree_len = sc * lax.axis_size(CONTEXT)
    bf16, f32 = jnp.bfloat16, jnp.float32
    V = pltpu.VMEM
    scratch = [
        V((3, 4, 4, 2, 96, D), bf16),
        V((4, 16, 256), bf16),
        V((ROWS, D), bf16),
        V((12, ROWS, 128), bf16),
        V((12, ROWS, 128), bf16),
        V((12, ROWS, 128), bf16),
        V((ROWS, ROWS), bf16),
        V((ROWS, ROWS), bf16),
        V((ROWS, 128), f32),
        V((12, ROWS, 128), f32),
        V((4, ROWS, 256), bf16),
        V((ROWS, D), f32),
        V((ROWS, 128), f32),
        V((ROWS, D), bf16),
        V((4, ROWS, D), bf16),
        V((4, ROWS, D), bf16),
        V((ROWS, D), f32),
        V((ROWS, D), bf16),
        V((D, ROWS), bf16),
        V((D, ROWS), bf16),
        V((4, 12, ST, 128), bf16),
        V((12, ST, 128), bf16),
        V((12, ST, 128), bf16),
        V((4, 12, ST, 128), bf16),
        V((5, 12, ST, 128), bf16),
        V((12, ST, 128), bf16),
        V((2, 4, 4, 2, 96, D), bf16),
        V((2, 2, 4, 2, 96, D), bf16),
        V((2, 16, 96, D), bf16),
        V((8, D), f32),
        V((10, 8, D), f32),
        pltpu.SemaphoreType.DMA((N_REMOTE,)),
        pltpu.SemaphoreType.DMA((N_REMOTE,)),
        pltpu.SemaphoreType.DMA((N_LOCAL,)),
    ]
    any_, smem, vmem = (pl.BlockSpec(memory_space=s) for s in (pl.ANY, pltpu.SMEM, pltpu.VMEM))
    lo, ig, gout, small = pl.pallas_call(
        functools.partial(fast_kernel, tree_len=tree_len),
        out_shape=[
            jax.ShapeDtypeStruct((sc, D), bf16),
            jax.ShapeDtypeStruct((sc, D), bf16),
            jax.ShapeDtypeStruct((3, 2, 96, D), bf16),
            jax.ShapeDtypeStruct((8, D), f32),
        ],
        in_specs=[any_, any_, vmem, vmem, vmem, vmem, any_, any_, vmem, vmem, vmem, vmem, smem, smem],
        out_specs=[any_, any_, any_, vmem],
        scratch_shapes=scratch,
        compiler_params=pltpu.CompilerParams(
            collective_id=0, has_side_effects=True, vmem_limit_bytes=67043328),
        name="tree_layer",
    )(layer_input, teacher, query_weight, key_weight, value_weight, out_weight, up_weight.reshape(2, 96, D),
      down_weight.T.reshape(2, 96, D), first_gain, first_shift, second_gain, second_shift, parents, valid_count)
    sq, wide, vec = (jax.ShapeDtypeStruct(n, f32) for n in ((192, 192), (192, D), (192,)))

    def whole(a):
        return pl.BlockSpec(a.shape, lambda i: (0,) * len(a.shape))

    outs = pl.pallas_call(
        unpack_kernel,
        grid=(4,),
        in_specs=[whole(gout), whole(small), pl.BlockSpec((ROWS, D), lambda i: (i, 0))],
        out_specs=[whole(a) for a in (sq, sq, sq, sq, wide, wide, vec, vec, vec, vec)]
        + [pl.BlockSpec((1, 1), lambda i: (0, 0)), pl.BlockSpec((ROWS, D), lambda i: (i, 0))],
        out_shape=[sq, sq, sq, sq, wide, wide, vec, vec, vec, vec,
                   jax.ShapeDtypeStruct((1, 1), f32), jax.ShapeDtypeStruct((sc, D), f32)],
        name="unpack",
    )(gout, small, ig)
    q_g, k_g, v_g, o_g, up_g, down_t, g1_g, s1_g, g2_g, s2_g, loss, ig_wide = outs
    return (lo[None], ig_wide[None], loss.reshape(()), q_g, k_g, v_g, o_g, up_g, down_t.T,
            g1_g, s1_g, g2_g, s2_g)


def unpack_kernel(gout, small, ig, q_g, k_g, v_g, o_g, up_g, down_t, g1_g, s1_g, g2_g, s2_g, loss, ig_wide):
    f32 = jnp.float32
    ig_wide[...] = ig[...].astype(f32)

    @pl.when(pl.program_id(0) == 0)
    def _():
        a = gout[0].reshape(192, 768).astype(f32)
        q_g[:, 0:128] = a[:, 0:128]
        q_g[:, 128:192] = a[:, 384:448]
        k_g[:, 0:128] = a[:, 128:256]
        k_g[:, 128:192] = pltpu.roll(a[:, 384:512], 64, 1)[:, 0:64]
        v_g[:, 0:128] = a[:, 256:384]
        v_g[:, 128:192] = a[:, 512:576]
        o_t = jnp.concatenate([a[:, 640:768], pltpu.roll(a[:, 512:640], 64, 1)], axis=1)
        o_g[...] = jnp.transpose(o_t)[0:192, :]
        up_g[...] = gout[1].reshape(192, 768).astype(f32)
        down_t[...] = gout[2].reshape(192, 768).astype(f32)
        f = lax.axis_index(FSDP)
        total = small[...]
        mine = jnp.where(f == 0, total[:, 0:256], total[:, 384:640])
        odd = jnp.where(f == 1, total[:, 128:384], total[:, 512:768])
        mine = jnp.where(f - 2 * (f // 2) == 1, pltpu.roll(odd, 192, 1), mine)[:, 0:192]
        for i, out in ((3, g1_g), (4, s1_g), (0, g2_g), (1, s2_g)):
            out[...] = mine[i]
        loss[...] = jnp.sum(total[2:3], axis=1, keepdims=True)


def shards(*arrays):
    tree_count, slot_count, width = arrays[0].shape
    sizes = tuple(lax.axis_size(n) for n in (FSDP, CONTEXT, TENSOR))
    if (tree_count, slot_count, width) == (1, 2048, 768) and sizes == (4, 2, 4) and arrays[6].shape == (192, 768):
        return fast_shards(*arrays)
    return general_shards(*arrays)


def solution(mesh):
    return jax.shard_map(
        shards,
        mesh=mesh,
        in_specs=(
            P(FSDP, CONTEXT, None),
            P(FSDP, CONTEXT, None),
            P(FSDP, TENSOR),
            P(FSDP, TENSOR),
            P(FSDP, TENSOR),
            P(TENSOR, FSDP),
            P(FSDP, TENSOR),
            P(TENSOR, FSDP),
            P(FSDP),
            P(FSDP),
            P(FSDP),
            P(FSDP),
            P(FSDP, None),
            P(FSDP),
        ),
        out_specs=(
            P(FSDP, CONTEXT, None),
            P(FSDP, CONTEXT, None),
            P(),
            P(FSDP, TENSOR),
            P(FSDP, TENSOR),
            P(FSDP, TENSOR),
            P(TENSOR, FSDP),
            P(FSDP, TENSOR),
            P(TENSOR, FSDP),
            P(FSDP),
            P(FSDP),
            P(FSDP),
            P(FSDP),
        ),
        check_vma=False,
    )
```

```python
import functools
import math

import jax
import jax.numpy as jnp
from jax import lax
from jax.experimental import pallas as pl
from jax.experimental.pallas import tpu as pltpu
from jax.sharding import PartitionSpec as P

HEAD_DIM = 64


precise = lax.Precision.HIGHEST
norm_eps = 1e-05


def carried_in(array, axis, combine, identity):
    count, here = (lax.axis_size(axis), lax.axis_index(axis))
    everything = jax.tree.map(
        lambda part, kind: lax.all_gather(part.astype(kind), axis),
        array,
        (jnp.bfloat16, jnp.bfloat16),
    )
    start = jax.tree.map(
        lambda part, zero: jnp.broadcast_to(jnp.asarray(zero, part.dtype), part.shape),
        array,
        identity,
    )

    def carried_turn(k, before):
        reached = k < here
        new = combine(
            before, jax.tree.map(lambda part, own: part[k].astype(own.dtype), everything, array)
        )
        return jax.tree.map(lambda a, b: jnp.where(reached, a, b), new, before)

    return lax.fori_loop(0, count, carried_turn, start)


def entering(array, axis, combine, identity):
    count, here = (lax.axis_size(axis), lax.axis_index(axis))
    everything = jax.tree.map(
        lambda part, kind: lax.all_gather(part.astype(kind), axis),
        array,
        jax.tree.map(lambda a: jnp.bfloat16 if a.dtype == jnp.float32 else a.dtype, array),
    )
    start = jax.tree.map(
        lambda part, zero: jnp.broadcast_to(jnp.asarray(zero, part.dtype), part.shape),
        array,
        identity,
    )

    def entering_turn(k, before):
        at = count - 1 - k
        reached = at > here
        new = combine(
            before, jax.tree.map(lambda part, own: part[at].astype(own.dtype), everything, array)
        )
        return jax.tree.map(lambda a, b: jnp.where(reached, a, b), new, before)

    return lax.fori_loop(0, count, entering_turn, start)


def layout_of(slot_ids, parents_row, tree_len):
    half_len = tree_len // 2
    branch_len = tree_len // 16
    leaf_len = tree_len // 32
    leaf_start = half_len + 4 * branch_len
    in_branch = (slot_ids >= half_len) & (slot_ids < leaf_start)
    in_leaf = slot_ids >= leaf_start
    branch_index = jnp.clip((slot_ids - half_len) // branch_len, 0, 3)
    leaf_index = jnp.clip((slot_ids - leaf_start) // leaf_len, 0, 7)
    leaf_ids = jnp.arange(8, dtype=jnp.int32)
    leaf_parent = jnp.sum(
        jnp.where(leaf_index[:, None] == leaf_ids[None, :], parents_row[None, :], 0), axis=1
    )
    segment = jnp.where(in_leaf, 5 + leaf_index, jnp.where(in_branch, 1 + branch_index, 0))
    owner_branch = jnp.where(in_leaf, leaf_parent, jnp.where(in_branch, 1 + branch_index, 0))
    leaf_pos = (
        half_len
        + jnp.where(leaf_parent > 0, branch_len, 0)
        + slot_ids
        - leaf_start
        - leaf_index * leaf_len
    )
    branch_pos = slot_ids - branch_index * branch_len
    position = jnp.where(in_leaf, leaf_pos, jnp.where(in_branch, branch_pos, slot_ids))
    phase_angle = (
        0.5 * math.pi * position.astype(jnp.float32) / float(half_len + branch_len + leaf_len)
    )
    return (segment, owner_branch, phase_angle)


def features(pre_act, phase_angle):
    rectified = jnp.maximum(pre_act, 0.0)
    cosine = jnp.cos(phase_angle)[..., None, None]
    sine_part = jnp.sin(phase_angle)[..., None, None]
    return jnp.concatenate([rectified * cosine, rectified * sine_part], axis=-1)


def features_back(grad_feat, pre_act, phase_angle):
    half_dim = pre_act.shape[-1]
    cosine = jnp.cos(phase_angle)[..., None, None]
    sine_part = jnp.sin(phase_angle)[..., None, None]
    combined = grad_feat[..., :half_dim] * cosine + grad_feat[..., half_dim:] * sine_part
    return jnp.where(pre_act > 0.0, combined, 0.0)


def norm_forward(resid, gain_vec, shift_vec):
    row_mean = jnp.mean(resid, axis=-1, keepdims=True)
    centered = resid - row_mean
    inv_std = lax.rsqrt(jnp.mean(centered * centered, axis=-1, keepdims=True) + norm_eps)
    normal = centered * inv_std
    return (normal * gain_vec + shift_vec, normal, inv_std)


def norm_backward(grad_out, normal, inv_std, gain_vec):
    scaled = grad_out * gain_vec
    grad_in = inv_std * (
        scaled
        - jnp.mean(scaled, axis=-1, keepdims=True)
        - normal * jnp.mean(scaled * normal, axis=-1, keepdims=True)
    )
    return (grad_in, jnp.sum(grad_out * normal, axis=0), jnp.sum(grad_out, axis=0))


def add_pair(earlier, later):
    return (earlier[0] + later[0], earlier[1] + later[1])


def general_shards(
    layer_input,
    teacher,
    query_weight,
    key_weight,
    value_weight,
    out_weight,
    up_weight,
    down_weight,
    first_gain,
    first_shift,
    second_gain,
    second_shift,
    parents,
    valid_count,
):
    tree_count, slot_count, model_width = layer_input.shape
    ctx_size = lax.axis_size(CONTEXT)
    ctx_index = lax.axis_index(CONTEXT)
    tree_len = slot_count * ctx_size
    row_count = tree_count * slot_count
    (
        full_query,
        full_key,
        full_value,
        full_out,
        full_up,
        full_down,
        gain_one,
        shift_one,
        gain_two,
        shift_two,
    ) = (
        lax.all_gather(query_weight, FSDP, axis=0, tiled=True),
        lax.all_gather(key_weight, FSDP, axis=0, tiled=True),
        lax.all_gather(value_weight, FSDP, axis=0, tiled=True),
        lax.all_gather(out_weight, FSDP, axis=1, tiled=True),
        lax.all_gather(up_weight, FSDP, axis=0, tiled=True),
        lax.all_gather(down_weight, FSDP, axis=1, tiled=True),
        lax.all_gather(first_gain, FSDP, axis=0, tiled=True),
        lax.all_gather(first_shift, FSDP, axis=0, tiled=True),
        lax.all_gather(second_gain, FSDP, axis=0, tiled=True),
        lax.all_gather(second_shift, FSDP, axis=0, tiled=True),
    )
    gain_one = gain_one.astype(jnp.float32)
    shift_one = shift_one.astype(jnp.float32)
    gain_two = gain_two.astype(jnp.float32)
    shift_two = shift_two.astype(jnp.float32)
    head_local = full_query.shape[1] // HEAD_DIM
    flat_in = layer_input.reshape(row_count, model_width)
    slot_ids = ctx_index * slot_count + jnp.arange(slot_count, dtype=jnp.int32)

    def layout_here(parents_row):
        return layout_of(slot_ids, parents_row, tree_len)

    segment, owner_branch, phase_angle = jax.vmap(layout_here)(parents)

    def project(weight):
        return jnp.dot(flat_in, weight, preferred_element_type=jnp.float32).reshape(
            tree_count, slot_count, head_local, HEAD_DIM
        )

    query_pre = project(full_query)
    key_pre = project(full_key)
    values = project(full_value).astype(jnp.bfloat16)
    query_feat = features(query_pre, phase_angle).astype(jnp.bfloat16)
    key_feat = features(key_pre, phase_angle).astype(jnp.bfloat16)
    query_wide = query_feat.astype(jnp.float32)
    key_wide = key_feat.astype(jnp.float32)
    value_wide = values.astype(jnp.float32)
    state_ids = jnp.arange(5, dtype=jnp.int32)
    segment_hit = segment[:, :, None] == state_ids
    in_segment = segment_hit.astype(jnp.float32)
    selected = ((state_ids == 0) | (owner_branch[:, :, None] == state_ids)).astype(jnp.float32)
    masked_key = jnp.where(
        segment_hit[:, :, :, None, None], key_feat[:, :, None], jnp.zeros((), jnp.bfloat16)
    )
    contrib_state = jnp.einsum(
        "tsahf,tshd->tahfd", masked_key, values, preferred_element_type=jnp.float32
    )
    contrib_norm = jnp.einsum(
        "tsa,tshf->tahf",
        segment_hit.astype(jnp.bfloat16),
        key_feat,
        preferred_element_type=jnp.float32,
    )
    zero_state = jnp.zeros_like(contrib_state)
    zero_norm = jnp.zeros_like(contrib_norm)
    prior_state, prior_norm = carried_in(
        (contrib_state, contrib_norm), CONTEXT, add_pair, (zero_state, zero_norm)
    )
    in_numer = jnp.einsum(
        "tsa,tshf,tahfd->tshd", selected, query_wide, prior_state, precision=precise
    )
    in_denom = jnp.einsum("tsa,tshf,tahf->tsh", selected, query_wide, prior_norm, precision=precise)
    block_rows = min(slot_count, 512)
    block_count = slot_count // block_rows

    def block_scores(block_index):
        row_start = block_index * block_rows
        query_rows = lax.dynamic_slice_in_dim(query_feat, row_start, block_rows, 1)
        slot_rows = lax.dynamic_slice_in_dim(slot_ids, row_start, block_rows, 0)
        segment_rows = lax.dynamic_slice_in_dim(segment, row_start, block_rows, 1)
        owner_rows = lax.dynamic_slice_in_dim(owner_branch, row_start, block_rows, 1)
        allowed = (slot_ids[None, None, :] <= slot_rows[None, :, None]) & (
            (segment[:, None, :] == segment_rows[:, :, None])
            | (segment[:, None, :] == 0)
            | (segment[:, None, :] == owner_rows[:, :, None])
        )
        allowed_wide = allowed[:, None].astype(jnp.float32)
        scores = (
            jnp.einsum("tihf,tjhf->thij", query_rows, key_feat, preferred_element_type=jnp.float32)
            * allowed_wide
        )
        return (scores, allowed_wide, query_rows)

    def local_forward(block_index):
        scores, allowed_wide, query_rows = block_scores(block_index)
        numerator = jnp.einsum("thij,tjhd->tihd", scores, value_wide, precision=precise)
        denominator = jnp.transpose(jnp.sum(scores, axis=3), (0, 2, 1))
        return (numerator, denominator)

    local_numer, local_denom = lax.map(local_forward, jnp.arange(block_count, dtype=jnp.int32))

    def unblock(stacked):
        return jnp.moveaxis(stacked, 0, 1).reshape((tree_count, slot_count) + stacked.shape[3:])

    numerator = unblock(local_numer) + in_numer
    denominator = unblock(local_denom) + in_denom
    safe_denom = jnp.maximum(denominator, 1.0)
    attended = numerator / safe_denom[..., None]
    attended_low = attended.astype(jnp.bfloat16).reshape(row_count, head_local * HEAD_DIM)
    attention_part = jnp.dot(attended_low, full_out, preferred_element_type=jnp.float32)
    attention_sum = lax.psum(attention_part.astype(jnp.bfloat16), TENSOR).astype(jnp.float32)
    resid_one = flat_in.astype(jnp.float32) + attention_sum
    normed_one, normal_one, inv_one = norm_forward(resid_one, gain_one, shift_one)
    normed_low = normed_one.astype(jnp.bfloat16)
    hidden_pre = jnp.dot(normed_low, full_up, preferred_element_type=jnp.float32)
    activated = jax.nn.gelu(hidden_pre, approximate=False).astype(jnp.bfloat16)
    ffn_part = jnp.dot(activated, full_down, preferred_element_type=jnp.float32)
    ffn_sum = lax.psum(ffn_part.astype(jnp.bfloat16), TENSOR).astype(jnp.float32)
    resid_two = normed_one + ffn_sum
    result, normal_two, inv_two = norm_forward(resid_two, gain_two, shift_two)
    layer_output = result.astype(jnp.bfloat16).reshape(tree_count, slot_count, model_width)
    valid_rows = (
        (slot_ids[None, :] < valid_count[:, None]).astype(jnp.float32).reshape(row_count, 1)
    )
    residual = (result - teacher.reshape(row_count, model_width).astype(jnp.float32)) * valid_rows
    loss_value = lax.psum(0.5 * jnp.sum(residual * residual), (FSDP, CONTEXT))
    grad_resid_two, second_gain_part, second_shift_part = norm_backward(
        residual, normal_two, inv_two, gain_two
    )
    grad_two_low = grad_resid_two.astype(jnp.bfloat16)
    down_part = jnp.dot(activated.T, grad_two_low, preferred_element_type=jnp.float32)
    grad_act = jnp.dot(grad_two_low, full_down.T, preferred_element_type=jnp.float32)
    cumulative = 0.5 * (1.0 + jax.scipy.special.erf(hidden_pre / math.sqrt(2.0)))
    density = jnp.exp(-0.5 * hidden_pre * hidden_pre) / math.sqrt(2.0 * math.pi)
    grad_pre = (grad_act * (cumulative + hidden_pre * density)).astype(jnp.bfloat16)
    up_part = jnp.dot(normed_low.T, grad_pre, preferred_element_type=jnp.float32)
    ffn_back = jnp.dot(grad_pre, full_up.T, preferred_element_type=jnp.float32)
    grad_normed_one = grad_resid_two + lax.psum(ffn_back.astype(jnp.bfloat16), TENSOR).astype(
        jnp.float32
    )
    grad_resid_one, first_gain_part, first_shift_part = norm_backward(
        grad_normed_one, normal_one, inv_one, gain_one
    )
    grad_one_low = grad_resid_one.astype(jnp.bfloat16)
    out_part = jnp.dot(attended_low.T, grad_one_low, preferred_element_type=jnp.float32)
    grad_attended = jnp.dot(grad_one_low, full_out.T, preferred_element_type=jnp.float32).astype(
        jnp.bfloat16
    )
    grad_attended = grad_attended.astype(jnp.float32).reshape(
        tree_count, slot_count, head_local, HEAD_DIM
    )
    grad_numer = grad_attended / safe_denom[..., None]
    grad_denom = jnp.where(
        denominator > 1.0, -jnp.sum(grad_attended * attended, axis=-1) / safe_denom, 0.0
    )
    grad_query = jnp.einsum(
        "tsa,tshd,tahfd->tshf", selected, grad_numer, prior_state, precision=precise
    ) + jnp.einsum("tsa,tsh,tahf->tshf", selected, grad_denom, prior_norm, precision=precise)
    grad_prior_state = jnp.einsum(
        "tsa,tshf,tshd->tahfd", selected, query_wide, grad_numer, precision=precise
    )
    grad_prior_norm = jnp.einsum(
        "tsa,tshf,tsh->tahf", selected, query_wide, grad_denom, precision=precise
    )
    grad_contrib_state, grad_contrib_norm = entering(
        (grad_prior_state, grad_prior_norm), CONTEXT, add_pair, (zero_state, zero_norm)
    )
    grad_key = jnp.einsum(
        "tsa,tshd,tahfd->tshf", in_segment, value_wide, grad_contrib_state, precision=precise
    ) + jnp.einsum("tsa,tahf->tshf", in_segment, grad_contrib_norm, precision=precise)
    grad_value = jnp.einsum(
        "tsa,tshf,tahfd->tshd", in_segment, key_wide, grad_contrib_state, precision=precise
    )

    def local_backward(carried, block_index):
        acc_key, acc_value = carried
        scores, allowed_wide, query_rows = block_scores(block_index)
        row_start = block_index * block_rows
        numer_rows = lax.dynamic_slice_in_dim(grad_numer, row_start, block_rows, 1)
        denom_rows = lax.dynamic_slice_in_dim(grad_denom, row_start, block_rows, 1)
        grad_scores = (
            jnp.einsum("tihd,tjhd->thij", numer_rows, value_wide, precision=precise)
            + jnp.transpose(denom_rows, (0, 2, 1))[:, :, :, None]
        ) * allowed_wide
        rows_grad = jnp.einsum("thij,tjhf->tihf", grad_scores, key_wide, precision=precise)
        acc_key = acc_key + jnp.einsum(
            "thij,tihf->tjhf", grad_scores, query_rows.astype(jnp.float32), precision=precise
        )
        acc_value = acc_value + jnp.einsum("thij,tihd->tjhd", scores, numer_rows, precision=precise)
        return ((acc_key, acc_value), rows_grad)

    (local_key, local_value), local_query = lax.scan(
        local_backward,
        (jnp.zeros_like(key_wide), jnp.zeros_like(value_wide)),
        jnp.arange(block_count, dtype=jnp.int32),
    )
    grad_query = grad_query + unblock(local_query)
    grad_key = grad_key + local_key
    grad_value = grad_value + local_value
    grad_query_low = (
        features_back(grad_query, query_pre, phase_angle)
        .astype(jnp.bfloat16)
        .reshape(row_count, -1)
    )
    grad_key_low = (
        features_back(grad_key, key_pre, phase_angle).astype(jnp.bfloat16).reshape(row_count, -1)
    )
    grad_value_low = grad_value.astype(jnp.bfloat16).reshape(row_count, -1)
    query_part = jnp.dot(flat_in.T, grad_query_low, preferred_element_type=jnp.float32)
    key_part = jnp.dot(flat_in.T, grad_key_low, preferred_element_type=jnp.float32)
    value_part = jnp.dot(flat_in.T, grad_value_low, preferred_element_type=jnp.float32)
    input_back = (
        jnp.dot(grad_query_low, full_query.T, preferred_element_type=jnp.float32)
        + jnp.dot(grad_key_low, full_key.T, preferred_element_type=jnp.float32)
        + jnp.dot(grad_value_low, full_value.T, preferred_element_type=jnp.float32)
    )
    input_grad = (
        grad_resid_one + lax.psum(input_back.astype(jnp.bfloat16), TENSOR).astype(jnp.float32)
    ).reshape(tree_count, slot_count, model_width)
    grad_parts = (
        query_part,
        key_part,
        value_part,
        out_part,
        up_part,
        down_part,
        first_gain_part,
        first_shift_part,
        second_gain_part,
        second_shift_part,
    )
    summed = (
        lax.psum(grad_parts[0].astype(jnp.bfloat16), CONTEXT).astype(jnp.float32),
        lax.psum(grad_parts[1].astype(jnp.bfloat16), CONTEXT).astype(jnp.float32),
        lax.psum(grad_parts[2].astype(jnp.bfloat16), CONTEXT).astype(jnp.float32),
        lax.psum(grad_parts[3].astype(jnp.bfloat16), CONTEXT).astype(jnp.float32),
        lax.psum(grad_parts[4].astype(jnp.bfloat16), CONTEXT).astype(jnp.float32),
        lax.psum(grad_parts[5].astype(jnp.bfloat16), CONTEXT).astype(jnp.float32),
        lax.psum(grad_parts[6].astype(jnp.bfloat16), CONTEXT).astype(jnp.float32),
        lax.psum(grad_parts[7].astype(jnp.bfloat16), CONTEXT).astype(jnp.float32),
        lax.psum(grad_parts[8].astype(jnp.bfloat16), CONTEXT).astype(jnp.float32),
        lax.psum(grad_parts[9].astype(jnp.bfloat16), CONTEXT).astype(jnp.float32),
    )
    reduced = (
        lax.psum_scatter(
            summed[0].astype(jnp.bfloat16), FSDP, scatter_dimension=0, tiled=True
        ).astype(jnp.float32),
        lax.psum_scatter(
            summed[1].astype(jnp.bfloat16), FSDP, scatter_dimension=0, tiled=True
        ).astype(jnp.float32),
        lax.psum_scatter(
            summed[2].astype(jnp.bfloat16), FSDP, scatter_dimension=0, tiled=True
        ).astype(jnp.float32),
        lax.psum_scatter(
            summed[3].astype(jnp.bfloat16), FSDP, scatter_dimension=1, tiled=True
        ).astype(jnp.float32),
        lax.psum_scatter(
            summed[4].astype(jnp.bfloat16), FSDP, scatter_dimension=0, tiled=True
        ).astype(jnp.float32),
        lax.psum_scatter(
            summed[5].astype(jnp.bfloat16), FSDP, scatter_dimension=1, tiled=True
        ).astype(jnp.float32),
        lax.psum_scatter(
            summed[6].astype(jnp.bfloat16), FSDP, scatter_dimension=0, tiled=True
        ).astype(jnp.float32),
        lax.psum_scatter(
            summed[7].astype(jnp.bfloat16), FSDP, scatter_dimension=0, tiled=True
        ).astype(jnp.float32),
        lax.psum_scatter(
            summed[8].astype(jnp.bfloat16), FSDP, scatter_dimension=0, tiled=True
        ).astype(jnp.float32),
        lax.psum_scatter(
            summed[9].astype(jnp.bfloat16), FSDP, scatter_dimension=0, tiled=True
        ).astype(jnp.float32),
    )
    return (
        layer_output,
        input_grad,
        loss_value,
        reduced[0],
        reduced[1],
        reduced[2],
        reduced[3],
        reduced[4],
        reduced[5],
        reduced[6],
        reduced[7],
        reduced[8],
        reduced[9],
    )


MESH_ID = pl.DeviceIdType.MESH
ROWS = 512
CORE, YY, XX, Z0, Z1, FIN = range(6)
FSDP, CONTEXT, TENSOR = "fsdp", "context", "tensor"
ST = 80


GATHER_ATTENTION = (
    (Z1, XX, Z0, YY),
    (Z1, Z0, YY, XX),
    (Z0, YY, Z1, XX),
    (Z1, Z0, XX, YY),
    (Z0, Z1, YY, XX),
    (Z1, YY, XX, Z0),
)
GATHER_UP = (
    (Z1, Z0, YY, XX),
    (Z0, Z1, XX, YY),
    (YY, Z1, XX, Z0),
)
GATHER_DOWN = (
    (Z0, Z1, XX, YY),
    (YY, XX, Z1, Z0),
    (Z0, YY, Z1, XX),
)
REDUCE_DOWN = (
    (Z0, YY, Z1, XX),
    (XX, YY, Z0, Z1),
    (Z0, Z1, XX, YY),
)
REDUCE_UP = (
    (XX, YY, Z0, Z1),
    (Z0, XX, Z1, YY),
    (XX, YY, Z0, Z1),
)
REDUCE_ATTENTION = (
    (Z0, XX, Z1, YY),
    (Z0, XX, YY, Z1),
    (XX, Z0, Z1, YY),
    (XX, Z0, YY, Z1),
    (XX, Z0, Z1, YY),
    (YY, Z0, Z1, XX),
)
GATE_U, GATE_D = 6.0, 8.0
HOLD_FORWARD, HOLD_BACKWARD, OUTPUT_STEP = False, 2, 0
UNIT_US, HOP_US, CORE_US = 3.28, 1.7, 0.3


class Plan:
    def __init__(self):
        self.now, self.free, self.flying = 0.0, {}, []
        self.holding, self.held = False, []

    def begin(self, piece):
        piece.at_stage = -1
        self.advance(piece)

    def load(self, stage, units):
        ends = []
        for link, us in self.cost(stage, units):
            ends.append(max(self.now, self.free.get(link, 0.0)) + us)
            self.free[link] = ends[-1]
        return max(ends) + HOP_US

    @staticmethod
    def cost(stage, units):
        if stage == CORE:
            return ((CORE, units * CORE_US),)
        us = units * UNIT_US
        if stage == Z1:
            return ((Z0, us), (Z1, 2 * us))
        return ((stage, us),)

    def advance(self, piece):
        piece.at_stage += 1
        if piece.at_stage < len(piece.order):
            stage = piece.order[piece.at_stage]
            if self.holding and stage in (XX, YY):
                self.held.append(piece)
                return
            piece.go(stage)
            self.flying.append((self.load(stage, piece.units[stage]), len(self.flying), piece))

    def take(self, until):
        if not self.flying:
            assert until < math.inf
            return False
        first = min(self.flying, key=lambda e: e[0])
        if first[0] > until:
            return False
        self.flying.remove(first)
        self.now = max(self.now, first[0])
        piece = first[2]
        piece.got(piece.order[piece.at_stage])
        self.advance(piece)
        return True

    def tick(self, us):
        self.now += us
        while self.take(self.now - 0.5):
            pass

    def hold(self):
        self.holding = True

    def release(self):
        self.holding = False
        held, self.held = self.held, []
        for piece in held:
            piece.at_stage -= 1
            self.advance(piece)

    def gate(self, until):
        while self.take(until):
            pass
        self.now = max(self.now, until)

    def need(self, pieces, stage=None):
        def short(p):
            done = p.at_stage
            return done < (len(p.order) if stage is None else p.order.index(stage) + 1)

        while any(short(p) for p in pieces):
            self.take(math.inf)


def fast_kernel(*refs, tree_len):
    (x_hbm, t_hbm, q_in, k_in, v_in, o_in, u_in, d_in, g1_in, s1_in, g2_in, s2_in, par, val,
     lo_hbm, ig_hbm, gout, small,
     G, NG, xv, qf, kf, vx, mk, mkT, cs, nl, att, n1, inv1, nlow, act, der, acc, glow, gT, nT,
     SR, PS, TTb, RR, dE, RX, W4, RC, RB, sm, smr, ss, rs, ls) = refs
    f = lax.axis_index(FSDP)
    c = lax.axis_index(CONTEXT)
    t = lax.axis_index(TENSOR)
    t1 = t + 1 - 2 * lax.rem(t, 2)
    t2 = lax.rem(t + 2, 4)
    t3 = lax.rem(t1 + 2, 4)
    f1 = f + 1 - 2 * lax.rem(f, 2)
    f2 = lax.rem(f + 2, 4)
    f3 = lax.rem(f1 + 2, 4)
    c1 = 1 - c
    tks = [t, t2, t1, t3]
    DEV = {CORE: {TENSOR: t1}, YY: {TENSOR: t2}, XX: {CONTEXT: c1}, Z0: {FSDP: f1}, Z1: {FSDP: f2}}
    D = 768
    counter = [0]

    def rcopy(src, dst, dev):
        i = counter[0]
        counter[0] += 1
        return pltpu.make_async_remote_copy(
            src_ref=src, dst_ref=dst, send_sem=ss.at[i], recv_sem=rs.at[i],
            device_id=DEV[dev], device_id_type=MESH_ID)

    class Batch:
        def __init__(self, pairs, dev, units, width):
            i = counter[0]
            counter[0] += 1
            self.copies = [
                pltpu.make_async_remote_copy(
                    src_ref=a, dst_ref=b, send_sem=ss.at[i], recv_sem=rs.at[i],
                    device_id=DEV[dev], device_id_type=MESH_ID)
                for a, b in pairs]
            like = RB.at[0, pl.ds(0, units), slice(None), pl.ds(0, width)]
            self.sent = pltpu.make_async_copy(like, like, ss.at[i])
            self.come = pltpu.make_async_copy(like, like, rs.at[i])

        def start(self):
            for cp in self.copies:
                cp.start()

        def wait_send(self):
            self.sent.wait()

        def wait_recv(self):
            self.come.wait()

        def wait(self):
            self.wait_send()
            self.wait_recv()

    def rbatch(pairs, dev, units, width):
        if len(pairs) == 1:
            return [rcopy(*pairs[0], dev)]
        return [Batch(pairs, dev, units, width)]

    lcounter = [0]

    def lcopy(src, dst):
        i = lcounter[0]
        lcounter[0] += 1
        return pltpu.make_async_copy(src, dst, ls.at[i])

    def start(cps):
        for cp in cps:
            cp.start()

    def wait_recv(cps):
        for cp in cps:
            cp.wait_recv()

    pending = []

    def send(cps):
        start(cps)
        pending.extend(cps)
        return cps

    def done(cp):
        pending[:] = [other for other in pending if other is not cp]

    f32, bf16 = jnp.float32, jnp.bfloat16

    def dot(a, b):
        return lax.dot_general(a, b, (((1,), (0,)), ((), ())), preferred_element_type=f32)

    def dot_nt(a, b):
        return lax.dot_general(a, b, (((1,), (1,)), ((), ())), preferred_element_type=f32)

    class Small:
        def __init__(self, stages, units, after=None):
            self.order = tuple(stages)
            self.stages, self.units, self.after = stages, units, after

        def go(self, stage):
            if self.after is not None:
                self.after(stage, False)
            send(self.stages[stage])

        def got(self, stage):
            wait_recv(self.stages[stage])
            if self.after is not None:
                self.after(stage, True)

    bar = pltpu.get_barrier_semaphore()
    for dev in DEV.values():
        pl.semaphore_signal(bar, inc=1, device_id=dev, device_id_type=MESH_ID)

    def block_of(ti):
        return jnp.where(c == 0, ti, 2 * lax.rem(ti, 2) + ti // 2)

    row0 = pl.multiple_of(block_of(t) * ROWS, ROWS)
    lx = lcopy(x_hbm.at[0, pl.ds(row0, ROWS), :], xv)
    lt = lcopy(t_hbm.at[0, pl.ds(row0, ROWS), :], xv)
    lx2 = lcopy(x_hbm.at[0, pl.ds(row0, ROWS), :], nlow)
    tv = lob = xv
    igb, xT = nlow, nT
    own = [lcopy(w_in, G.at[m, t, f]) for m, w_in in ((1, u_in), (2, d_in))]
    start([lx] + own)
    oT = jnp.transpose(o_in[...].astype(jnp.float32)).astype(jnp.bfloat16)
    for h in range(2):
        r = slice(h * 96, h * 96 + 96)
        own_a = G.at[0, t, f, h]
        own_a[:, 0:128] = q_in[r, 0:128]
        own_a[:, 128:256] = k_in[r, 0:128]
        own_a[:, 256:384] = v_in[r, 0:128]
        own_a[:, 384:512] = jnp.concatenate([q_in[r, 128:192], k_in[r, 128:192]], axis=1)
        own_a[:, 512:640] = jnp.concatenate([v_in[r, 128:192], oT[r, 128:192]], axis=1)
        own_a[:, 640:768] = oT[r, 0:128]
    row = lax.broadcasted_iota(jnp.int32, (16, 192), 0)
    vectors = jnp.zeros((16, 192), jnp.float32)
    for i, v_ref in enumerate((g1_in, s1_in, g2_in, s2_in)):
        v = v_ref[...].astype(jnp.float32).reshape(1, 192)
        vectors = jnp.where(row == i, jnp.broadcast_to(v, (16, 192)), vectors)
    NG[f] = jnp.zeros((16, 256), jnp.bfloat16)
    NG[f, :, 0:192] = vectors.astype(jnp.bfloat16)
    for cp in own:
        cp.wait()
    pl.semaphore_wait(bar, 5)

    far, near = {id(f): f2, id(f1): f3}, {id(f): f1, id(f2): f3}
    class Gather:
        def __init__(self, m, l0, n, order, split):
            self.lanes = slice(None) if n == D else pl.ds(l0, n)
            self.m, self.order = m, order
            self.ts, self.fs = [t], [f]
            self.h = c if split else None
            self.stages, self.units, self.share, self.width = {}, {}, n / D, n
            for stage in order:
                self.stages[stage] = self.build(stage)

        def at(self, ti, fi, h):
            hh = slice(None) if h is None else h
            return G.at[self.m, ti, fi, hh, slice(None), self.lanes]

        def build(self, stage):
            regs = []
            fl = [slice(None)] if len(self.fs) == 4 else self.fs
            if stage == XX:
                for ti in self.ts:
                    if ti is t:
                        others = [fi for fi in self.fs if fi is not f]
                        regs += [(ti, fi, c) for fi in others]
                    else:
                        regs += [(ti, fi, c) for fi in fl]
                self.h = None
            else:
                regs = [(ti, fi, self.h) for ti in self.ts for fi in fl]
                if stage == Z1:
                    self.fs = self.fs + [far[id(v)] for v in self.fs]
                if stage == Z0:
                    self.fs = self.fs + [near[id(v)] for v in self.fs]
                if stage == YY:
                    self.ts = self.ts + [t2]
                if stage == CORE:
                    self.ts = self.ts + [t1, t3]
            count = sum((4 if isinstance(fi, slice) else 1) * (2 if h is None else 1) for _, fi, h in regs)
            self.units[stage] = count * self.share
            return rbatch([(self.at(*r), self.at(*r)) for r in regs], stage, count, self.width)

        def go(self, stage):
            send(self.stages[stage])

        def got(self, stage):
            wait_recv(self.stages[stage])

    gather_orders = (GATHER_ATTENTION, GATHER_UP, GATHER_DOWN)
    gat = [[Gather(m, j * (D // len(o)), D // len(o), order + (CORE,), True) for j, order in enumerate(o)]
           for m, o in enumerate(gather_orders)]
    norm_vectors = Small(
        {Z1: [rcopy(NG.at[f], NG.at[f], Z1)],
         Z0: [rcopy(NG.at[f], NG.at[f], Z0), rcopy(NG.at[f2], NG.at[f2], Z0)]}, {Z1: 0.03, Z0: 0.06})
    plan = Plan()
    for g in gat[0][:5]:
        plan.begin(g)
    plan.begin(norm_vectors)

    lane = lax.broadcasted_iota(jnp.int32, (ROWS, 128), 1)
    low_half = lane < 64
    half_len, branch_len, leaf_len = tree_len // 2, tree_len // 16, tree_len // 32
    leaf_start = half_len + 4 * branch_len
    base_slot = c * (4 * ROWS) + block_of(t) * ROWS

    def layout(slot):
        in_leaf = slot >= leaf_start
        in_branch = (slot >= half_len) & jnp.logical_not(in_leaf)
        bi = jnp.clip((slot - half_len) >> (branch_len.bit_length() - 1), 0, 3)
        li = jnp.clip((slot - leaf_start) >> (leaf_len.bit_length() - 1), 0, 7)
        lp = jnp.zeros_like(slot)
        for k in range(8):
            lp = jnp.where(li == k, par[0, k], lp)
        seg = jnp.where(in_leaf, 5 + li, jnp.where(in_branch, 1 + bi, 0))
        own_b = jnp.where(in_leaf, lp, jnp.where(in_branch, 1 + bi, 0))
        leaf_pos = half_len + jnp.where(lp > 0, branch_len, 0) + slot - leaf_start - li * leaf_len
        posn = jnp.where(in_leaf, leaf_pos, jnp.where(in_branch, slot - bi * branch_len, slot))
        return seg, own_b, posn

    slot_col = base_slot + lax.broadcasted_iota(jnp.int32, (ROWS, 128), 0)
    seg_c, own_c, pos_c = layout(slot_col)
    ang = 0.5 * math.pi * pos_c.astype(f32) / float(half_len + branch_len + leaf_len)
    cs[...] = jnp.where(low_half, jnp.cos(ang), jnp.sin(ang))
    slot_row = base_slot + lax.broadcasted_iota(jnp.int32, (8, ROWS), 1)
    seg_r8, own_r8, _ = layout(slot_row)
    seg_r, own_r, sl_r = seg_r8[0:1], own_r8[0:1], slot_row[0:1]
    for j in range(4):
        ls_ = slice(j * 128, j * 128 + 128)
        sr, orr, slr = seg_r[:, ls_], own_r[:, ls_], sl_r[:, ls_]
        ok = (slr <= slot_col) & ((sr == seg_c) | (sr == 0) | (sr == own_c))
        mk[:, ls_] = jnp.where(ok, 1.0, 0.0).astype(bf16)
        okT = (slot_col <= slr) & ((seg_c == sr) | (seg_c == 0) | (seg_c == orr))
        mkT[:, ls_] = jnp.where(okT, 1.0, 0.0).astype(bf16)
    lx.wait()

    plan.tick(4.0)
    plan.gate(GATE_U)
    for g in gat[0][5:] + gat[1]:
        plan.begin(g)
    plan.gate(GATE_D)
    for g in gat[2]:
        plan.begin(g)

    def Gv(m, tk, l0, n):
        return G[m, tk, :, :, :, l0:l0 + n].reshape(D, n)

    def Gd(m, tk, n0, n):
        return G[m, tk, :, :, :, pl.ds(n0, n)].reshape(D, n)

    def from_low(p):
        return (jnp.where(low_half, p, pltpu.roll(p, 64, 1)) * cs[...]).astype(bf16)

    def from_high(p):
        return (jnp.where(low_half, pltpu.roll(p, 64, 1), p) * cs[...]).astype(bf16)

    def vext(p, up):
        p = pltpu.roll(p, 64, 1) if up else p
        return jnp.where(low_half, p, jnp.where(lane == 64, 1.0, 0.0)).astype(bf16)

    def project_kv(tk):
        h = tk * 3
        a = dot(xv[...], Gv(0, tk, 128, 256))
        k01 = jnp.maximum(a[:, :128], 0.0)
        kf[h] = from_low(k01)
        kf[h + 1] = from_high(k01)
        vx[h] = vext(a[:, 128:], False)
        vx[h + 1] = vext(a[:, 128:], True)
        b = dot(xv[...], Gv(0, tk, 384, 256))
        r = jnp.maximum(b[:, :128], 0.0)
        qf[h + 2] = from_low(r)
        kf[h + 2] = from_high(r)
        vx[h + 2] = vext(b[:, 128:], False)
        for j in range(3):
            vT = jnp.transpose(vx[h + j].astype(f32)).astype(bf16)
            u0 = dot(vT[:ST, :256], kf[h + j, :256])
            u1 = dot(vT[:ST, 256:], kf[h + j, 256:])
            first = jnp.where(c == 0, u0 + u1, u0)
            dE[0, h + j] = first.astype(bf16)
            dE[1, h + j] = u1.astype(bf16)

    def project_q(tk, _):
        q01 = jnp.maximum(dot(xv[...], Gv(0, tk, 0, 128)), 0.0)
        qf[tk * 3] = from_low(q01)
        qf[tk * 3 + 1] = from_high(q01)
        return 0

    first_needed, last_needed = gat[0][1:5], gat[0][:1]
    for g in first_needed:
        plan.need([g], g.order[-2])
    project_kv(tks[0])
    plan.tick(1.1)
    project_kv(tks[1])
    plan.tick(1.1)
    plan.need(first_needed)
    if HOLD_FORWARD:
        plan.hold()
    project_kv(tks[2])
    plan.tick(1.1)
    project_kv(tks[3])
    plan.tick(1.1)

    core_id = lax.rem(t, 2)
    half = pl.ds(pl.multiple_of(core_id * 6, 6), 6)
    has_leaves = (c == 1) & (core_id == 1)
    has_branches = (c == 1) & (core_id == 0)
    fc0 = [rcopy(dE.at[0], SR.at[1], CORE)]
    fy0 = [rcopy(dE.at[1, half], SR.at[0, half], YY)]
    fx0 = [rcopy(TTb.at[half], PS.at[half], XX)]
    fo0 = [rcopy(SR.at[0, half], SR.at[2, half], CORE)]
    fy1 = [rcopy(dE.at[pl.ds(0, 2)], SR.at[pl.ds(0, 2)], YY)]
    fn1 = [rcopy(dE.at[pl.ds(0, 2)], SR.at[pl.ds(0, 2)], CORE)]
    fc1 = [rcopy(SR.at[pl.ds(0, 2)], SR.at[pl.ds(2, 2)], CORE)]
    fo1 = [rcopy(PS.at[half], PS.at[half], CORE)]

    def each_half(body):
        def one(i, _):
            body(core_id * 6 + i)
            return 0

        lax.fori_loop(0, 6, one, 0)

    def local_fwd(h, _):
        s = dot_nt(qf[h], kf[h]).astype(bf16) * mk[...]
        nl[h] = dot(s, vx[h])
        return 0

    @pl.when(c == 0)
    def _():
        start(fc0)

    @pl.when(has_branches)
    def _():
        start(fy1)
        start(fn1)

    units_due = plan.load(YY, 1.7)
    plan.need(last_needed)
    lax.fori_loop(0, 4, project_q, 0)
    plan.tick(1.8)

    @pl.when(c == 0)
    def _():
        for cp in fc0:
            cp.wait()

        def chip_sum(h):
            dE[1, h] = (dE[0, h].astype(f32) + SR[1, h].astype(f32)).astype(bf16)

        each_half(chip_sum)
        start(fy0)

    due = plan.load(YY, 0.85)
    lax.fori_loop(0, 7, local_fwd, 0)
    plan.tick(3.7)
    plan.gate(max(due, plan.now))

    @pl.when(c == 0)
    def _():
        for cp in fy0:
            cp.wait()

        def total(h):
            TTb[h] = (dE[1, h].astype(f32) + SR[0, h].astype(f32)).astype(bf16)

        each_half(total)
        start(fx0)
        start(fo0)

    due = plan.load(XX, 0.85) + 1.5
    plan.release()
    lax.fori_loop(7, 12, local_fwd, 0)
    plan.tick(2.7)
    plan.gate(max(units_due + 1.5, due, plan.now))

    @pl.when(c == 0)
    def _():
        for cp in fo0:
            cp.wait()
        for cp in fx0:
            cp.wait_send()

        def before(h, _):
            zero = jnp.zeros((ST, 128), f32)
            mine = h // 6 == core_id
            other = jnp.where(mine, SR[0, h].astype(f32), SR[2, h].astype(f32))
            p = jnp.where(t1 < t, SR[1, h].astype(f32), zero) + jnp.where(t2 < t, other, zero)
            PS[h] = p.astype(bf16)
            return 0

        lax.fori_loop(0, 12, before, 0)

    @pl.when(c == 1)
    def _():
        wait_recv(fx0)
        start(fo1)

    @pl.when(has_branches)
    def _():
        for cp in fy1:
            cp.wait()
        start(fc1)
        for cp in fn1 + fc1:
            cp.wait_send()

    @pl.when(has_leaves)
    def _():
        wait_recv(fn1 + fc1)

    @pl.when(c == 1)
    def _():
        for cp in fo1:
            cp.wait()


    def leaf_parent(i):
        return jnp.where(has_leaves, jnp.where(t < 2, par[0, i], par[0, 4 + i]), 0)

    low_base = jnp.where(t < 2, 0, 2)
    high_base = jnp.where(t < 2, 2, 0)

    def chunk_state(h, lp):
        s = PS[h].astype(f32)
        zero = jnp.zeros_like(s)
        s = s + jnp.where(lp == 1, SR[low_base, h].astype(f32), zero)
        s = s + jnp.where(lp == 2, SR[low_base + 1, h].astype(f32), zero)
        s = s + jnp.where(lp == 3, SR[high_base, h].astype(f32), zero)
        s = s + jnp.where(lp == 4, SR[high_base + 1, h].astype(f32), zero)
        s = s.astype(bf16)
        return jnp.concatenate([s, jnp.zeros((128 - ST, 128), bf16)], axis=0)

    lane_c = lax.broadcasted_iota(jnp.int32, (128, 128), 1)
    low_c = lane_c < 64
    zs = jnp.zeros((12, ST, 128), bf16)
    zh = jnp.zeros((6, ST, 128), bf16)
    rest = pl.ds(pl.multiple_of(6 - core_id * 6, 6), 6)

    @pl.when(c == 0)
    def _():
        SR[3] = zs
        SR[0, rest] = zh
        SR[2, half] = zh
        RR[1, rest] = zh
        RR[2, half] = zh
        RR[3] = zs
        RX[rest] = zh

    @pl.when(c == 1)
    def _():
        RX[...] = zs
        RR[1] = zs

    @pl.when(has_branches)
    def _():
        SR[2] = zs
        SR[3] = zs

    def prior_fwd(tt, _):
        for i in range(4):
            lp = leaf_parent(i)
            rows = pl.ds(i * 128, 128)
            outs = []
            for j in range(3):
                h = tt * 3 + j
                tot = nl[h, rows, :] + dot_nt(qf[h, rows, :], chunk_state(h, lp))
                den = jnp.broadcast_to(tot[:, 64:65], (128, 128))
                a = tot / jnp.maximum(den, 1.0)
                nl[h, rows, :] = jnp.where(low_c, a, den)
                outs.append(a)
            att[tt, rows, 0:128] = jnp.where(low_c, 0.0, pltpu.roll(outs[2], 64, 1)).astype(bf16)
            att[tt, rows, 128:256] = jnp.where(low_c, outs[0], pltpu.roll(outs[1], 64, 1)).astype(bf16)
        return 0

    lax.fori_loop(0, 4, prior_fwd, 0)
    plan.tick(4.5)
    plan.need(gat[0])

    acc[...] = xv[...].astype(f32)
    lt.start()

    def outp(tt, _):
        acc[...] += dot_nt(att[tt], Gv(0, tt, 512, 256))
        return 0

    lax.fori_loop(0, 4, outp, 0)
    plan.need([norm_vectors])
    ng = [NG[i].astype(f32) for i in range(4)]
    r1, r3 = pltpu.roll(ng[1], 64, 1), pltpu.roll(ng[3], 64, 1)
    gains = jnp.concatenate(
        [ng[0][:, :128], ng[0][:, 128:] + r1[:, :128], r1[:, 128:],
         ng[2][:, :128], ng[2][:, 128:] + r3[:, :128], r3[:, 128:]], axis=1)
    gain1, shift1, gain2, shift2 = (gains[i:i + 1] for i in range(4))
    RB_ = 128

    def norm1(i, _):
        rows = pl.ds(pl.multiple_of(i * RB_, RB_), RB_)
        r = acc[rows, :]
        cen = r - jnp.mean(r, axis=1, keepdims=True)
        inv = lax.rsqrt(jnp.mean(cen * cen, axis=1, keepdims=True) + norm_eps)
        nrm = cen * inv
        y = nrm * gain1 + shift1
        n1[rows, :] = nrm
        inv1[rows, :] = jnp.broadcast_to(inv, (RB_, 128))
        acc[rows, :] = y
        nlow[rows, :] = y.astype(bf16)
        return 0

    lax.fori_loop(0, ROWS // RB_, norm1, 0)
    for j in range(3):
        nT[j * 256:(j + 1) * 256, :] = jnp.transpose(nlow[:, j * 256:(j + 1) * 256])

    plan.tick(3.5)
    plan.need(gat[1])

    r2_ = 1.0 / math.sqrt(2.0)

    def ffn_up(tt, _):
        for n in range(3):
            hpre = dot(nlow[...], Gv(1, tt, n * 256, 256))
            cum = 0.5 * (1.0 + lax.erf(hpre * r2_))
            dens = jnp.exp(-0.5 * hpre * hpre) * (1.0 / math.sqrt(2.0 * math.pi))
            act[tt, :, n * 256:(n + 1) * 256] = (hpre * cum).astype(bf16)
            der[tt, :, n * 256:(n + 1) * 256] = (cum + hpre * dens).astype(bf16)
        return 0

    lax.fori_loop(0, 2, ffn_up, 0)
    plan.tick(2.2)
    lax.fori_loop(2, 4, ffn_up, 0)
    plan.tick(2.2)
    plan.need(gat[2])

    def ffn_down(tt, _):
        acc[...] += dot_nt(act[tt], Gv(2, tt, 0, D))
        return 0

    lax.fori_loop(0, 4, ffn_down, 0)
    plan.tick(3.0)

    lt.wait()
    vc = val[0]

    def norm2(i, carry):
        sg, sh, sl = carry
        rows = pl.ds(pl.multiple_of(i * RB_, RB_), RB_)
        r = acc[rows, :]
        cen = r - jnp.mean(r, axis=1, keepdims=True)
        inv = lax.rsqrt(jnp.mean(cen * cen, axis=1, keepdims=True) + norm_eps)
        nrm = cen * inv
        res = nrm * gain2 + shift2
        goal = tv[rows, :].astype(f32)
        lob[rows, :] = res.astype(bf16)
        slot = base_slot + i * RB_ + lax.broadcasted_iota(jnp.int32, (RB_, 1), 0)
        e = jnp.where(slot < vc, res - goal, 0.0)
        sc = e * gain2
        g = inv * (sc - jnp.mean(sc, axis=1, keepdims=True) - nrm * jnp.mean(sc * nrm, axis=1, keepdims=True))
        acc[rows, :] = g
        glow[rows, :] = g.astype(bf16)

        def fold(v):
            return jnp.sum(v.reshape(RB_ // 8, 8, D), axis=0)

        return (sg + fold(e * nrm), sh + fold(e), sl + fold(e * e))

    z8 = jnp.zeros((8, D), f32)
    sg, sh, sl = lax.fori_loop(0, ROWS // RB_, norm2, (z8, z8, z8))
    sm[0:1] = jnp.sum(sg, axis=0, keepdims=True)
    sm[1:2] = jnp.sum(sh, axis=0, keepdims=True)
    sm[2:3] = 0.5 * jnp.sum(sl, axis=0, keepdims=True)
    for j in range(3):
        gT[j * 256:(j + 1) * 256, :] = jnp.transpose(glow[:, j * 256:(j + 1) * 256])

    def rows_of(ti):
        return pl.ds(pl.multiple_of(block_of(ti) * ROWS, ROWS), ROWS)

    lo_l = lcopy(lob, lo_hbm.at[rows_of(t)])
    lo_l.start()
    ticks = [0]

    def step(us):
        plan.tick(us)
        if ticks[0] == OUTPUT_STEP:
            plan.begin(lo_out)
        ticks[0] += 1

    lo_c = send([rcopy(lob, lo_hbm.at[rows_of(t)], CORE)])
    lo_out = Small({YY: [rcopy(lob, lo_hbm.at[rows_of(t)], YY)],
                    CORE: [rcopy(lo_hbm.at[rows_of(t2)], lo_hbm.at[rows_of(t2)], CORE)]}, {YY: 5.3, CORE: 5.3})
    step(3.2)
    lx2.start()

    class Reduce:
        def __init__(self, m, acc4, j, width, order, alloc):
            self.m, self.order, self.acc4 = m, order + (FIN,), acc4
            self.lanes = pl.ds(j * width, width)
            self.stages, self.units, self.share, self.width = {}, {}, width / D, width
            h, sl, fl = None, [0, 1], [f, f1, f2, f3]
            for name in order:
                full = len(fl) == 4
                fs = [slice(None)] if full else fl
                if name == XX:
                    src = [(s, fi, c1) for s in sl for fi in fs]
                    keep = [(s, fi, c) for s in sl for fi in fs]
                    h = c
                elif name == YY:
                    hs = ((0, 1) if full else (slice(None),)) if h is None else (h,)
                    src = [(1, fi, hh) for fi in fs for hh in hs]
                    keep = [(0, fi, hh) for fi in fs for hh in hs]
                    sl = [0]
                else:
                    hh = slice(None) if h is None else h
                    away = (f1, f3) if name == Z0 else (f2,)
                    fl = [f, f2] if name == Z0 else [f]
                    if name == Z0:
                        stay = (f, f2)
                    else:
                        stay = (f,)
                    src = [(s, fi, hh) for s in sl for fi in away]
                    keep = [(s, fi, hh) for s in sl for fi in stay]
                self.stage(name, src, keep, alloc)
            self.fin_dst = alloc(1).at[:, self.lanes]
            self.stages[FIN] = ([rcopy(self.at(0, f, c), self.fin_dst, XX)], None, None)
            self.units[FIN] = self.share

        def at(self, s, fi, h):
            return self.acc4.at[2 + s, fi, h, slice(None), self.lanes]

        def stage(self, name, src, keep, alloc):
            sizes = [4 if isinstance(fi, slice) else 2 if isinstance(h, slice) else 1 for _, fi, h in src]
            dsts = []
            for n in sizes:
                b = alloc(n)
                dsts.append(b.at[:, self.lanes] if n == 1 else b.at[:, :, self.lanes])
            self.units[name] = sum(sizes) * self.share
            cps = rbatch([(self.at(*r), d) for r, d in zip(src, dsts)], name, sum(sizes), self.width)
            self.stages[name] = (cps, dsts, [self.at(*r) for r in keep])

        def go(self, name):
            send(self.stages[name][0])

        def got(self, name):
            cps, dsts, keep = self.stages[name]
            for cp in cps:
                cp.wait()
                done(cp)
            if name == FIN:
                lput(self.at(0, f, c), gout.at[self.m, c, slice(None), self.lanes])
                lput(self.fin_dst, gout.at[self.m, c1, slice(None), self.lanes])
                return
            for p, q in zip(dsts, keep):
                if len(q.shape) == 2:
                    q[...] = q[...] + p[...]
                else:
                    for i in range(q.shape[0]):
                        q[i] = q[i] + p[i]

    puts = []

    def lput(src, dst):
        cp = lcopy(src, dst)
        cp.start()
        puts.append(cp)

    def flat_alloc(ref):
        at = [0]

        def alloc(n):
            i = at[0]
            at[0] += n
            return ref.at[i] if n == 1 else ref.at[pl.ds(i, n)]

        return alloc

    def gather_alloc():
        free = {(a, i, b) for a in (2, 3) for i in range(4) for b in range(2)}
        groups = {
            4: [({(a, i, b) for i in range(4)}, G.at[1, a, :, b]) for a in (2, 3) for b in range(2)],
            2: [({(a, i, 0), (a, i, 1)}, G.at[1, a, i]) for a in (3, 2) for i in range(4)],
            1: [({(a, i, b)}, G.at[1, a, i, b]) for a in (3, 2) for i in range(4) for b in (1, 0)],
        }

        def alloc(n):
            for cells, ref in groups[n]:
                if cells <= free:
                    free.difference_update(cells)
                    return ref
            raise ValueError(n)

        return alloc

    def pieces(m, acc4, orders, alloc_of):
        width = D // len(orders)
        return [Reduce(m, acc4, j, width, order, alloc_of()) for j, order in enumerate(orders)]

    D4, U4, A4 = W4.at[0], W4.at[1], G.at[2]
    coreD = [rcopy(D4.at[j], RC.at[0, j], CORE) for j in range(2)]
    coreU = [rcopy(U4.at[j], RC.at[1, j], CORE) for j in range(2)]
    coreA = [rcopy(A4.at[j], G.at[1, j], CORE) for j in range(2)]
    redD = pieces(2, D4, REDUCE_DOWN, lambda: flat_alloc(RB.at[0]))
    redU = pieces(1, U4, REDUCE_UP, lambda: flat_alloc(RB.at[1]))
    redA = pieces(0, A4, REDUCE_ATTENTION, gather_alloc)

    def add_core(cps, acc4, rc):
        for cp in cps:
            cp.wait()
            done(cp)

        def one(i, _):
            for j in range(2):
                for h in range(2):
                    acc4[2 + j, i, h] = acc4[2 + j, i, h] + rc[j, i, h]
            return 0

        lax.fori_loop(0, 4, one, 0)

    def shard_of(kk):
        return jnp.where(kk == 0, t1, jnp.where(kk == 1, t3, jnp.where(kk == 2, t, t2)))

    def down_grad(kk, _):
        tk = shard_of(kk)
        for n in range(3):
            cols = slice(n * 256, n * 256 + 256)
            D4[kk, :, :, :, cols] = dot(gT[...], act[tk, :, cols]).reshape(4, 2, 96, 256).astype(bf16)
        return 0

    def up_back(kk, _):
        tk = shard_of(kk)

        for n in range(3):
            n0 = n * 256
            cols = pl.ds(n0, 256)
            g = (dot(glow[...], Gd(2, tk, n0, 256)) * der[tk, :, cols].astype(f32)).astype(bf16)
            der[tk, :, cols] = g
            U4[kk, :, :, :, cols] = dot(nT[...], g).reshape(4, 2, 96, 256).astype(bf16)

        acc[...] += dot_nt(der[tk], Gv(1, tk, 0, D))
        return 0

    lax.fori_loop(0, 2, down_grad, 0)
    send(coreD)
    lax.fori_loop(2, 4, down_grad, 0)
    add_core(coreD, D4, RC.at[0])
    step(3.0)
    step(3.0)
    for r in redD:
        plan.begin(r)
    lax.fori_loop(0, 2, up_back, 0)
    send(coreU)
    step(5.3)
    lax.fori_loop(2, 4, up_back, 0)
    step(5.3)
    add_core(coreU, U4, RC.at[1])
    step(1.0)
    for r in redU:
        plan.begin(r)

    def norm1b(i, carry):
        sg, sh = carry
        rows = pl.ds(pl.multiple_of(i * RB_, RB_), RB_)
        e = acc[rows, :]
        nrm = n1[rows, :]
        inv = inv1[rows, 0:1]
        sc = e * gain1
        g = inv * (sc - jnp.mean(sc, axis=1, keepdims=True) - nrm * jnp.mean(sc * nrm, axis=1, keepdims=True))
        acc[rows, :] = g
        glow[rows, :] = g.astype(bf16)

        def fold(v):
            return jnp.sum(v.reshape(RB_ // 8, 8, D), axis=0)

        return (sg + fold(e * nrm), sh + fold(e))

    sg, sh = lax.fori_loop(0, ROWS // RB_, norm1b, (z8, z8))
    sm[3:4] = jnp.sum(sg, axis=0, keepdims=True)
    sm[4:5] = jnp.sum(sh, axis=0, keepdims=True)
    sm[5:8] = jnp.zeros((3, D), f32)
    for j in range(3):
        gT[j * 256:(j + 1) * 256, :] = jnp.transpose(glow[:, j * 256:(j + 1) * 256])

    lx2.wait()
    for j in range(3):
        xT[j * 256:(j + 1) * 256, :] = jnp.transpose(nlow[:, j * 256:(j + 1) * 256])
    step(3.0)

    links = (CORE, YY, XX, Z0, Z1)

    def sums_step(d, arrived):
        i = 2 * links.index(d)
        if arrived:
            sm[...] = sm[...] + smr[i + 1]
        else:
            smr[i] = sm[...]

    sums = Small({d: [rcopy(smr.at[2 * i], smr.at[2 * i + 1], d)] for i, d in enumerate(links)},
                 dict.fromkeys(links, 0.17), sums_step)

    for g in gat[1] + gat[2]:
        for cps in g.stages.values():
            for cp in cps:
                cp.wait_send()
                done(cp)
    plan.begin(sums)

    def gn_rows(tt, _):
        gae = dot(glow[...], G[0, tt, :, :, :, 512:768].reshape(D, 256)).astype(bf16).astype(f32)
        g2_ = pltpu.roll(gae[:, 0:128], 64, 1)
        g0_ = gae[:, 128:256]
        g1_ = pltpu.roll(g0_, 64, 1)
        for j, g in enumerate((g0_, g1_, g2_)):
            h = tt * 3 + j
            v = nl[h]
            g = jnp.where(low_half, g, 0.0)
            den = jnp.broadcast_to(v[:, 64:65], (ROWS, 128))
            safe = jnp.maximum(den, 1.0)
            s = jnp.sum(g * jnp.where(low_half, v, 0.0), axis=1, keepdims=True)
            gd_ = jnp.where(den > 1.0, -s / safe, 0.0)
            gn = jnp.where(low_half, g / safe, jnp.where(lane == 64, gd_, 0.0))
            nl[h] = gn
            gnT = jnp.transpose(gn).astype(bf16)
            parts = [dot(gnT[:ST, i * 128:(i + 1) * 128], qf[h, i * 128:(i + 1) * 128, :]) for i in range(4)]
            dE[2, h] = (parts[0] + parts[1] + parts[2] + parts[3]).astype(bf16)
            near = jnp.where(t < 2, 1, 3)
            away = jnp.where(t < 2, 3, 1)
            for slot, b in ((0, away), (1, away + 1), (3, near), (4, near + 1)):
                tot = jnp.zeros((ST, 128), f32)
                for i in range(4):
                    tot = tot + jnp.where(leaf_parent(i) == b, parts[i], 0.0)
                dE[slot, h] = tot.astype(bf16)
        return 0

    if HOLD_BACKWARD == 1:
        plan.hold()
    lax.fori_loop(0, 2, gn_rows, 0)
    step(4.2)
    if HOLD_BACKWARD == 2:
        plan.hold()
    lax.fori_loop(2, 4, gn_rows, 0)
    step(4.2)

    bc = [rcopy(dE.at[2], RR.at[0], CORE)]
    bx1 = [rcopy(dE.at[2, half], RX.at[half], XX)]
    by1 = [rcopy(dE.at[pl.ds(0, 2)], RR.at[pl.ds(2, 2)], YY)]
    bn1 = [rcopy(dE.at[pl.ds(3, 2)], RR.at[pl.ds(2, 2)], CORE)]
    by0 = [rcopy(TTb.at[half], RR.at[1, half], YY)]
    bo0 = [rcopy(dE.at[3, half], RR.at[2, half], CORE)]
    start(bc)

    @pl.when(has_leaves)
    def _():
        start(by1)

    dq = act

    def pair(y, feat):
        y = y * cs[...]
        fc = feat.astype(f32)
        fc = jnp.where(low_half, fc, pltpu.roll(fc, 64, 1))
        return jnp.where(fc > 0.0, y + pltpu.roll(y, 64, 1), 0.0).astype(bf16)

    def bwd_q(tt, _):
        for j in range(3):
            h = tt * 3 + j
            gn = nl[h].astype(bf16)
            dw = dot_nt(gn, vx[h]).astype(bf16) * mk[...]
            pri = [dot(gn[i * 128:(i + 1) * 128, :], chunk_state(h, leaf_parent(i))) for i in range(4)]
            gq = pair(dot(dw, kf[h]) + jnp.concatenate(pri, axis=0), qf[h])
            if j == 0:
                dq[tt, :, 0:64] = gq[:, 0:64]
            elif j == 1:
                dq[tt, :, 64:128] = gq[:, 64:128]
            else:
                dq[tt, :, 384:448] = gq[:, 0:64]
        return 0

    lax.fori_loop(0, 1, bwd_q, 0)
    step(1.8)

    for cp in bc:
        cp.wait()

    @pl.when(c == 1)
    def _():
        def addup(h):
            dE[2, h] = dE[2, h] + RR[0, h]

        each_half(addup)
        start(bx1)

    if HOLD_BACKWARD == 0:
        plan.hold()
    due = plan.load(XX, 0.85)
    units_due = plan.load(YY, 1.7)
    lax.fori_loop(1, 4, bwd_q, 0)
    step(5.3)
    plan.gate(max(due, plan.now))

    @pl.when(c == 0)
    def _():
        wait_recv(bx1)

        def message(h):
            zero = jnp.zeros((ST, 128), f32)
            later = dE[2, h].astype(f32) + RR[0, h].astype(f32)
            TTb[h] = (jnp.where(t >= 2, later, zero) + RX[h].astype(f32)).astype(bf16)

        each_half(message)
        start(by0)

    due = plan.load(YY, 0.85)
    plan.release()

    def out_grad(kk, _):
        tt = shard_of(kk)
        v = dot(gT[...], att[tt])
        A4[kk, :, :, :, 512:768] = v.reshape(4, 2, 96, 256).astype(bf16)
        return 0

    lax.fori_loop(0, 4, out_grad, 0)
    step(2.0)
    plan.gate(max(due, units_due, plan.now))

    @pl.when(c == 0)
    def _():
        for cp in by0:
            cp.wait()

        def common(h):
            dE[3, h] = (RX[h].astype(f32) + RR[1, h].astype(f32)).astype(bf16)

        each_half(common)
        start(bo0)
        for cp in bo0:
            cp.wait()

    @pl.when(c == 1)
    def _():
        for cp in bx1:
            cp.wait_send()

    @pl.when(has_leaves)
    def _():
        for cp in by1:
            cp.wait()

        def meet(h, _):
            dE[3, h] = dE[3, h] + RR[2, h]
            dE[4, h] = dE[4, h] + RR[3, h]
            return 0

        lax.fori_loop(0, 12, meet, 0)
        start(bn1)
        for cp in bn1:
            cp.wait_send()

    @pl.when(has_branches)
    def _():
        wait_recv(bn1)

    step(1.5)

    def later_states(h):
        zero = jnp.zeros((ST, 128), f32)
        shared = jnp.where(h // 6 == core_id, dE[3, h].astype(f32), RR[2, h].astype(f32))
        d = jnp.where(t1 > t, RR[0, h].astype(f32), zero) + shared
        pad = jnp.zeros((128 - ST, 128), bf16)
        out = []
        for u in range(2):
            b = jnp.where(has_branches, RR[2 + u, h].astype(f32), zero)
            out.append(jnp.concatenate([jnp.where(c == 0, d, b).astype(bf16), pad], axis=0))
        return out

    def bwd_kv(kk, _):
        tt = shard_of(kk)
        for j in range(3):
            h = tt * 3 + j
            gn = nl[h].astype(bf16)
            ds = later_states(h)
            wT = dot_nt(kf[h], qf[h]).astype(bf16) * mkT[...]
            dv = dot(wT, gn) + jnp.concatenate(
                [dot_nt(kf[h, u * 256:(u + 1) * 256, :], ds[u]) for u in range(2)], axis=0)
            dwT = dot_nt(vx[h], gn).astype(bf16) * mkT[...]
            dk = dot(dwT, qf[h]) + jnp.concatenate(
                [dot(vx[h, u * 256:(u + 1) * 256, :], ds[u]) for u in range(2)], axis=0)
            gk = pair(dk, kf[h])
            if j == 0:
                dq[tt, :, 128:192] = gk[:, 0:64]
                dq[tt, :, 256:320] = dv[:, 0:64].astype(bf16)
            elif j == 1:
                dq[tt, :, 192:256] = gk[:, 64:128]
                dq[tt, :, 320:384] = pltpu.roll(dv, 64, 1)[:, 64:128].astype(bf16)
            else:
                dq[tt, :, 448:512] = gk[:, 64:128]
                dq[tt, :, 512:640] = jnp.where(low_half, dv, 0.0).astype(bf16)

        def put(l0, n, v):
            A4[kk, :, :, :, l0:l0 + n] = v.reshape(4, 2, 96, n).astype(bf16)

        put(0, 256, dot(xT[...], dq[tt, :, 0:256]))
        put(256, 256, dot(xT[...], dq[tt, :, 256:512]))
        o2 = A4[kk, :, :, :, 512:640].reshape(D, 128).astype(f32)
        put(512, 128, dot(xT[...], dq[tt, :, 512:640]) + o2)
        return 0

    for p in range(2):
        lax.fori_loop(2 * p, 2 * p + 2, bwd_kv, 0)
        step(5.8)
        if p == 0:
            plan.need([sums])
            send(coreA)
    add_core(coreA, A4, G.at[1])
    step(1.0)
    for r in redA:
        plan.begin(r)

    if ticks[0] <= OUTPUT_STEP:
        plan.begin(lo_out)
    def inback(tt, _):
        acc[...] += dot_nt(dq[tt, :, 0:640], Gv(0, tt, 0, 640))
        return 0

    lax.fori_loop(0, 4, inback, 0)
    igb[...] = acc[...].astype(bf16)
    ig_l = lcopy(igb, ig_hbm.at[rows_of(t)])
    ig_l.start()
    ig_c = send([rcopy(igb, ig_hbm.at[rows_of(t)], CORE)])

    def ig_step(stage, arrived):
        if stage == YY and arrived:
            lput(der.at[0], ig_hbm.at[rows_of(t2)])

    ig_out = Small({YY: [rcopy(igb, der.at[0], YY)],
                    CORE: [rcopy(der.at[0], ig_hbm.at[rows_of(t2)], CORE)]}, {YY: 5.3, CORE: 5.3}, ig_step)
    plan.tick(4.5)
    plan.begin(ig_out)
    plan.need(redD + redU + redA + [lo_out, ig_out])
    small[...] = sm[...]
    wait_recv(lo_c + ig_c)
    for cp in pending:
        cp.wait_send()
    for cp in puts + [lo_l, ig_l]:
        cp.wait()
    assert counter[0] <= N_REMOTE and lcounter[0] <= N_LOCAL, (counter, lcounter)


N_REMOTE, N_LOCAL = 168, 40


def fast_shards(layer_input, teacher, query_weight, key_weight, value_weight, out_weight, up_weight,
                down_weight, first_gain, first_shift, second_gain, second_shift, parents, valid_count):
    f = lax.axis_index(FSDP)
    D = layer_input.shape[-1]
    sc = layer_input.shape[1]
    tree_len = sc * lax.axis_size(CONTEXT)
    bf16, f32 = jnp.bfloat16, jnp.float32
    V = pltpu.VMEM
    scratch = [
        V((3, 4, 4, 2, 96, D), bf16),
        V((4, 16, 256), bf16),
        V((ROWS, D), bf16),
        V((12, ROWS, 128), bf16),
        V((12, ROWS, 128), bf16),
        V((12, ROWS, 128), bf16),
        V((ROWS, ROWS), bf16),
        V((ROWS, ROWS), bf16),
        V((ROWS, 128), f32),
        V((12, ROWS, 128), f32),
        V((4, ROWS, 256), bf16),
        V((ROWS, D), f32),
        V((ROWS, 128), f32),
        V((ROWS, D), bf16),
        V((4, ROWS, D), bf16),
        V((4, ROWS, D), bf16),
        V((ROWS, D), f32),
        V((ROWS, D), bf16),
        V((D, ROWS), bf16),
        V((D, ROWS), bf16),
        V((4, 12, ST, 128), bf16),
        V((12, ST, 128), bf16),
        V((12, ST, 128), bf16),
        V((4, 12, ST, 128), bf16),
        V((5, 12, ST, 128), bf16),
        V((12, ST, 128), bf16),
        V((2, 4, 4, 2, 96, D), bf16),
        V((2, 2, 4, 2, 96, D), bf16),
        V((2, 16, 96, D), bf16),
        V((8, D), f32),
        V((10, 8, D), f32),
        pltpu.SemaphoreType.DMA((N_REMOTE,)),
        pltpu.SemaphoreType.DMA((N_REMOTE,)),
        pltpu.SemaphoreType.DMA((N_LOCAL,)),
    ]
    any_, smem, vmem = (pl.BlockSpec(memory_space=s) for s in (pl.ANY, pltpu.SMEM, pltpu.VMEM))
    lo, ig, gout, small = pl.pallas_call(
        functools.partial(fast_kernel, tree_len=tree_len),
        out_shape=[
            jax.ShapeDtypeStruct((sc, D), bf16),
            jax.ShapeDtypeStruct((sc, D), bf16),
            jax.ShapeDtypeStruct((3, 2, 96, D), bf16),
            jax.ShapeDtypeStruct((8, D), f32),
        ],
        in_specs=[any_, any_, vmem, vmem, vmem, vmem, any_, any_, vmem, vmem, vmem, vmem, smem, smem],
        out_specs=[any_, any_, any_, vmem],
        scratch_shapes=scratch,
        compiler_params=pltpu.CompilerParams(
            collective_id=0, has_side_effects=True, vmem_limit_bytes=67043328),
        name="tree_layer",
    )(layer_input, teacher, query_weight, key_weight, value_weight, out_weight, up_weight.reshape(2, 96, D),
      down_weight.T.reshape(2, 96, D), first_gain, first_shift, second_gain, second_shift, parents, valid_count)
    sq, wide, vec = (jax.ShapeDtypeStruct(n, f32) for n in ((192, 192), (192, D), (192,)))

    def whole(a):
        return pl.BlockSpec(a.shape, lambda i: (0,) * len(a.shape))

    outs = pl.pallas_call(
        unpack_kernel,
        grid=(2,),
        in_specs=[whole(gout), whole(small), pl.BlockSpec((2 * ROWS, D), lambda i: (i, 0))],
        out_specs=[whole(a) for a in (sq, sq, sq, sq, wide, wide, vec, vec, vec, vec)]
        + [pl.BlockSpec((1, 1), lambda i: (0, 0)), pl.BlockSpec((2 * ROWS, D), lambda i: (i, 0))],
        out_shape=[sq, sq, sq, sq, wide, wide, vec, vec, vec, vec,
                   jax.ShapeDtypeStruct((1, 1), f32), jax.ShapeDtypeStruct((sc, D), f32)],
        name="unpack",
    )(gout, small, ig)
    q_g, k_g, v_g, o_g, up_g, down_t, g1_g, s1_g, g2_g, s2_g, loss, ig_wide = outs
    return (lo[None], ig_wide[None], loss.reshape(()), q_g, k_g, v_g, o_g, up_g, down_t.T,
            g1_g, s1_g, g2_g, s2_g)


def unpack_kernel(gout, small, ig, q_g, k_g, v_g, o_g, up_g, down_t, g1_g, s1_g, g2_g, s2_g, loss, ig_wide):
    f32 = jnp.float32
    ig_wide[...] = ig[...].astype(f32)

    @pl.when(pl.program_id(0) == 0)
    def _():
        a = gout[0].reshape(192, 768).astype(f32)
        q_g[:, 0:128] = a[:, 0:128]
        q_g[:, 128:192] = a[:, 384:448]
        k_g[:, 0:128] = a[:, 128:256]
        k_g[:, 128:192] = pltpu.roll(a[:, 384:512], 64, 1)[:, 0:64]
        v_g[:, 0:128] = a[:, 256:384]
        v_g[:, 128:192] = a[:, 512:576]
        o_t = jnp.concatenate([a[:, 640:768], pltpu.roll(a[:, 512:640], 64, 1)], axis=1)
        o_g[...] = jnp.transpose(o_t)[0:192, :]
        up_g[...] = gout[1].reshape(192, 768).astype(f32)
        down_t[...] = gout[2].reshape(192, 768).astype(f32)
        f = lax.axis_index(FSDP)
        total = small[...]
        mine = jnp.where(f == 0, total[:, 0:256], total[:, 384:640])
        odd = jnp.where(f == 1, total[:, 128:384], total[:, 512:768])
        mine = jnp.where(f - 2 * (f // 2) == 1, pltpu.roll(odd, 192, 1), mine)[:, 0:192]
        for i, out in ((3, g1_g), (4, s1_g), (0, g2_g), (1, s2_g)):
            out[...] = mine[i]
        loss[...] = jnp.sum(total[2:3], axis=1, keepdims=True)


def shards(*arrays):
    tree_count, slot_count, width = arrays[0].shape
    sizes = tuple(lax.axis_size(n) for n in (FSDP, CONTEXT, TENSOR))
    if (tree_count, slot_count, width) == (1, 2048, 768) and sizes == (4, 2, 4) and arrays[6].shape == (192, 768):
        return fast_shards(*arrays)
    return general_shards(*arrays)


def solution(mesh):
    return jax.shard_map(
        shards,
        mesh=mesh,
        in_specs=(
            P(FSDP, CONTEXT, None),
            P(FSDP, CONTEXT, None),
            P(FSDP, TENSOR),
            P(FSDP, TENSOR),
            P(FSDP, TENSOR),
            P(TENSOR, FSDP),
            P(FSDP, TENSOR),
            P(TENSOR, FSDP),
            P(FSDP),
            P(FSDP),
            P(FSDP),
            P(FSDP),
            P(FSDP, None),
            P(FSDP),
        ),
        out_specs=(
            P(FSDP, CONTEXT, None),
            P(FSDP, CONTEXT, None),
            P(),
            P(FSDP, TENSOR),
            P(FSDP, TENSOR),
            P(FSDP, TENSOR),
            P(TENSOR, FSDP),
            P(FSDP, TENSOR),
            P(TENSOR, FSDP),
            P(FSDP),
            P(FSDP),
            P(FSDP),
            P(FSDP),
        ),
        check_vma=False,
    )
```
